32 devices in a mesh: tower: 2 (over core), batch: 16 (over z, y, x).
Axes of the slice: x: 2, y: 2, z: 4, core: 2. Of those that a mesh axis runs over, the one named last changes fastest.
Arguments:
- tokens: bfloat16 [2, 32768, 768], P('tower', 'batch'), may hold values from -6 to 6
- lengths: int32 [2, 64], P('tower', 'batch'), may hold values from 64 to 512, as said below
- prefixes: int32 [2, 64], P('tower', 'batch'), may hold values from 1 to 32
- positives: int32 [64], replicated, may hold values from 0 to 63, each once
- gain_attention: float32 [768], replicated, may hold values from 0.5 to 1.5
- query_weight: bfloat16 [768, 768], replicated, may hold values from -0.02734375 to 0.02734375
- key_weight: bfloat16 [768, 768], replicated, may hold values from -0.21875 to 0.21875
- value_weight: bfloat16 [768, 768], replicated, may hold values from -0.21875 to 0.21875
- output_weight: bfloat16 [768, 768], replicated, may hold values from -1.75 to 1.75
- bucket_bias: float32 [32, 12], replicated, may hold values from -4 to 4
- gain_feedforward: float32 [768], replicated, may hold values from 0.5 to 1.5
- widen_weight: bfloat16 [768, 3072], replicated, may hold values from -0.21875 to 0.21875
- narrow_weight: bfloat16 [3072, 768], replicated, may hold values from -0.109375 to 0.109375
- gain_final: float32 [768], replicated, may hold values from 0.5 to 1.5
Outputs:
- contrast_loss: float32 [], replicated
- score_gradient: float32 [64, 64], P('batch')
- token_gradient: bfloat16 [2, 32768, 768], P('tower', 'batch')
- grad_attention: float32 [768], replicated
- grad_query: float32 [768, 768], replicated
- grad_key: float32 [768, 768], replicated
- grad_value: float32 [768, 768], replicated
- grad_output: float32 [768, 768], replicated
- grad_bucket: float32 [32, 12], replicated
- grad_feedforward: float32 [768], replicated
- grad_widen: float32 [768, 3072], replicated
- grad_narrow: float32 [3072, 768], replicated
- grad_final: float32 [768], replicated
The draws below stay inside these ranges and needn't reach their ends.
Inputs may be any that keep to these rules, and one draw needn't show every extreme that they name: `lengths`: sequence 0 of each side uses all 512 positions. `positives`: every document is the positive of exactly one query.
All inputs are finite; a program needn't handle non-finite values.
Results may differ from the reference program's by a relative error of at most 0.025.
The reference program's roundings to bfloat16 on the way count: a program that leaves them out, or rounds other values in their place, can miss the bound.
Values sent between devices are 32-bit elements; how exact they have to be, the bound alone decides.
A program may use at most 320 MiB of HBM per device.

```python
import jax
import jax.numpy as jnp
from jax import lax

D = 768
HEADS = 12
HEAD_DIM = 64
FF = 3072
BUCKETS = 32
SLOT = 512
SEQ_DEV = 4
NSEQ = 64
TOKENS = 32768


def draw_lengths(key, part):
    counts = jax.random.randint(key, (2, NSEQ), SLOT // 8, SLOT + 1, dtype=jnp.int32)
    return counts.at[:, 0].set(SLOT)


def with_ends(result, key, smallest, high):
    longest = result.shape.index(max(result.shape))
    spots = []
    for shift in (0, 1):
        where = [jax.random.randint(jax.random.fold_in(key, axis), (), 0, length) for axis, length in enumerate(result.shape)]
        where[longest] = (where[longest] + shift) % result.shape[longest]
        spots.append(tuple(where))
    return result.at[spots[0]].set(smallest).at[spots[1]].set(high)


def block_levels(key, dims, shards, least, high):
    gain = 1.0
    for position, blocks in shards:
        steps = jax.random.uniform(jax.random.fold_in(jax.random.fold_in(key, 6), position), (blocks,), jnp.float32, least / len(shards), high / len(shards))
        gain = gain * jnp.repeat(jnp.exp(steps), dims[position] // blocks).reshape((-1,) + (1,) * (len(dims) - 1 - position))
    return gain


def noise(rng, shape, scale, most, shards=(), kind=jnp.bfloat16):
    values = jax.random.normal(rng, shape, jnp.float32) * scale
    if len(shards) > 0:
        values = block_levels(rng, shape, shards, -0.22, 0.18) * values
    return jnp.clip(values, min=-most, max=most).astype(kind)


def setup_inputs(seed: int = 0) -> dict:
    streams_of = jax.random.split(jax.random.key(seed), 15)
    return {
        "tokens": noise(streams_of[0], (2, TOKENS, D), 1.0, 6.0, ((0, 2), (1, 16))),
        "lengths": draw_lengths(jax.random.fold_in(streams_of[14], 71), 0),
        "prefixes": with_ends(jax.random.randint(streams_of[2], (2, NSEQ), 1, SLOT // 16 + 1), jax.random.fold_in(streams_of[2], 1), 1, (SLOT // 16 + 1) - 1).astype(jnp.int32),
        "positives": jax.random.permutation(streams_of[3], NSEQ).astype(jnp.int32),
        "gain_attention": jnp.clip(1.0 + 0.1 * jax.random.normal(streams_of[4], (D,), jnp.float32), 0.5, 1.5),
        "query_weight": noise(streams_of[5], (D, HEADS * HEAD_DIM), (D * HEAD_DIM) ** -0.5, 0.02734375),
        "key_weight": noise(streams_of[6], (D, HEADS * HEAD_DIM), D ** -0.5, 0.21875),
        "value_weight": noise(streams_of[7], (D, HEADS * HEAD_DIM), D ** -0.5, 0.21875),
        "output_weight": noise(streams_of[8], (HEADS * HEAD_DIM, D), (max(HEADS * HEAD_DIM // 64, 1)) ** -0.5, 1.75),
        "bucket_bias": noise(streams_of[9], (BUCKETS, HEADS), 1.0, 4.0, (), jnp.float32),
        "gain_feedforward": jnp.clip(1.0 + 0.1 * jax.random.normal(streams_of[10], (D,), jnp.float32), 0.5, 1.5),
        "widen_weight": noise(streams_of[11], (D, FF), D ** -0.5, 0.21875),
        "narrow_weight": noise(streams_of[12], (FF, D), FF ** -0.5, 0.109375),
        "gain_final": jnp.clip(1.0 + 0.1 * jax.random.normal(streams_of[13], (D,), jnp.float32), 0.5, 1.5),
    }


@jax.custom_vjp
def low(v):
    return lax.optimization_barrier(v.astype(jnp.bfloat16)).astype(jnp.float32)

@jax.custom_vjp
def low_back(v):
    return v

def low_keep(v):
    return (low(v), None)

def low_pass(kept, grad):
    return (grad,)

def back_keep(v):
    return (v, None)

def back_low(kept, grad):
    return (low(grad),)
low.defvjp(low_keep, low_pass)
low_back.defvjp(back_keep, back_low)
epsilon = 1e-06
masked_score = -1000000000.0
score_scale = 100.0
far_steps = (12, 16, 23, 32, 46, 64, 91)
highest = lax.Precision.HIGHEST

def bucket_onehot(slot_len, bucket_count):
    places = jnp.arange(slot_len, dtype=jnp.int32)
    offset = places[None, :] - places[:, None]
    spread = jnp.abs(offset)
    far_bucket = 8 + sum(((spread >= step).astype(jnp.int32) for step in far_steps))
    bucket = jnp.where(spread < 8, spread, far_bucket) + jnp.where(offset > 0, bucket_count // 2, 0).astype(jnp.int32)
    labels = jnp.arange(bucket_count, dtype=jnp.int32)
    return (bucket[:, :, None] == labels[None, None, :]).astype(jnp.float32)

def norm_apply(values, scale_vec):
    return values * lax.rsqrt(lax.optimization_barrier(jnp.mean(values * values, axis=-1, keepdims=True)) + epsilon) * scale_vec

def attend_one(query_rows, key_rows, value_rows, valid_keys, bias):
    raw_scores = jnp.einsum('ihd,jhd->hij', query_rows, key_rows, precision=highest)
    scores = low_back(raw_scores) + bias
    scores = jnp.where(valid_keys[None, None, :], scores, masked_score)
    row_peak = lax.optimization_barrier(jnp.max(scores, axis=-1, keepdims=True))
    raised = jnp.exp(scores - row_peak)
    soft = raised / lax.optimization_barrier(jnp.sum(raised, axis=-1, keepdims=True))
    context = jnp.einsum('hij,jhd->ihd', low(soft), value_rows, precision=highest)
    return low(low_back(context))

def encode(tokens_group, lengths_group, prefix_group, weights, onehot):
    gain_attention, query_weight, key_weight, value_weight, output_weight, bucket_bias, gain_feedforward, widen_weight, narrow_weight, gain_final = weights
    seqs = lengths_group.shape[0]
    bias = jnp.einsum('ijb,bh->hij', onehot, bucket_bias, precision=highest)
    normed = low(norm_apply(tokens_group, gain_attention))

    def project(matrix):
        projected = low(low_back(jnp.dot(normed, matrix, precision=highest)))
        return projected.reshape(seqs, SLOT, HEADS, HEAD_DIM)
    places = jnp.arange(SLOT, dtype=jnp.int32)
    valid = places[None, :] < lengths_group[:, None]
    attend = jax.checkpoint(lambda parts: attend_one(parts[0], parts[1], parts[2], parts[3], bias))
    context = lax.map(attend, (project(query_weight), project(key_weight), project(value_weight), valid))
    attn_out = jnp.dot(context.reshape(seqs * SLOT, HEADS * HEAD_DIM), output_weight, precision=highest)
    mixed = tokens_group + low_back(attn_out)
    ffn_in = low(norm_apply(mixed, gain_feedforward))
    pre_act = low_back(jnp.dot(ffn_in, widen_weight, precision=highest))
    hidden = low(jnp.where(pre_act > 0, pre_act, 0.0))
    output = mixed + low_back(jnp.dot(hidden, narrow_weight, precision=highest))
    final = norm_apply(output, gain_final)
    pool_mask = ((places[None, :] >= prefix_group[:, None]) & valid).astype(jnp.float32)
    pool_weight = pool_mask / lax.optimization_barrier(jnp.sum(pool_mask, axis=1, keepdims=True))
    pooled = lax.optimization_barrier(jnp.sum(final.reshape(seqs, SLOT, D) * pool_weight[:, :, None], axis=1))
    return pooled * lax.rsqrt(lax.optimization_barrier(jnp.sum(pooled * pooled, axis=-1, keepdims=True)) + epsilon)

def reference(tokens, lengths, prefixes, positives, gain_attention, query_weight, key_weight, value_weight, output_weight, bucket_bias, gain_feedforward, widen_weight, narrow_weight, gain_final):
    groups = 2 * NSEQ // SEQ_DEV
    tokens_all = tokens.astype(jnp.float32).reshape(groups, SEQ_DEV * SLOT, D)
    lengths_all = lengths.reshape(groups, SEQ_DEV)
    prefix_all = prefixes.reshape(groups, SEQ_DEV)
    weights = (gain_attention, query_weight.astype(jnp.float32), key_weight.astype(jnp.float32), value_weight.astype(jnp.float32), output_weight.astype(jnp.float32), bucket_bias, gain_feedforward, widen_weight.astype(jnp.float32), narrow_weight.astype(jnp.float32), gain_final)
    onehot = bucket_onehot(SLOT, BUCKETS)

    def score_matrix(tokens_in, weight_in):
        encode_group = jax.checkpoint(lambda parts: encode(parts[0], parts[1], parts[2], weight_in, onehot))
        units = lax.map(encode_group, (tokens_in, lengths_all, prefix_all)).reshape(2, NSEQ, D)
        return score_scale * jnp.dot(units[0], units[1].T, precision=highest)

    def contrast(scores):
        labels = jnp.arange(NSEQ, dtype=jnp.int32)
        target = (positives[:, None] == labels[None, :]).astype(jnp.float32)
        row_peak = lax.optimization_barrier(jnp.max(scores, axis=1, keepdims=True))
        row_total = row_peak[:, 0] + jnp.log(lax.optimization_barrier(jnp.sum(jnp.exp(scores - row_peak), axis=1)))
        col_peak = lax.optimization_barrier(jnp.max(scores, axis=0, keepdims=True))
        col_total = col_peak[0] + jnp.log(lax.optimization_barrier(jnp.sum(jnp.exp(scores - col_peak), axis=0)))
        return 0.5 * jnp.sum(row_total) + 0.5 * jnp.sum(col_total) - jnp.sum(target * scores)
    scores, pull_back = jax.vjp(score_matrix, tokens_all, weights)
    loss_value, loss_back = jax.vjp(contrast, scores)
    score_grad, = loss_back(jnp.ones((), jnp.float32))
    grad_tokens, grads = pull_back(score_grad)
    return (loss_value, score_grad, grad_tokens.reshape(2, NSEQ * SLOT, D).astype(jnp.bfloat16), grads[0], grads[1], grads[2], grads[3], grads[4], grads[5], grads[6], grads[7], grads[8], grads[9])
```

```python
import functools

import jax
import jax.numpy as jnp
from jax import lax
from jax.experimental import pallas as pl
from jax.experimental.pallas import tpu as pltpu
from jax.sharding import PartitionSpec as P

epsilon = 1e-06
masked_score = -1000000000.0
score_scale = 100.0
far_steps = (12, 16, 23, 32, 46, 64, 91)
highest = lax.Precision.HIGHEST

MESH = pl.DeviceIdType.MESH
job_rows = 384
unit_rows = 128


def batch_dims(size):
    sizes = {16: (2, 2, 4), 64: (4, 4, 4)}[size]
    strides = (1, sizes[0], sizes[0] * sizes[1])
    return dict(zip("xyz", zip(strides, sizes)))


def place():
    return lax.axis_index("tower"), lax.axis_index("batch")


def gather_kernel(groups, block_ref, out_ref, slots, send_sem, recv_sem, mate_sem):
    tower, batch = place()
    barrier = pltpu.get_barrier_semaphore()
    mate = (1 - tower, batch)

    def peer(step):
        return tower, lax.rem(batch + step, groups)

    def greet(step, carry):
        pl.semaphore_signal(barrier, 1, device_id=peer(step), device_id_type=MESH)
        return carry

    lax.fori_loop(1, groups, greet, 0)
    pl.semaphore_signal(barrier, 1, device_id=mate, device_id_type=MESH)
    slots[tower, batch] = block_ref[...]
    pl.semaphore_wait(barrier, groups)

    def copy(step, owner):
        return pltpu.make_async_remote_copy(
            src_ref=block_ref,
            dst_ref=slots.at[tower, owner],
            send_sem=send_sem.at[step],
            recv_sem=recv_sem.at[owner],
            device_id=peer(step),
            device_id_type=MESH,
        )

    def begin(step, carry):
        copy(step, batch).start()
        return carry

    def finish(step, carry):
        copy(step, batch).wait_send()
        copy(step, peer(step)[1]).wait_recv()
        return carry

    lax.fori_loop(1, groups, begin, 0)
    lax.fori_loop(1, groups, finish, 0)
    side = pltpu.make_async_remote_copy(
        src_ref=slots.at[tower],
        dst_ref=slots.at[tower],
        send_sem=mate_sem.at[0],
        recv_sem=mate_sem.at[1],
        device_id=mate,
        device_id_type=MESH,
    )
    side.start()
    side.wait()
    out_ref[...] = slots[...]


def gather_blocks(block, groups, collective):
    whole = (2, groups) + block.shape
    return pl.pallas_call(
        functools.partial(gather_kernel, groups),
        out_shape=jax.ShapeDtypeStruct(whole, jnp.float32),
        in_specs=[pl.BlockSpec(memory_space=pltpu.VMEM)],
        out_specs=pl.BlockSpec(memory_space=pltpu.VMEM),
        scratch_shapes=[
            pltpu.VMEM(whole, jnp.float32),
            pltpu.SemaphoreType.DMA((groups,)),
            pltpu.SemaphoreType.DMA((groups,)),
            pltpu.SemaphoreType.DMA((2,)),
        ],
        compiler_params=pltpu.CompilerParams(collective_id=collective, has_side_effects=True),
        name="gather_blocks",
    )(block)


def both(first, second):
    if first is None:
        return second
    if second is None:
        return first
    return jnp.logical_and(first, second)


def guarded(condition, action):
    if condition is None:
        action()
    else:
        pl.when(condition)(action)


def plan_unit(order, dims, batch, rows):
    add, spread = [], []
    start, active = 0, None
    for name in order:
        stride, size = dims[name]
        coord = lax.rem(batch // stride, size)
        if size == 4:
            inner = jnp.logical_or(coord == 1, coord == 2)
            outer = jnp.logical_not(inner)
            mate = batch + stride * (1 - 2 * lax.rem(coord, 2))
            add.append(
                dict(rows=rows, send=start, keep=start, peer=mate,
                     sends=both(active, outer), receives=both(active, inner)))
            spread.append(
                dict(rows=rows, send=start, peer=mate,
                     sends=both(active, inner), receives=both(active, outer)))
            active = both(active, inner)
            bit = coord // 2
            mate = batch + stride * (3 - 2 * coord)
        else:
            bit = coord
            mate = batch + stride * (1 - 2 * coord)
        rows = rows // 2
        kept = start + bit * rows
        add.append(
            dict(rows=rows, send=start + (1 - bit) * rows, keep=kept, peer=mate,
                 sends=active, receives=active))
        spread.append(dict(rows=rows, send=kept, peer=mate, sends=active, receives=active))
        start = kept
    return add, spread[::-1]


def step_rings(order, dims):
    one_way = []
    for name in order:
        one_way += [True, False] if dims[name][1] == 4 else [False]
    count = len(one_way)
    steps = 2 + 2 * count
    rings = [3] * steps
    for index, single in enumerate(one_way):
        if single:
            first, last = 1 + index, steps - 2 - index
            rings[first] = rings[last] = last - first + 2
    return rings


def stage_rows(order, dims, rows):
    result = []
    for name in order:
        if dims[name][1] == 4:
            result.append(rows)
        rows //= 2
        result.append(rows)
    return result


orders = ("xyz", "yxz", "zxy")


def sums_kernel(dims, jobs, *refs):
    (hidden, ffn_in, context, normed, branch, pre, attn, dq, dk, dv, small, out, small_out) = refs[:13]
    (left, right, part, acc, full, mate_in, small_own, small_in) = refs[13:21]
    rest = refs[21:]
    counts = [len(stage_rows(order, dims, 8)) for order in orders]
    inbox, where = [], 0
    for count in counts:
        inbox.append(rest[where : where + count])
        where += count
    load_sem, send_sem, recv_sem, keep_sem, small_sem = rest[where:]
    tower, batch = place()
    half = unit_rows // 2
    steps = 2 + 2 * counts[0]
    plans = [plan_unit(order, dims, batch, half) for order in orders]
    rings = [step_rings(order, dims) for order in orders]
    held, spread_held = acc.shape[0], full.shape[0]

    barrier = pltpu.get_barrier_semaphore()
    mate = (1 - tower, batch)
    mates, turns = [mate], [mate]
    for stride, size in dims.values():
        coord = lax.rem(batch // stride, size)
        near = (tower, batch + stride * (1 - 2 * lax.rem(coord, 2)))
        mates.append(near)
        turns.append(near)
        if size == 4:
            mates.append((tower, batch + stride * (3 - 2 * coord)))
            turns.append((tower, batch + stride * (2 - 4 * (coord // 2))))
            mates.append(turns[-1])
    for mate in mates:
        pl.semaphore_signal(barrier, 1, device_id=mate, device_id_type=MESH)
    pl.semaphore_wait(barrier, len(mates))

    width = out.shape[1]

    def load(job, begin):
        slot = lax.rem(job, 2)

        def copies(left_ref, left_block, right_ref, right_block):
            for index, (ref, block, size, target) in enumerate(
                ((left_ref, left_block, job_rows, left), (right_ref, right_block, width, right))
            ):
                columns = pl.ds(pl.multiple_of(block * size, 128), size)
                copy = pltpu.make_async_copy(
                    ref.at[:, columns], target.at[slot], load_sem.at[index, slot]
                )
                copy.start() if begin else copy.wait()

        if not begin:
            copies(hidden, 0, branch, 0)
            return
        per_narrow = hidden.shape[1] // job_rows
        per_side = width // job_rows
        first = 0
        table = [(hidden, branch, per_narrow)]
        table.append((ffn_in, pre, per_narrow))
        table += [(context, attn, per_side), (normed, dq, per_side), (normed, dk, per_side), (normed, dv, per_side)]
        for index, (left_ref, right_ref, count) in enumerate(table):
            local = job - first

            def go(local=local, left_ref=left_ref, right_ref=right_ref, index=index):
                if index == 1:
                    copies(left_ref, lax.rem(local, per_side), right_ref, local // per_side)
                else:
                    copies(left_ref, local, right_ref, 0)

            pl.when(jnp.logical_and(local >= 0, local < count))(go)
            first += count

    def compute(job):
        slot = lax.rem(job, 2)
        load(job, False)
        pl.when(job + 1 < jobs)(lambda: load(job + 1, True))
        part[slot] = lax.dot_general(
            left[slot], right[slot], (((0,), (0,)), ((), ())), preferred_element_type=jnp.float32
        )

    def remote(unit, step, job):
        add, spread = plans[unit]
        turn = lax.rem(job, rings[unit][step])
        place_in = lax.rem(job, held)
        sems = dict(
            send_sem=send_sem.at[unit * steps + step, turn],
            recv_sem=recv_sem.at[unit * steps + step, turn],
            device_id_type=MESH,
        )
        base = unit * half
        if step == 0:
            src = part.at[lax.rem(job, 2), pl.ds(pl.multiple_of(unit * unit_rows + (1 - tower) * half, 8), half)]
            dst = mate_in.at[turn, pl.ds(base, half)]
            return pltpu.make_async_remote_copy(src, dst, device_id=(1 - tower, batch), **sems), None, None
        if step == steps - 1:
            src = full.at[lax.rem(job, spread_held), pl.ds(base, half)]
            first = pl.multiple_of(job * job_rows + unit * unit_rows + tower * half, 8)
            dst = out.at[pl.ds(first, half)]
            return pltpu.make_async_remote_copy(src, dst, device_id=(1 - tower, batch), **sems), None, None
        count = counts[unit]
        item = add[step - 1] if step <= count else spread[step - 1 - count]
        rows = pl.ds(pl.multiple_of(base + item["send"], 8), item["rows"])
        if step <= count:
            src, dst = acc.at[place_in, rows], inbox[unit][step - 1].at[turn]
        else:
            src = dst = full.at[lax.rem(job, spread_held), rows]
        copy = pltpu.make_async_remote_copy(src, dst, device_id=(tower, item["peer"]), **sems)
        return copy, item["sends"], item["receives"]

    def keep(unit, job):
        base = unit * half
        first = pl.multiple_of(job * job_rows + unit * unit_rows + tower * half, 8)
        return pltpu.make_async_copy(
            full.at[lax.rem(job, spread_held), pl.ds(base, half)], out.at[pl.ds(first, half)], keep_sem.at[unit, lax.rem(job, 2)]
        )

    def finish(unit, step, job):
        copy, sends, receives = remote(unit, step, job)
        add, _ = plans[unit]
        base = unit * half
        guarded(sends, copy.wait_send)
        turn = lax.rem(job, rings[unit][step])
        place_in = lax.rem(job, held)

        def arrived():
            copy.wait_recv()
            if step == 0:
                own = pl.ds(pl.multiple_of(unit * unit_rows + tower * half, 8), half)
                acc[place_in, pl.ds(base, half)] = part[lax.rem(job, 2), own] + mate_in[turn, pl.ds(base, half)]
            elif step <= counts[unit]:
                item = add[step - 1]
                rows = pl.ds(pl.multiple_of(base + item["keep"], 8), item["rows"])
                total = acc[place_in, rows] + inbox[unit][step - 1][turn]
                if step == counts[unit]:
                    full[lax.rem(job, spread_held), rows] = total
                else:
                    acc[place_in, rows] = total

        guarded(receives, arrived)
        if step == steps - 1:
            keep(unit, job).wait()

    def advance(step, job):
        for unit in range(len(orders)):
            if step > 0:
                finish(unit, step - 1, job)
            if step < steps:
                copy, sends, _ = remote(unit, step, job)
                guarded(sends, copy.start)
                if step == steps - 1:
                    keep(unit, job).start()

    def small_copy(turn):
        return pltpu.make_async_remote_copy(
            src_ref=small_own.at[turn],
            dst_ref=small_in.at[turn],
            send_sem=small_sem.at[0, turn],
            recv_sem=small_sem.at[1, turn],
            device_id=turns[turn],
            device_id_type=MESH,
        )

    def small_turn(turn):
        if turn == 0:
            small_own[0] = small[...]
        else:
            small_copy(turn - 1).wait()
            total = small_own[turn - 1] + small_in[turn - 1]
            if turn == len(turns):
                small_out[...] = total
            else:
                small_own[turn] = total
        if turn < len(turns):
            small_copy(turn).start()

    load(0, True)

    def slot(time, carry):
        for step in range(steps, -1, -1):
            job = time - 1 - step
            pl.when(jnp.logical_and(job >= 0, job < jobs))(functools.partial(advance, step, job))
        for turn in range(len(turns) + 1):
            pl.when(time == turn)(functools.partial(small_turn, turn))
        pl.when(time < jobs)(functools.partial(compute, time))
        return carry

    lax.fori_loop(0, jobs + steps + 1, slot, 0)


def sum_weights(batch_size, collective, *arrays):
    hidden, normed = arrays[0], arrays[3]
    tokens, width = normed.shape
    total = 2 * hidden.shape[1] + 4 * width
    jobs = total // job_rows
    dims = batch_dims(batch_size)
    half = unit_rows // 2
    rings = [step_rings(order, dims) for order in orders]
    inboxes = [
        pltpu.VMEM((rings[unit][1 + index], rows, width), jnp.float32)
        for unit, order in enumerate(orders)
        for index, rows in enumerate(stage_rows(order, dims, half))
    ]
    steps = len(rings[0])
    longest = max(max(ring) for ring in rings)
    turns = 1 + sum(size // 2 for _, size in dims.values())
    small = arrays[-1]
    return pl.pallas_call(
        functools.partial(sums_kernel, dims, jobs),
        out_shape=(
            jax.ShapeDtypeStruct((total, width), jnp.float32),
            jax.ShapeDtypeStruct(small.shape, jnp.float32),
        ),
        in_specs=[pl.BlockSpec(memory_space=pl.ANY)] * 10 + [pl.BlockSpec(memory_space=pltpu.VMEM)],
        out_specs=(pl.BlockSpec(memory_space=pl.ANY), pl.BlockSpec(memory_space=pltpu.VMEM)),
        scratch_shapes=[
            pltpu.VMEM((2, tokens, job_rows), jnp.bfloat16),
            pltpu.VMEM((2, tokens, width), jnp.bfloat16),
            pltpu.VMEM((2, job_rows, width), jnp.float32),
            pltpu.VMEM((steps // 2, 3 * half, width), jnp.float32),
            pltpu.VMEM((steps, 3 * half, width), jnp.float32),
            pltpu.VMEM((3, 3 * half, width), jnp.float32),
            pltpu.VMEM((turns,) + small.shape, jnp.float32),
            pltpu.VMEM((turns,) + small.shape, jnp.float32),
            *inboxes,
            pltpu.SemaphoreType.DMA((2, 2)),
            pltpu.SemaphoreType.DMA((3 * steps, longest)),
            pltpu.SemaphoreType.DMA((3 * steps, longest)),
            pltpu.SemaphoreType.DMA((3, 2)),
            pltpu.SemaphoreType.DMA((2, turns)),
        ],
        compiler_params=pltpu.CompilerParams(
            collective_id=collective, has_side_effects=True, vmem_limit_bytes=56000000
        ),
        name="sum_weights",
    )(*arrays)


def bucket_onehot(slot_len, bucket_count):
    places = jnp.arange(slot_len, dtype=jnp.int32)
    offset = places[None, :] - places[:, None]
    spread = jnp.abs(offset)
    far_bucket = 8 + sum(((spread >= step).astype(jnp.int32) for step in far_steps))
    bucket = jnp.where(spread < 8, spread, far_bucket) + jnp.where(
        offset > 0, bucket_count // 2, 0
    ).astype(jnp.int32)
    labels = jnp.arange(bucket_count, dtype=jnp.int32)
    return (bucket[:, :, None] == labels[None, None, :]).astype(jnp.float32)


def norm_forward(values, scale_vec):
    inverse = lax.rsqrt(jnp.mean(values * values, axis=-1, keepdims=True) + epsilon)
    return (values * inverse * scale_vec, inverse)


def norm_backward(values, inverse, scale_vec, upstream):
    scaled = upstream * scale_vec
    inner_mean = jnp.mean(scaled * values, axis=-1, keepdims=True)
    grad_values = inverse * scaled - values * (inverse * inverse * inverse) * inner_mean
    grad_scale = jnp.sum(upstream * values * inverse, axis=0)
    return (grad_values, grad_scale)


def local(
    batch_size,
    tokens,
    lengths,
    prefixes,
    positives,
    gain_attention,
    query_weight,
    key_weight,
    value_weight,
    output_weight,
    bucket_bias,
    gain_feedforward,
    widen_weight,
    narrow_weight,
    gain_final,
):
    seqs = lengths.shape[1]
    rows = tokens.shape[1]
    slot_len = rows // seqs
    width = tokens.shape[2]
    heads = bucket_bias.shape[1]
    head_dim = query_weight.shape[1] // heads
    inner = heads * head_dim
    tokens_f = tokens[0].astype(jnp.float32)
    seq_lengths = lengths[0]
    seq_prefix = prefixes[0]
    onehot = bucket_onehot(slot_len, bucket_bias.shape[0])
    bias = jnp.einsum("ijb,bh->hij", onehot, bucket_bias, precision=highest)
    normed_f, inverse_first = norm_forward(tokens_f, gain_attention)
    normed = normed_f.astype(jnp.bfloat16)

    def project(matrix):
        projected = jnp.dot(normed, matrix, preferred_element_type=jnp.float32).astype(jnp.bfloat16)
        return projected.reshape(seqs, slot_len, heads, head_dim)

    query_all = project(query_weight)
    key_all = project(key_weight)
    value_all = project(value_weight)
    places = jnp.arange(slot_len, dtype=jnp.int32)
    valid = places[None, :] < seq_lengths[:, None]

    def score_block(query_rows, key_rows, valid_keys):
        raw_scores = jnp.einsum(
            "ihd,jhd->hij", query_rows, key_rows, preferred_element_type=jnp.float32
        )
        return jnp.where(valid_keys[None, None, :], raw_scores + bias, masked_score)

    def attend_forward(parts):
        query_rows, key_rows, value_rows, valid_keys = parts
        scores = score_block(query_rows, key_rows, valid_keys)
        row_peak = jnp.max(scores, axis=-1, keepdims=True)
        raised = jnp.exp(scores - row_peak)
        totals = jnp.sum(raised, axis=-1, keepdims=True)
        soft_low = (raised / totals).astype(jnp.bfloat16)
        context = jnp.einsum(
            "hij,jhd->ihd", soft_low, value_rows, preferred_element_type=jnp.float32
        )
        return (context.astype(jnp.bfloat16), (row_peak + jnp.log(totals))[:, :, 0])

    context, log_totals = lax.map(attend_forward, (query_all, key_all, value_all, valid))
    context_flat = context.reshape(rows, inner)
    mixed = tokens_f + jnp.dot(context_flat, output_weight, preferred_element_type=jnp.float32)
    ffn_in_f, inverse_second = norm_forward(mixed, gain_feedforward)
    ffn_in = ffn_in_f.astype(jnp.bfloat16)
    pre_act = jnp.dot(ffn_in, widen_weight, preferred_element_type=jnp.float32)
    hidden = jnp.where(pre_act > 0, pre_act, 0.0).astype(jnp.bfloat16)
    output = mixed + jnp.dot(hidden, narrow_weight, preferred_element_type=jnp.float32)
    final, inverse_third = norm_forward(output, gain_final)
    pool_mask = ((places[None, :] >= seq_prefix[:, None]) & valid).astype(jnp.float32)
    pool_weight = pool_mask / jnp.sum(pool_mask, axis=1, keepdims=True)
    pooled = jnp.sum(final.reshape(seqs, slot_len, width) * pool_weight[:, :, None], axis=1)
    inverse_pool = lax.rsqrt(jnp.sum(pooled * pooled, axis=-1, keepdims=True) + epsilon)
    unit = pooled * inverse_pool
    gathered = gather_blocks(unit, batch_size, 0).reshape(2 * batch_size * seqs, width)
    total_seqs = gathered.shape[0] // 2
    query_units = gathered[:total_seqs]
    doc_units = gathered[total_seqs:]
    scores = score_scale * jnp.dot(query_units, doc_units.T, precision=highest)
    labels = jnp.arange(total_seqs, dtype=jnp.int32)
    target = (positives[:, None] == labels[None, :]).astype(jnp.float32)
    row_peak = jnp.max(scores, axis=1, keepdims=True)
    row_raised = jnp.exp(scores - row_peak)
    row_sum = jnp.sum(row_raised, axis=1, keepdims=True)
    col_peak = jnp.max(scores, axis=0, keepdims=True)
    col_raised = jnp.exp(scores - col_peak)
    col_sum = jnp.sum(col_raised, axis=0, keepdims=True)
    loss_value = (
        0.5 * jnp.sum(row_peak[:, 0] + jnp.log(row_sum[:, 0]))
        + 0.5 * jnp.sum(col_peak[0] + jnp.log(col_sum[0]))
        - jnp.sum(target * scores)
    )
    score_grad = 0.5 * row_raised / row_sum + 0.5 * col_raised / col_sum - target
    tower = lax.axis_index("tower")
    first_row = lax.axis_index("batch") * seqs
    my_rows = lax.dynamic_slice_in_dim(score_grad, first_row, seqs, 0)
    my_cols = lax.dynamic_slice_in_dim(score_grad, first_row, seqs, 1)
    grad_as_query = score_scale * jnp.dot(my_rows, doc_units, precision=highest)
    grad_as_doc = score_scale * jnp.dot(my_cols.T, query_units, precision=highest)
    grad_unit = jnp.where(tower == 0, grad_as_query, grad_as_doc)
    cubed = inverse_pool * inverse_pool * inverse_pool
    grad_pooled = inverse_pool * grad_unit - pooled * cubed * jnp.sum(
        grad_unit * pooled, axis=-1, keepdims=True
    )
    grad_fin = (pool_weight[:, :, None] * grad_pooled[:, None, :]).reshape(rows, width)
    grad_out, grad_final = norm_backward(output, inverse_third, gain_final, grad_fin)
    grad_branch = grad_out.astype(jnp.bfloat16)
    grad_hidden = jnp.einsum(
        "td,fd->tf", grad_branch, narrow_weight, preferred_element_type=jnp.float32
    )
    grad_pre = jnp.where(pre_act > 0, grad_hidden, 0.0).astype(jnp.bfloat16)
    grad_ffn_in = jnp.einsum(
        "tf,df->td", grad_pre, widen_weight, preferred_element_type=jnp.float32
    )
    grad_mixed_norm, grad_feedforward = norm_backward(
        mixed, inverse_second, gain_feedforward, grad_ffn_in
    )
    grad_mixed = grad_out + grad_mixed_norm
    grad_attn = grad_mixed.astype(jnp.bfloat16)
    grad_context = jnp.einsum(
        "td,id->ti", grad_attn, output_weight, preferred_element_type=jnp.float32
    )
    grad_context = grad_context.astype(jnp.bfloat16).reshape(seqs, slot_len, heads, head_dim)

    def attend_backward(bias_total, parts):
        query_rows, key_rows, value_rows, valid_keys, log_rows, context_grad = parts
        scores_here = score_block(query_rows, key_rows, valid_keys)
        soft = jnp.exp(scores_here - log_rows[:, :, None])
        soft_low = soft.astype(jnp.bfloat16)
        value_part = jnp.einsum(
            "hij,ihd->jhd", soft_low, context_grad, preferred_element_type=jnp.float32
        )
        grad_soft = jnp.einsum(
            "ihd,jhd->hij", context_grad, value_rows, preferred_element_type=jnp.float32
        )
        grad_scores = soft * (grad_soft - jnp.sum(grad_soft * soft, axis=-1, keepdims=True))
        scores_low = grad_scores.astype(jnp.bfloat16)
        query_part = jnp.einsum(
            "hij,jhd->ihd", scores_low, key_rows, preferred_element_type=jnp.float32
        )
        key_part = jnp.einsum(
            "hij,ihd->jhd", scores_low, query_rows, preferred_element_type=jnp.float32
        )
        return (
            bias_total + grad_scores,
            (
                query_part.astype(jnp.bfloat16),
                key_part.astype(jnp.bfloat16),
                value_part.astype(jnp.bfloat16),
            ),
        )

    bias_total, (query_grads, key_grads, value_grads) = lax.scan(
        attend_backward,
        jnp.zeros(bias.shape, jnp.float32),
        (query_all, key_all, value_all, valid, log_totals, grad_context),
    )
    query_grads = query_grads.reshape(rows, inner)
    key_grads = key_grads.reshape(rows, inner)
    value_grads = value_grads.reshape(rows, inner)
    grad_bucket = jnp.einsum("ijb,hij->bh", onehot, bias_total, precision=highest)
    grad_normed = (
        jnp.einsum("ti,di->td", query_grads, query_weight, preferred_element_type=jnp.float32)
        + jnp.einsum("ti,di->td", key_grads, key_weight, preferred_element_type=jnp.float32)
        + jnp.einsum("ti,di->td", value_grads, value_weight, preferred_element_type=jnp.float32)
    )
    grad_tokens_norm, grad_attention = norm_backward(
        tokens_f, inverse_first, gain_attention, grad_normed
    )
    token_gradient = (grad_mixed + grad_tokens_norm).astype(jnp.bfloat16)[None]
    buckets = grad_bucket.reshape(-1)
    lines = [grad_attention, grad_feedforward, grad_final]
    lines.append(jnp.pad(buckets, (0, width - buckets.shape[0])))
    block = jnp.concatenate([jnp.stack(lines), jnp.zeros((4, width), jnp.float32)])
    weights, sums = sum_weights(
        batch_size, 1, hidden, ffn_in, context_flat, normed,
        grad_branch, grad_pre, grad_attn, query_grads, key_grads, value_grads, block,
    )
    sum_attention, sum_feedforward, sum_final = sums[0], sums[1], sums[2]
    sum_bucket = sums[3, : buckets.shape[0]].reshape(grad_bucket.shape)
    ff = hidden.shape[1]
    sum_narrow = weights[:ff]
    sum_widen = weights[ff : 2 * ff].reshape(ff // width, width, width)
    sum_widen = sum_widen.transpose(1, 0, 2).reshape(width, ff)
    sum_output, sum_query, sum_key, sum_value = (
        weights[2 * ff + n * width : 2 * ff + (n + 1) * width] for n in range(4)
    )
    return (
        loss_value,
        my_rows,
        token_gradient,
        sum_attention,
        sum_query,
        sum_key,
        sum_value,
        sum_output,
        sum_bucket,
        sum_feedforward,
        sum_widen,
        sum_narrow,
        sum_final,
    )


def solution(mesh):
    placed = (
        P("tower", "batch", None),
        P("tower", "batch"),
        P("tower", "batch"),
        P(),
        P(),
        P(),
        P(),
        P(),
        P(),
        P(),
        P(),
        P(),
        P(),
        P(),
    )
    return jax.shard_map(
        functools.partial(local, mesh.shape["batch"]),
        mesh=mesh,
        in_specs=placed,
        out_specs=(
            P(),
            P("batch", None),
            P("tower", "batch", None),
            P(),
            P(),
            P(),
            P(),
            P(),
            P(),
            P(),
            P(),
            P(),
            P(),
        ),
        check_vma=False,
    )
```

```python
import functools

import jax
import jax.numpy as jnp
from jax import lax
from jax.experimental import pallas as pl
from jax.experimental.pallas import tpu as pltpu
from jax.sharding import PartitionSpec as P

epsilon = 1e-06
masked_score = -1000000000.0
score_scale = 100.0
far_steps = (12, 16, 23, 32, 46, 64, 91)
highest = lax.Precision.HIGHEST


MESH = pl.DeviceIdType.MESH
job_rows = 384
unit_rows = 128


def batch_dims(size):
    sizes = {16: (2, 2, 4), 64: (4, 4, 4)}[size]
    strides = (1, sizes[0], sizes[0] * sizes[1])
    return dict(zip("xyz", zip(strides, sizes)))


def place():
    return lax.axis_index("tower"), lax.axis_index("batch")


def gather_kernel(groups, block_ref, out_ref, slots, send_sem, recv_sem, mate_sem):
    tower, batch = place()
    barrier = pltpu.get_barrier_semaphore()
    mate = (1 - tower, batch)

    def peer(step):
        return tower, lax.rem(batch + step, groups)

    def greet(step, carry):
        pl.semaphore_signal(barrier, 1, device_id=peer(step), device_id_type=MESH)
        return carry

    lax.fori_loop(1, groups, greet, 0)
    pl.semaphore_signal(barrier, 1, device_id=mate, device_id_type=MESH)
    slots[tower, batch] = block_ref[...]
    pl.semaphore_wait(barrier, groups)

    def copy(step, owner):
        return pltpu.make_async_remote_copy(
            src_ref=block_ref,
            dst_ref=slots.at[tower, owner],
            send_sem=send_sem.at[step],
            recv_sem=recv_sem.at[owner],
            device_id=peer(step),
            device_id_type=MESH,
        )

    def begin(step, carry):
        copy(step, batch).start()
        return carry

    def finish(step, carry):
        copy(step, batch).wait_send()
        copy(step, peer(step)[1]).wait_recv()
        return carry

    lax.fori_loop(1, groups, begin, 0)
    lax.fori_loop(1, groups, finish, 0)
    side = pltpu.make_async_remote_copy(
        src_ref=slots.at[tower],
        dst_ref=slots.at[tower],
        send_sem=mate_sem.at[0],
        recv_sem=mate_sem.at[1],
        device_id=mate,
        device_id_type=MESH,
    )
    side.start()
    side.wait()
    out_ref[...] = slots[...]


def gather_blocks(block, groups, collective):
    whole = (2, groups) + block.shape
    return pl.pallas_call(
        functools.partial(gather_kernel, groups),
        out_shape=jax.ShapeDtypeStruct(whole, jnp.float32),
        in_specs=[pl.BlockSpec(memory_space=pltpu.VMEM)],
        out_specs=pl.BlockSpec(memory_space=pltpu.VMEM),
        scratch_shapes=[
            pltpu.VMEM(whole, jnp.float32),
            pltpu.SemaphoreType.DMA((groups,)),
            pltpu.SemaphoreType.DMA((groups,)),
            pltpu.SemaphoreType.DMA((2,)),
        ],
        compiler_params=pltpu.CompilerParams(collective_id=collective, has_side_effects=True),
        name="gather_blocks",
    )(block)


def both(first, second):
    if first is None:
        return second
    if second is None:
        return first
    return jnp.logical_and(first, second)


def guarded(condition, action):
    if condition is None:
        action()
    else:
        pl.when(condition)(action)


def plan_unit(order, dims, batch, rows):
    add, spread = [], []
    start, active = 0, None
    for name in order:
        stride, size = dims[name]
        coord = lax.rem(batch // stride, size)
        if size == 4:
            inner = jnp.logical_or(coord == 1, coord == 2)
            outer = jnp.logical_not(inner)
            mate = batch + stride * (1 - 2 * lax.rem(coord, 2))
            add.append(
                dict(rows=rows, send=start, keep=start, peer=mate,
                     sends=both(active, outer), receives=both(active, inner)))
            spread.append(
                dict(rows=rows, send=start, peer=mate,
                     sends=both(active, inner), receives=both(active, outer)))
            active = both(active, inner)
            bit = coord // 2
            mate = batch + stride * (3 - 2 * coord)
        else:
            bit = coord
            mate = batch + stride * (1 - 2 * coord)
        rows = rows // 2
        kept = start + bit * rows
        add.append(
            dict(rows=rows, send=start + (1 - bit) * rows, keep=kept, peer=mate,
                 sends=active, receives=active))
        spread.append(dict(rows=rows, send=kept, peer=mate, sends=active, receives=active))
        start = kept
    return add, spread[::-1]


def step_rings(order, dims):
    one_way = []
    for name in order:
        one_way += [True, False] if dims[name][1] == 4 else [False]
    count = len(one_way)
    steps = 2 + 2 * count
    rings = [3] * steps
    for index, single in enumerate(one_way):
        if single:
            first, last = 1 + index, steps - 2 - index
            rings[first] = rings[last] = last - first + 2
    return rings


def stage_rows(order, dims, rows):
    result = []
    for name in order:
        if dims[name][1] == 4:
            result.append(rows)
        rows //= 2
        result.append(rows)
    return result


orders = ("xyz", "yxz", "zxy")


def sums_kernel(dims, jobs, *refs):
    (hidden, ffn_in, context, normed, branch, pre, attn, dq, dk, dv, small, out, small_out) = refs[:13]
    (left, right, part, acc, full, mate_in, small_own, small_in) = refs[13:21]
    rest = refs[21:]
    counts = [len(stage_rows(order, dims, 8)) for order in orders]
    inbox, where = [], 0
    for count in counts:
        inbox.append(rest[where : where + count])
        where += count
    load_sem, send_sem, recv_sem, keep_sem, small_sem = rest[where:]
    tower, batch = place()
    half = unit_rows // 2
    steps = 2 + 2 * counts[0]
    plans = [plan_unit(order, dims, batch, half) for order in orders]
    rings = [step_rings(order, dims) for order in orders]
    held, spread_held = acc.shape[0], full.shape[0]

    barrier = pltpu.get_barrier_semaphore()
    mate = (1 - tower, batch)
    mates, turns = [mate], [mate]
    for stride, size in dims.values():
        coord = lax.rem(batch // stride, size)
        near = (tower, batch + stride * (1 - 2 * lax.rem(coord, 2)))
        mates.append(near)
        turns.append(near)
        if size == 4:
            mates.append((tower, batch + stride * (3 - 2 * coord)))
            turns.append((tower, batch + stride * (2 - 4 * (coord // 2))))
            mates.append(turns[-1])
    for mate in mates:
        pl.semaphore_signal(barrier, 1, device_id=mate, device_id_type=MESH)
    pl.semaphore_wait(barrier, len(mates))

    width = out.shape[1]

    def load(job, begin):
        slot = lax.rem(job, 2)

        def copies(left_ref, left_block, right_ref, right_block):
            for index, (ref, block, size, target) in enumerate(
                ((left_ref, left_block, job_rows, left), (right_ref, right_block, width, right))
            ):
                columns = pl.ds(pl.multiple_of(block * size, 128), size)
                copy = pltpu.make_async_copy(
                    ref.at[:, columns], target.at[slot], load_sem.at[index, slot]
                )
                copy.start() if begin else copy.wait()

        if not begin:
            copies(hidden, 0, branch, 0)
            return
        per_narrow = hidden.shape[1] // job_rows
        per_side = width // job_rows
        first = 0
        table = [(hidden, branch, per_narrow)]
        table.append((ffn_in, pre, per_narrow))
        table += [(context, attn, per_side), (normed, dq, per_side), (normed, dk, per_side), (normed, dv, per_side)]
        for index, (left_ref, right_ref, count) in enumerate(table):
            local = job - first

            def go(local=local, left_ref=left_ref, right_ref=right_ref, index=index):
                if index == 1:
                    copies(left_ref, lax.rem(local, per_side), right_ref, local // per_side)
                else:
                    copies(left_ref, local, right_ref, 0)

            pl.when(jnp.logical_and(local >= 0, local < count))(go)
            first += count

    def compute(job):
        slot = lax.rem(job, 2)
        load(job, False)
        pl.when(job + 1 < jobs)(lambda: load(job + 1, True))
        part[slot] = lax.dot_general(
            left[slot], right[slot], (((0,), (0,)), ((), ())), preferred_element_type=jnp.float32
        )

    def remote(unit, step, job):
        add, spread = plans[unit]
        turn = lax.rem(job, rings[unit][step])
        place_in = lax.rem(job, held)
        sems = dict(
            send_sem=send_sem.at[unit * steps + step, turn],
            recv_sem=recv_sem.at[unit * steps + step, turn],
            device_id_type=MESH,
        )
        base = unit * half
        if step == 0:
            src = part.at[lax.rem(job, 2), pl.ds(pl.multiple_of(unit * unit_rows + (1 - tower) * half, 8), half)]
            dst = mate_in.at[turn, pl.ds(base, half)]
            return pltpu.make_async_remote_copy(src, dst, device_id=(1 - tower, batch), **sems), None, None
        if step == steps - 1:
            src = full.at[lax.rem(job, spread_held), pl.ds(base, half)]
            first = pl.multiple_of(job * job_rows + unit * unit_rows + tower * half, 8)
            dst = out.at[pl.ds(first, half)]
            return pltpu.make_async_remote_copy(src, dst, device_id=(1 - tower, batch), **sems), None, None
        count = counts[unit]
        item = add[step - 1] if step <= count else spread[step - 1 - count]
        rows = pl.ds(pl.multiple_of(base + item["send"], 8), item["rows"])
        if step <= count:
            src, dst = acc.at[place_in, rows], inbox[unit][step - 1].at[turn]
        else:
            src = dst = full.at[lax.rem(job, spread_held), rows]
        copy = pltpu.make_async_remote_copy(src, dst, device_id=(tower, item["peer"]), **sems)
        return copy, item["sends"], item["receives"]

    def keep(unit, job):
        base = unit * half
        first = pl.multiple_of(job * job_rows + unit * unit_rows + tower * half, 8)
        return pltpu.make_async_copy(
            full.at[lax.rem(job, spread_held), pl.ds(base, half)], out.at[pl.ds(first, half)], keep_sem.at[unit, lax.rem(job, 2)]
        )

    def finish(unit, step, job):
        copy, sends, receives = remote(unit, step, job)
        add, _ = plans[unit]
        base = unit * half
        guarded(sends, copy.wait_send)
        turn = lax.rem(job, rings[unit][step])
        place_in = lax.rem(job, held)

        def arrived():
            copy.wait_recv()
            if step == 0:
                own = pl.ds(pl.multiple_of(unit * unit_rows + tower * half, 8), half)
                acc[place_in, pl.ds(base, half)] = part[lax.rem(job, 2), own] + mate_in[turn, pl.ds(base, half)]
            elif step <= counts[unit]:
                item = add[step - 1]
                rows = pl.ds(pl.multiple_of(base + item["keep"], 8), item["rows"])
                total = acc[place_in, rows] + inbox[unit][step - 1][turn]
                if step == counts[unit]:
                    full[lax.rem(job, spread_held), rows] = total
                else:
                    acc[place_in, rows] = total

        guarded(receives, arrived)
        if step == steps - 1:
            keep(unit, job).wait()

    def advance(step, job):
        for unit in range(len(orders)):
            if step > 0:
                finish(unit, step - 1, job)
            if step < steps:
                copy, sends, _ = remote(unit, step, job)
                guarded(sends, copy.start)
                if step == steps - 1:
                    keep(unit, job).start()

    def small_copy(turn):
        return pltpu.make_async_remote_copy(
            src_ref=small_own.at[turn],
            dst_ref=small_in.at[turn],
            send_sem=small_sem.at[0, turn],
            recv_sem=small_sem.at[1, turn],
            device_id=turns[turn],
            device_id_type=MESH,
        )

    def small_turn(turn):
        if turn == 0:
            small_own[0] = small[...]
        else:
            small_copy(turn - 1).wait()
            total = small_own[turn - 1] + small_in[turn - 1]
            if turn == len(turns):
                small_out[...] = total
            else:
                small_own[turn] = total
        if turn < len(turns):
            small_copy(turn).start()

    load(0, True)

    def slot(time, carry):
        for step in range(steps, -1, -1):
            job = time - 1 - step
            pl.when(jnp.logical_and(job >= 0, job < jobs))(functools.partial(advance, step, job))
        for turn in range(len(turns) + 1):
            pl.when(time == turn)(functools.partial(small_turn, turn))
        pl.when(time < jobs)(functools.partial(compute, time))
        return carry

    lax.fori_loop(0, jobs + steps + 1, slot, 0)


def sum_weights(batch_size, collective, *arrays):
    hidden, normed = arrays[0], arrays[3]
    tokens, width = normed.shape
    total = 2 * hidden.shape[1] + 4 * width
    jobs = total // job_rows
    dims = batch_dims(batch_size)
    half = unit_rows // 2
    rings = [step_rings(order, dims) for order in orders]
    inboxes = [
        pltpu.VMEM((rings[unit][1 + index], rows, width), jnp.float32)
        for unit, order in enumerate(orders)
        for index, rows in enumerate(stage_rows(order, dims, half))
    ]
    steps = len(rings[0])
    longest = max(max(ring) for ring in rings)
    turns = 1 + sum(size // 2 for _, size in dims.values())
    small = arrays[-1]
    return pl.pallas_call(
        functools.partial(sums_kernel, dims, jobs),
        out_shape=(
            jax.ShapeDtypeStruct((total, width), jnp.float32),
            jax.ShapeDtypeStruct(small.shape, jnp.float32),
        ),
        in_specs=[pl.BlockSpec(memory_space=pl.ANY)] * 10 + [pl.BlockSpec(memory_space=pltpu.VMEM)],
        out_specs=(pl.BlockSpec(memory_space=pl.ANY), pl.BlockSpec(memory_space=pltpu.VMEM)),
        scratch_shapes=[
            pltpu.VMEM((2, tokens, job_rows), jnp.bfloat16),
            pltpu.VMEM((2, tokens, width), jnp.bfloat16),
            pltpu.VMEM((2, job_rows, width), jnp.float32),
            pltpu.VMEM((steps // 2, 3 * half, width), jnp.float32),
            pltpu.VMEM((steps, 3 * half, width), jnp.float32),
            pltpu.VMEM((3, 3 * half, width), jnp.float32),
            pltpu.VMEM((turns,) + small.shape, jnp.float32),
            pltpu.VMEM((turns,) + small.shape, jnp.float32),
            *inboxes,
            pltpu.SemaphoreType.DMA((2, 2)),
            pltpu.SemaphoreType.DMA((3 * steps, longest)),
            pltpu.SemaphoreType.DMA((3 * steps, longest)),
            pltpu.SemaphoreType.DMA((3, 2)),
            pltpu.SemaphoreType.DMA((2, turns)),
        ],
        compiler_params=pltpu.CompilerParams(
            collective_id=collective, has_side_effects=True, vmem_limit_bytes=56000000
        ),
        name="sum_weights",
    )(*arrays)


tile = 128
near = 3 * tile


def bias_lines(bucket_bias, mirrored):
    buckets, heads = bucket_bias.shape
    spots = jnp.arange(4 * tile, dtype=jnp.int32)
    moved = jnp.where(spots >= near, spots - 4 * tile, spots)
    offset = tile - moved if mirrored else moved - tile
    onehot = offset_onehot(offset, buckets)
    lines = jnp.dot(bucket_bias.T, onehot.T, precision=highest)
    return jnp.pad(lines, ((0, 16 - heads), (0, 0)))


def offset_onehot(offset, buckets):
    spread = jnp.abs(offset)
    far_bucket = 8 + sum(((spread >= step).astype(jnp.int32) for step in far_steps))
    bucket = jnp.where(spread < 8, spread, far_bucket) + jnp.where(offset > 0, buckets // 2, 0)
    return (bucket[:, None] == jnp.arange(buckets, dtype=jnp.int32)[None, :]).astype(jnp.float32)


def spread_bias(lines_ref, near_ref, heads):
    for head in range(heads):
        line = jnp.broadcast_to(lines_ref[head : head + 1, :], (tile, 4 * tile))
        near_ref[head] = pltpu.roll(line, 0, 1, stride=1, stride_axis=0)[:, :near]


def bias_row(near_ref, head, block, blocks, low_far, high_far, mirrored):
    parts = []
    for other in range(blocks):
        ahead = block - other if mirrored else other - block
        if abs(ahead) <= 1:
            spot = 1 - ahead if mirrored else 1 + ahead
            parts.append(near_ref[head, :, spot * tile : (spot + 1) * tile])
        else:
            parts.append(jnp.full((tile, tile), high_far if ahead > 0 else low_far, jnp.float32))
    return jnp.concatenate(parts, axis=1)


def unit_scale(values):
    return lax.rsqrt(jnp.mean(values * values, axis=-1, keepdims=True) + epsilon)


def low_dot(left, right):
    return jnp.dot(left, right, preferred_element_type=jnp.float32)


def dot_across(left, right):
    return lax.dot_general(left, right, (((1,), (1,)), ((), ())), preferred_element_type=jnp.float32)


def forward_kernel(
    lengths, prefixes, far, x_ref, lines_ref, gain_a, wq, wk, wv, wo, gain_f, widen, narrow, gain_z,
    normed_ref, q_ref, k_ref, v_ref, lse_ref, context_ref, mixed_ref, ffn_ref, hidden_ref, output_ref, pooled_ref,
    near_ref, lse_cols,
):
    seq = pl.program_id(0)
    heads = far.shape[1]
    slot_len, width = x_ref.shape
    blocks = slot_len // tile
    pair = 2 * width // heads
    length = lengths[seq]
    pl.when(seq == 0)(lambda: spread_bias(lines_ref, near_ref, heads))
    tokens = x_ref[...].astype(jnp.float32)
    normed = (tokens * unit_scale(tokens) * gain_a[...]).astype(jnp.bfloat16)
    normed_ref[...] = normed
    q_ref[...] = low_dot(normed, wq[...]).astype(jnp.bfloat16)
    k_ref[...] = low_dot(normed, wk[...]).astype(jnp.bfloat16)
    v_ref[...] = low_dot(normed, wv[...]).astype(jnp.bfloat16)
    lanes = lax.broadcasted_iota(jnp.int32, (1, pair), 1)
    valid = lax.broadcasted_iota(jnp.int32, (1, slot_len), 1) < length
    columns = lax.broadcasted_iota(jnp.int32, (tile, tile), 1)

    def attend(index, carry):
        span = pl.ds(pl.multiple_of(index * pair, pair), pair)
        keys = k_ref[:, span]
        queries = q_ref[:, span]
        values = v_ref[:, span]
        total = None
        for side in range(2):
            head = 2 * index + side
            mine = (lanes // (pair // 2) == side).astype(jnp.bfloat16)
            raw = dot_across(queries * mine, keys)
            rows = []
            for block in range(blocks):
                part = slice(block * tile, (block + 1) * tile)
                bias = bias_row(near_ref, head, block, blocks, far[0, head], far[1, head], False)
                scores = jnp.where(valid, raw[part] + bias, masked_score)
                peak = jnp.max(scores, axis=-1, keepdims=True)
                raised = jnp.exp(scores - peak)
                total_raised = jnp.sum(raised, axis=-1, keepdims=True)
                rows.append((raised * (1.0 / total_raised)).astype(jnp.bfloat16))
                lse_cols[part] = jnp.where(columns == head, peak + jnp.log(total_raised), lse_cols[part])
            soft_low = jnp.concatenate(rows, axis=0)
            piece = low_dot(soft_low, values * mine)
            total = piece if total is None else total + piece
        context_ref[:, span] = total.astype(jnp.bfloat16)
        return carry

    lax.fori_loop(0, heads // 2, attend, 0)
    lse_ref[0] = lse_cols[...].T[: lse_ref.shape[1]]
    mixed = tokens + low_dot(context_ref[...], wo[...])
    mixed_ref[...] = mixed
    ffn_in = (mixed * unit_scale(mixed) * gain_f[...]).astype(jnp.bfloat16)
    ffn_ref[...] = ffn_in
    output_ref[...] = mixed

    def feed(index, carry):
        span = pl.ds(pl.multiple_of(index * width, 128), width)
        pre_act = low_dot(ffn_ref[...], widen[:, span])
        hidden = jnp.where(pre_act > 0, pre_act, 0.0).astype(jnp.bfloat16)
        hidden_ref[:, span] = hidden
        output_ref[...] += low_dot(hidden, narrow[span, :])
        return carry

    lax.fori_loop(0, widen.shape[1] // width, feed, 0)
    output = output_ref[...]
    places = lax.broadcasted_iota(jnp.int32, (slot_len, 1), 0)
    mask = jnp.logical_and(places >= prefixes[seq], places < length).astype(jnp.float32)
    count = (length - prefixes[seq]).astype(jnp.float32)
    final = output * unit_scale(output) * gain_z[...]
    pooled_ref[0] = jnp.sum(final * (mask / count), axis=0, keepdims=True)


def run_forward(tokens, lengths, prefixes, far, lines, gains, weights):
    rows, width = tokens.shape
    seqs = lengths.shape[0]
    slot_len = rows // seqs
    heads = far.shape[1]
    wq, wk, wv, wo, widen, narrow = weights
    gain_a, gain_f, gain_z = gains
    ff = widen.shape[1]

    def whole(shape):
        return pl.BlockSpec(shape, lambda n, *_: (0,) * len(shape), pipeline_mode=pl.Buffered(1))

    def block(columns):
        return pl.BlockSpec((slot_len, columns), lambda n, *_: (n, 0))

    square = whole((width, width))
    line = whole((1, width))
    low, full = jnp.bfloat16, jnp.float32

    def shape(columns, kind):
        return jax.ShapeDtypeStruct((rows, columns), kind)

    return pl.pallas_call(
        forward_kernel,
        grid_spec=pltpu.PrefetchScalarGridSpec(
            num_scalar_prefetch=3,
            grid=(seqs,),
            in_specs=[
                block(width), whole((16, 4 * tile)), line, square, square, square, square,
                line, whole((width, ff)), whole((ff, width)), line,
            ],
            out_specs=[
                block(width), block(width), block(width), block(width),
                pl.BlockSpec((1, 16, slot_len), lambda n, *_: (n, 0, 0)),
                block(width), block(width), block(width), block(ff), block(width),
                pl.BlockSpec((1, 1, width), lambda n, *_: (n, 0, 0)),
            ],
            scratch_shapes=[
                pltpu.VMEM((heads, tile, near), jnp.float32),
                pltpu.VMEM((slot_len, tile), jnp.float32),
            ],
        ),
        out_shape=(
            shape(width, low), shape(width, low), shape(width, low), shape(width, low),
            jax.ShapeDtypeStruct((seqs, 16, slot_len), full),
            shape(width, low), shape(width, full), shape(width, low), shape(ff, low), shape(width, full),
            jax.ShapeDtypeStruct((seqs, 1, width), full),
        ),
        compiler_params=pltpu.CompilerParams(vmem_limit_bytes=60000000),
        name="forward",
    )(lengths, prefixes, far, tokens, lines, gain_a[None], wq, wk, wv, wo, gain_f[None], widen, narrow, gain_z[None])


def norm_back(values, gain, upstream):
    inverse = unit_scale(values)
    scaled = upstream * gain
    inner = jnp.mean(scaled * values, axis=-1, keepdims=True)
    by_values = inverse * scaled - values * (inverse * inverse * inverse) * inner
    return by_values, jnp.sum(upstream * values * inverse, axis=0, keepdims=True)


def feed_back_kernel(
    lengths, prefixes, wo, gain_f, widen, narrow, gain_z, mixed_ref, hidden_ref, output_ref, pooled_ref,
    branch_ref, pre_ref, attn_ref, context_ref, mixed_grad, gains_ref, feed_grad,
):
    seq = pl.program_id(0)
    slot_len, width = mixed_ref.shape
    length = lengths[seq]

    def clear():
        gains_ref[...] = jnp.zeros_like(gains_ref)

    pl.when(seq == 0)(clear)
    places = lax.broadcasted_iota(jnp.int32, (slot_len, 1), 0)
    mask = jnp.logical_and(places >= prefixes[seq], places < length).astype(jnp.float32)
    count = (length - prefixes[seq]).astype(jnp.float32)
    final_grad = (mask / count) * pooled_ref[0]
    output_grad, final_gain = norm_back(output_ref[...], gain_z[...], final_grad)
    gains_ref[2:3] += final_gain
    mixed_grad[...] = output_grad
    branch_ref[...] = output_grad.astype(jnp.bfloat16)
    feed_grad[...] = jnp.zeros_like(feed_grad)

    def feed(index, carry):
        span = pl.ds(pl.multiple_of(index * width, 128), width)
        hidden_grad = dot_across(branch_ref[...], narrow[span, :])
        pre_grad = jnp.where(hidden_ref[:, span] > 0, hidden_grad, 0.0).astype(jnp.bfloat16)
        pre_ref[:, span] = pre_grad
        feed_grad[...] += dot_across(pre_grad, widen[:, span])
        return carry

    lax.fori_loop(0, widen.shape[1] // width, feed, 0)
    by_mixed, feed_gain = norm_back(mixed_ref[...], gain_f[...], feed_grad[...])
    gains_ref[1:2] += feed_gain
    total_grad = mixed_grad[...] + by_mixed
    mixed_grad[...] = total_grad
    attn_low = total_grad.astype(jnp.bfloat16)
    attn_ref[...] = attn_low
    context_ref[...] = dot_across(attn_low, wo[...]).astype(jnp.bfloat16)


def attend_back_kernel(
    lengths, far, x_ref, lines_ref, gain_a, wq, wk, wv, q_ref, k_ref, v_ref, lse_ref, context_grad, mixed_grad,
    dq_ref, dk_ref, dv_ref, token_ref, gains_ref, sums_ref,
    near_ref, far_sums, near_sums, soft_ref,
):
    seq = pl.program_id(0)
    heads = far.shape[1]
    slot_len, width = x_ref.shape
    blocks = slot_len // tile
    pair = 2 * width // heads
    length = lengths[seq]

    def clear():
        spread_bias(lines_ref, near_ref, heads)
        near_sums[...] = jnp.zeros_like(near_sums)
        far_sums[...] = jnp.zeros_like(far_sums)
        gains_ref[...] = jnp.zeros_like(gains_ref)

    pl.when(seq == 0)(clear)
    places = lax.broadcasted_iota(jnp.int32, (slot_len, 1), 0)
    lanes = lax.broadcasted_iota(jnp.int32, (1, pair), 1)

    def attend(index, carry):
        span = pl.ds(pl.multiple_of(index * pair, pair), pair)
        keys = k_ref[:, span]
        queries = q_ref[:, span]
        values = v_ref[:, span]
        upstream = context_grad[:, span]
        by_query = by_key = by_value = None
        for side in range(2):
            head = 2 * index + side
            mine = (lanes // (pair // 2) == side).astype(jnp.bfloat16)
            my_queries, my_upstream = queries * mine, upstream * mine
            raw = dot_across(keys, my_queries)
            soft_grad = dot_across(values, my_upstream)
            totals = lse_ref[0, pl.ds(head, 1), :]
            inner = jnp.zeros((1, slot_len), jnp.float32)
            low_rows = []
            for block in range(blocks):
                part = slice(block * tile, (block + 1) * tile)
                bias = bias_row(near_ref, head, block, blocks, far[0, head], far[1, head], True)
                scores = jnp.where(places[part] < length, raw[part] + bias, masked_score)
                soft = jnp.exp(scores - totals)
                soft_ref[part] = soft
                low_rows.append(soft.astype(jnp.bfloat16))
                inner += jnp.sum(soft * soft_grad[part], axis=0, keepdims=True)
            soft_low = jnp.concatenate(low_rows, axis=0)
            grad_rows = []
            near_total = [None] * 3
            far_total = [None] * 2
            for block in range(blocks):
                part = slice(block * tile, (block + 1) * tile)
                grads = soft_ref[part] * (soft_grad[part] - inner)
                grad_rows.append(grads.astype(jnp.bfloat16))
                for other in range(blocks):
                    piece = grads[:, other * tile : (other + 1) * tile]
                    ahead = block - other
                    group, spot = (near_total, 1 - ahead) if abs(ahead) <= 1 else (far_total, int(ahead > 0))
                    group[spot] = piece if group[spot] is None else group[spot] + piece
            for spot in range(3):
                if near_total[spot] is not None:
                    near_sums[head, :, spot * tile : (spot + 1) * tile] += near_total[spot]
            for spot in range(2):
                if far_total[spot] is not None:
                    far_sums[spot, pl.ds(head, 1), :] += jnp.sum(far_total[spot], axis=0, keepdims=True)
            grads_low = jnp.concatenate(grad_rows, axis=0)
            pieces = (
                lax.dot_general(grads_low, keys * mine, (((0,), (0,)), ((), ())), preferred_element_type=jnp.float32),
                low_dot(grads_low, my_queries),
                low_dot(soft_low, my_upstream),
            )
            if side == 0:
                by_query, by_key, by_value = pieces
            else:
                by_query, by_key, by_value = by_query + pieces[0], by_key + pieces[1], by_value + pieces[2]
        dq_ref[:, span] = by_query.astype(jnp.bfloat16)
        dk_ref[:, span] = by_key.astype(jnp.bfloat16)
        dv_ref[:, span] = by_value.astype(jnp.bfloat16)
        return carry

    lax.fori_loop(0, heads // 2, attend, 0)
    normed_grad = dot_across(dq_ref[...], wq[...]) + dot_across(dk_ref[...], wk[...])
    normed_grad += dot_across(dv_ref[...], wv[...])
    by_tokens, token_gain = norm_back(x_ref[...].astype(jnp.float32), gain_a[...], normed_grad)
    gains_ref[0:1] += token_gain
    token_ref[...] = (mixed_grad[...] + by_tokens).astype(jnp.bfloat16)

    def close():
        for head in range(heads):
            turned = jnp.concatenate([near_sums[head], jnp.zeros((tile, tile), jnp.float32)], axis=1)
            count = tile // 2
            while count:
                upper = turned[count : 2 * count]
                turned = turned[:count] + pltpu.roll(upper, 4 * tile - count, 1)
                count //= 2
            line = turned
            sums_ref[head : head + 1, :] = line
        sums_ref[:, 2 * tile : 3 * tile] += far_sums[0]
        sums_ref[:, 3 * tile : 4 * tile] += far_sums[1]

    sums_ref[...] = jnp.zeros_like(sums_ref)
    pl.when(seq == pl.num_programs(0) - 1)(close)


def whole(shape):
    return pl.BlockSpec(shape, lambda n, *_: (0,) * len(shape), pipeline_mode=pl.Buffered(1))


def run_feed_back(lengths, prefixes, gains, weights, mixed, hidden, output, pooled_grad):
    rows, width = mixed.shape
    seqs = lengths.shape[0]
    slot_len = rows // seqs
    wo, widen, narrow = weights
    ff = widen.shape[1]

    def block(columns):
        return pl.BlockSpec((slot_len, columns), lambda n, *_: (n, 0))

    def shape(columns, kind):
        return jax.ShapeDtypeStruct((rows, columns), kind)

    low, full = jnp.bfloat16, jnp.float32
    return pl.pallas_call(
        feed_back_kernel,
        grid_spec=pltpu.PrefetchScalarGridSpec(
            num_scalar_prefetch=2,
            grid=(seqs,),
            in_specs=[
                whole((width, width)), whole((1, width)), whole((width, ff)), whole((ff, width)), whole((1, width)),
                block(width), block(ff), block(width),
                pl.BlockSpec((1, 1, width), lambda n, *_: (n, 0, 0)),
            ],
            out_specs=[
                block(width), block(ff), block(width), block(width), block(width),
                pl.BlockSpec((8, width), lambda n, *_: (0, 0)),
            ],
            scratch_shapes=[pltpu.VMEM((slot_len, width), jnp.float32)],
        ),
        out_shape=(
            shape(width, low), shape(ff, low), shape(width, low), shape(width, low), shape(width, full),
            jax.ShapeDtypeStruct((8, width), full),
        ),
        compiler_params=pltpu.CompilerParams(vmem_limit_bytes=60000000),
        name="feed_back",
    )(lengths, prefixes, wo, gains[0][None], widen, narrow, gains[1][None], mixed, hidden, output, pooled_grad)


def run_attend_back(tokens, lengths, far, lines, gain, weights, saved, context_grad, mixed_grad):
    rows, width = tokens.shape
    seqs = lengths.shape[0]
    slot_len = rows // seqs
    heads = far.shape[1]

    def block(columns):
        return pl.BlockSpec((slot_len, columns), lambda n, *_: (n, 0))

    square = whole((width, width))
    low, full = jnp.bfloat16, jnp.float32
    return pl.pallas_call(
        attend_back_kernel,
        grid_spec=pltpu.PrefetchScalarGridSpec(
            num_scalar_prefetch=2,
            grid=(seqs,),
            in_specs=[
                block(width), whole((16, 4 * tile)), whole((1, width)), square, square, square,
                block(width), block(width), block(width),
                pl.BlockSpec((1, 16, slot_len), lambda n, *_: (n, 0, 0)),
                block(width), block(width),
            ],
            out_specs=[
                block(width), block(width), block(width), block(width),
                pl.BlockSpec((8, width), lambda n, *_: (0, 0)),
                pl.BlockSpec((16, 4 * tile), lambda n, *_: (0, 0)),
            ],
            scratch_shapes=[
                pltpu.VMEM((heads, tile, near), full),
                pltpu.VMEM((2, 16, tile), full),
                pltpu.VMEM((heads, tile, near), full),
                pltpu.VMEM((slot_len, slot_len), full),
            ],
        ),
        out_shape=(
            *(jax.ShapeDtypeStruct((rows, width), low) for _ in range(4)),
            jax.ShapeDtypeStruct((8, width), full),
            jax.ShapeDtypeStruct((16, 4 * tile), full),
        ),
        compiler_params=pltpu.CompilerParams(vmem_limit_bytes=60000000),
        name="attend_back",
    )(lengths, far, tokens, lines, gain[None], *weights, *saved, context_grad, mixed_grad)


def bucket_sums(offset_sums, shape):
    spots = jnp.arange(4 * tile, dtype=jnp.int32)
    moved = jnp.where(spots >= near, spots - 4 * tile, spots)
    onehot = offset_onehot(tile - moved, shape[0])
    return jnp.dot(onehot.T, offset_sums[: shape[1]].T, precision=highest)


def local(
    batch_size,
    tokens,
    lengths,
    prefixes,
    positives,
    gain_attention,
    query_weight,
    key_weight,
    value_weight,
    output_weight,
    bucket_bias,
    gain_feedforward,
    widen_weight,
    narrow_weight,
    gain_final,
):
    seqs = lengths.shape[1]
    width = tokens.shape[2]
    buckets = bucket_bias.shape[0]
    far = jnp.stack([bucket_bias[buckets // 2 - 1], bucket_bias[buckets - 1]])
    gains = (gain_attention, gain_feedforward, gain_final)
    weights = (query_weight, key_weight, value_weight, output_weight, widen_weight, narrow_weight)
    normed, query, key, value, totals, context, mixed, ffn_in, hidden, output, pooled = run_forward(
        tokens[0], lengths[0], prefixes[0], far, bias_lines(bucket_bias, False), gains, weights
    )
    pooled = pooled[:, 0]
    inverse_pool = lax.rsqrt(jnp.sum(pooled * pooled, axis=-1, keepdims=True) + epsilon)
    unit = pooled * inverse_pool
    gathered = gather_blocks(unit, batch_size, 0).reshape(2 * batch_size * seqs, width)
    total_seqs = gathered.shape[0] // 2
    query_units = gathered[:total_seqs]
    doc_units = gathered[total_seqs:]
    scores = score_scale * jnp.dot(query_units, doc_units.T, precision=highest)
    labels = jnp.arange(total_seqs, dtype=jnp.int32)
    target = (positives[:, None] == labels[None, :]).astype(jnp.float32)
    row_peak = jnp.max(scores, axis=1, keepdims=True)
    row_raised = jnp.exp(scores - row_peak)
    row_sum = jnp.sum(row_raised, axis=1, keepdims=True)
    col_peak = jnp.max(scores, axis=0, keepdims=True)
    col_raised = jnp.exp(scores - col_peak)
    col_sum = jnp.sum(col_raised, axis=0, keepdims=True)
    loss_value = (
        0.5 * jnp.sum(row_peak[:, 0] + jnp.log(row_sum[:, 0]))
        + 0.5 * jnp.sum(col_peak[0] + jnp.log(col_sum[0]))
        - jnp.sum(target * scores)
    )
    score_grad = 0.5 * row_raised / row_sum + 0.5 * col_raised / col_sum - target
    tower = lax.axis_index("tower")
    first_row = lax.axis_index("batch") * seqs
    my_rows = lax.dynamic_slice_in_dim(score_grad, first_row, seqs, 0)
    my_cols = lax.dynamic_slice_in_dim(score_grad, first_row, seqs, 1)
    grad_as_query = score_scale * jnp.dot(my_rows, doc_units, precision=highest)
    grad_as_doc = score_scale * jnp.dot(my_cols.T, query_units, precision=highest)
    grad_unit = jnp.where(tower == 0, grad_as_query, grad_as_doc)
    cubed = inverse_pool * inverse_pool * inverse_pool
    grad_pooled = inverse_pool * grad_unit - pooled * cubed * jnp.sum(
        grad_unit * pooled, axis=-1, keepdims=True
    )
    branch, pre, attn, context_grad, mixed_grad, feed_gains = run_feed_back(
        lengths[0], prefixes[0], gains[1:], weights[3:], mixed, hidden, output, grad_pooled[:, None]
    )
    by_query, by_key, by_value, token_gradient, token_gains, offset_sums = run_attend_back(
        tokens[0], lengths[0], far, bias_lines(bucket_bias, True), gain_attention, weights[:3],
        (query, key, value, totals), context_grad, mixed_grad,
    )
    gain_sums = feed_gains + token_gains
    grad_bucket = bucket_sums(offset_sums, bucket_bias.shape)
    flat = grad_bucket.reshape(-1)
    block = gain_sums.at[3, : flat.shape[0]].set(flat)
    summed, sums = sum_weights(
        batch_size, 1, hidden, ffn_in, context, normed, branch, pre, attn, by_query, by_key, by_value, block
    )
    sum_bucket = sums[3, : flat.shape[0]].reshape(bucket_bias.shape)
    ff = hidden.shape[1]
    sum_widen = summed[ff : 2 * ff].reshape(ff // width, width, width)
    sum_widen = sum_widen.transpose(1, 0, 2).reshape(width, ff)
    sum_output, sum_query, sum_key, sum_value = (
        summed[2 * ff + n * width : 2 * ff + (n + 1) * width] for n in range(4)
    )
    return (
        loss_value,
        my_rows,
        token_gradient[None],
        sums[0],
        sum_query,
        sum_key,
        sum_value,
        sum_output,
        sum_bucket,
        sums[1],
        sum_widen,
        summed[:ff],
        sums[2],
    )


def solution(mesh):
    placed = (
        P("tower", "batch", None),
        P("tower", "batch"),
        P("tower", "batch"),
        P(),
        P(),
        P(),
        P(),
        P(),
        P(),
        P(),
        P(),
        P(),
        P(),
        P(),
    )
    return jax.shard_map(
        functools.partial(local, mesh.shape["batch"]),
        mesh=mesh,
        in_specs=placed,
        out_specs=(
            P(),
            P("batch", None),
            P("tower", "batch", None),
            P(),
            P(),
            P(),
            P(),
            P(),
            P(),
            P(),
            P(),
            P(),
            P(),
        ),
        check_vma=False,
    )
```

```python
import functools

import jax
import jax.numpy as jnp
from jax import lax
from jax.experimental import pallas as pl
from jax.experimental.pallas import tpu as pltpu
from jax.sharding import PartitionSpec as P

epsilon = 1e-06
masked_score = -1000000000.0
score_scale = 100.0
far_steps = (12, 16, 23, 32, 46, 64, 91)
highest = lax.Precision.HIGHEST


MESH = pl.DeviceIdType.MESH
job_rows = 384
unit_rows = 128


def batch_dims(size):
    sizes = {16: (2, 2, 4), 64: (4, 4, 4)}[size]
    strides = (1, sizes[0], sizes[0] * sizes[1])
    return dict(zip("xyz", zip(strides, sizes)))


def place():
    return lax.axis_index("tower"), lax.axis_index("batch")


def gather_kernel(groups, block_ref, out_ref, slots, send_sem, recv_sem, mate_sem):
    tower, batch = place()
    barrier = pltpu.get_barrier_semaphore()
    mate = (1 - tower, batch)

    def peer(step):
        return tower, lax.rem(batch + step, groups)

    def greet(step, carry):
        pl.semaphore_signal(barrier, 1, device_id=peer(step), device_id_type=MESH)
        return carry

    lax.fori_loop(1, groups, greet, 0)
    pl.semaphore_signal(barrier, 1, device_id=mate, device_id_type=MESH)
    slots[tower, batch] = block_ref[...]
    pl.semaphore_wait(barrier, groups)

    def copy(step, owner):
        return pltpu.make_async_remote_copy(
            src_ref=block_ref,
            dst_ref=slots.at[tower, owner],
            send_sem=send_sem.at[step],
            recv_sem=recv_sem.at[owner],
            device_id=peer(step),
            device_id_type=MESH,
        )

    def begin(step, carry):
        copy(step, batch).start()
        return carry

    def finish(step, carry):
        copy(step, batch).wait_send()
        copy(step, peer(step)[1]).wait_recv()
        return carry

    lax.fori_loop(1, groups, begin, 0)
    lax.fori_loop(1, groups, finish, 0)
    side = pltpu.make_async_remote_copy(
        src_ref=slots.at[tower],
        dst_ref=slots.at[tower],
        send_sem=mate_sem.at[0],
        recv_sem=mate_sem.at[1],
        device_id=mate,
        device_id_type=MESH,
    )
    side.start()
    side.wait()
    out_ref[...] = slots[...]


def gather_blocks(block, groups, collective):
    whole = (2, groups) + block.shape
    return pl.pallas_call(
        functools.partial(gather_kernel, groups),
        out_shape=jax.ShapeDtypeStruct(whole, jnp.float32),
        in_specs=[pl.BlockSpec(memory_space=pltpu.VMEM)],
        out_specs=pl.BlockSpec(memory_space=pltpu.VMEM),
        scratch_shapes=[
            pltpu.VMEM(whole, jnp.float32),
            pltpu.SemaphoreType.DMA((groups,)),
            pltpu.SemaphoreType.DMA((groups,)),
            pltpu.SemaphoreType.DMA((2,)),
        ],
        compiler_params=pltpu.CompilerParams(collective_id=collective, has_side_effects=True),
        name="gather_blocks",
    )(block)


def both(first, second):
    if first is None:
        return second
    if second is None:
        return first
    return jnp.logical_and(first, second)


def guarded(condition, action):
    if condition is None:
        action()
    else:
        pl.when(condition)(action)


def plan_unit(order, dims, batch, rows):
    add, spread = [], []
    start, active = 0, None
    for name in order:
        stride, size = dims[name]
        coord = lax.rem(batch // stride, size)
        if size == 4:
            inner = jnp.logical_or(coord == 1, coord == 2)
            outer = jnp.logical_not(inner)
            mate = batch + stride * (1 - 2 * lax.rem(coord, 2))
            add.append(
                dict(rows=rows, send=start, keep=start, peer=mate,
                     sends=both(active, outer), receives=both(active, inner)))
            spread.append(
                dict(rows=rows, send=start, peer=mate,
                     sends=both(active, inner), receives=both(active, outer)))
            active = both(active, inner)
            bit = coord // 2
            mate = batch + stride * (3 - 2 * coord)
        else:
            bit = coord
            mate = batch + stride * (1 - 2 * coord)
        rows = rows // 2
        kept = start + bit * rows
        add.append(
            dict(rows=rows, send=start + (1 - bit) * rows, keep=kept, peer=mate,
                 sends=active, receives=active))
        spread.append(dict(rows=rows, send=kept, peer=mate, sends=active, receives=active))
        start = kept
    return add, spread[::-1]


def one_way_steps(order, dims):
    flags = []
    for name in order:
        flags += [True, False] if dims[name][1] == 4 else [False]
    return flags


def step_rings(order, dims):
    flags = one_way_steps(order, dims)
    steps = 2 + 2 * len(flags)
    rings = [3] * steps
    for index, single in enumerate(flags):
        if single:
            first, last = 1 + index, steps - 2 - index
            rings[last] = last - first + 2
    return rings


def stage_rows(order, dims, rows):
    result = []
    for name in order:
        if dims[name][1] == 4:
            result.append(rows)
        rows //= 2
        result.append(rows)
    return result


orders = ("xyz", "yxz", "zxy")


def sums_kernel(dims, jobs, *refs):
    (lengths, far, hidden, ffn_in, context, normed, branch, pre, attn, query, key, value, upstream) = refs[:13]
    (tokens, mixed_grad, small, totals, lines, gain, wq, wk, wv) = refs[13:22]
    (out, token_out, small_out) = refs[22:25]
    (left, right, part, acc, full, mate_in, small_own, small_in, heads_in, by_query, by_key, by_value) = refs[25:37]
    (near_ref, near_sums, far_sums, soft_ref, token_in, mixed_in, token_buffer) = refs[37:44]
    rest = refs[44:]
    counts = [len(stage_rows(order, dims, 8)) for order in orders]
    inbox, where = [], 0
    for count in counts:
        inbox.append(rest[where : where + count])
        where += count
    load_sem, send_sem, recv_sem, keep_sem, small_sem, heads_sem, token_sem, credit = rest[where:]
    tower, batch = place()
    half = unit_rows // 2
    steps = 2 + 2 * counts[0]
    slots = jobs + steps + 1
    plans = [plan_unit(order, dims, batch, half) for order in orders]
    rings = [step_rings(order, dims) for order in orders]
    single = [one_way_steps(order, dims) for order in orders]
    held, spread_held = acc.shape[0], full.shape[0]
    width = out.shape[1]
    heads = far.shape[1]
    seqs = lengths.shape[0]
    slot_len = tokens.shape[0] // seqs
    pair = 2 * width // heads
    pairs = heads // 2
    tasks = seqs * pairs
    blocks = slot_len // tile

    barrier = pltpu.get_barrier_semaphore()
    mate = (1 - tower, batch)
    mates, turns = [mate], [mate]
    for stride, size in dims.values():
        coord = lax.rem(batch // stride, size)
        near_mate = (tower, batch + stride * (1 - 2 * lax.rem(coord, 2)))
        mates.append(near_mate)
        turns.append(near_mate)
        if size == 4:
            mates.append((tower, batch + stride * (3 - 2 * coord)))
            turns.append((tower, batch + stride * (2 - 4 * (coord // 2))))
            mates.append(turns[-1])
    for other in mates:
        pl.semaphore_signal(barrier, 1, device_id=other, device_id_type=MESH)

    def load(job, begin):
        slot = lax.rem(job, 2)

        def copies(left_ref, left_block, right_ref, right_block):
            for index, (ref, block, size, target) in enumerate(
                ((left_ref, left_block, job_rows, left), (right_ref, right_block, width, right))
            ):
                columns = pl.ds(pl.multiple_of(block * size, 128), size)
                copy = pltpu.make_async_copy(
                    ref.at[:, columns], target.at[slot], load_sem.at[index, slot]
                )
                copy.start() if begin else copy.wait()

        if not begin:
            copies(hidden, 0, branch, 0)
            return
        per_narrow = hidden.shape[1] // job_rows
        per_side = width // job_rows
        first = 0
        table = [(hidden, branch, per_narrow)]
        table.append((ffn_in, pre, per_narrow))
        table += [
            (context, attn, per_side), (normed, by_query, per_side),
            (normed, by_key, per_side), (normed, by_value, per_side),
        ]
        for index, (left_ref, right_ref, count) in enumerate(table):
            local = job - first

            def go(local=local, left_ref=left_ref, right_ref=right_ref, index=index):
                if index == 1:
                    copies(left_ref, lax.rem(local, per_side), right_ref, local // per_side)
                else:
                    copies(left_ref, local, right_ref, 0)

            pl.when(jnp.logical_and(local >= 0, local < count))(go)
            first += count

    def compute(job):
        slot = lax.rem(job, 2)
        load(job, False)
        pl.when(job + 1 < jobs)(lambda: load(job + 1, True))
        part[slot] = lax.dot_general(
            left[slot], right[slot], (((0,), (0,)), ((), ())), preferred_element_type=jnp.float32
        )

    def remote(unit, step, job):
        add, spread = plans[unit]
        turn = lax.rem(job, rings[unit][step])
        place_in = lax.rem(job, held)
        sems = dict(
            send_sem=send_sem.at[unit * steps + step, turn],
            recv_sem=recv_sem.at[unit * steps + step, turn],
            device_id_type=MESH,
        )
        base = unit * half
        if step == 0:
            src = part.at[lax.rem(job, 2), pl.ds(pl.multiple_of(unit * unit_rows + (1 - tower) * half, 8), half)]
            dst = mate_in.at[turn, pl.ds(base, half)]
            return pltpu.make_async_remote_copy(src, dst, device_id=(1 - tower, batch), **sems), None, None
        if step == steps - 1:
            src = full.at[lax.rem(job, spread_held), pl.ds(base, half)]
            first = pl.multiple_of(job * job_rows + unit * unit_rows + tower * half, 8)
            dst = out.at[pl.ds(first, half)]
            return pltpu.make_async_remote_copy(src, dst, device_id=(1 - tower, batch), **sems), None, None
        count = counts[unit]
        item = add[step - 1] if step <= count else spread[step - 1 - count]
        rows = pl.ds(pl.multiple_of(base + item["send"], 8), item["rows"])
        if step <= count:
            src, dst = acc.at[place_in, rows], inbox[unit][step - 1].at[turn]
        else:
            src = dst = full.at[lax.rem(job, spread_held), rows]
        copy = pltpu.make_async_remote_copy(src, dst, device_id=(tower, item["peer"]), **sems)
        return copy, item["sends"], item["receives"]

    def keep(unit, job):
        base = unit * half
        first = pl.multiple_of(job * job_rows + unit * unit_rows + tower * half, 8)
        return pltpu.make_async_copy(
            full.at[lax.rem(job, spread_held), pl.ds(base, half)], out.at[pl.ds(first, half)],
            keep_sem.at[unit, lax.rem(job, 2)],
        )

    def one_way(unit, step):
        return 1 <= step <= counts[unit] and single[unit][step - 1]

    def finish(unit, step, job):
        copy, sends, receives = remote(unit, step, job)
        add, _ = plans[unit]
        base = unit * half
        guarded(sends, copy.wait_send)
        turn = lax.rem(job, rings[unit][step])
        place_in = lax.rem(job, held)

        def arrived():
            copy.wait_recv()
            if step == 0:
                own = pl.ds(pl.multiple_of(unit * unit_rows + tower * half, 8), half)
                acc[place_in, pl.ds(base, half)] = part[lax.rem(job, 2), own] + mate_in[turn, pl.ds(base, half)]
            elif step <= counts[unit]:
                item = add[step - 1]
                rows = pl.ds(pl.multiple_of(base + item["keep"], 8), item["rows"])
                total = acc[place_in, rows] + inbox[unit][step - 1][turn]
                if step == counts[unit]:
                    full[lax.rem(job, spread_held), rows] = total
                else:
                    acc[place_in, rows] = total
                if one_way(unit, step):
                    pl.when(job + rings[unit][step] < jobs)(
                        lambda: pl.semaphore_signal(
                            credit.at[unit * steps + step], 1,
                            device_id=(tower, item["peer"]), device_id_type=MESH,
                        )
                    )

        guarded(receives, arrived)
        if step == steps - 1:
            keep(unit, job).wait()

    def advance(step, job):
        for unit in range(len(orders)):
            if step > 0:
                finish(unit, step - 1, job)
            if step < steps:
                copy, sends, _ = remote(unit, step, job)

                def begin(copy=copy, unit=unit):
                    if one_way(unit, step):
                        pl.when(job >= rings[unit][step])(
                            lambda: pl.semaphore_wait(credit.at[unit * steps + step], 1)
                        )
                    copy.start()

                guarded(sends, begin)
                if step == steps - 1:
                    keep(unit, job).start()

    def small_copy(turn):
        return pltpu.make_async_remote_copy(
            src_ref=small_own.at[turn],
            dst_ref=small_in.at[turn],
            send_sem=small_sem.at[0, turn],
            recv_sem=small_sem.at[1, turn],
            device_id=turns[turn],
            device_id_type=MESH,
        )

    def small_turn(turn):
        if turn > 0:
            small_copy(turn - 1).wait()
            total = small_own[turn - 1] + small_in[turn - 1]
            if turn == len(turns):
                small_out[...] = total
            else:
                small_own[turn] = total
        if turn < len(turns):
            small_copy(turn).start()

    def heads_load(task, begin):
        rows = pl.ds(pl.multiple_of(task // pairs * slot_len, slot_len), slot_len)
        columns = pl.ds(pl.multiple_of(lax.rem(task, pairs) * pair, pair), pair)
        slot = lax.rem(task, 2)
        for index, ref in enumerate((query, key, value, upstream)):
            copy = pltpu.make_async_copy(
                ref.at[rows, columns], heads_in.at[slot, index], heads_sem.at[slot, index]
            )
            copy.start() if begin else copy.wait()

    places = lax.broadcasted_iota(jnp.int32, (slot_len, 1), 0)
    lanes = lax.broadcasted_iota(jnp.int32, (1, pair), 1)

    def attend(task, carry):
        seq, index = task // pairs, lax.rem(task, pairs)
        slot = lax.rem(task, 2)
        heads_load(task, False)
        pl.when(task + 1 < tasks)(lambda: heads_load(task + 1, True))
        queries, keys, values, upper = (heads_in[slot, n] for n in range(4))
        length = lengths[seq]
        grads_out = [None] * 3
        for side in range(2):
            head = 2 * index + side
            mine = (lanes // (pair // 2) == side).astype(jnp.bfloat16)
            my_queries, my_upper = queries * mine, upper * mine
            raw = dot_across(keys, my_queries)
            soft_grad = dot_across(values, my_upper)
            line = totals[seq, pl.ds(head, 1), :]
            inner = jnp.zeros((1, slot_len), jnp.float32)
            low_rows = []
            for block in range(blocks):
                span = slice(block * tile, (block + 1) * tile)
                bias = bias_row(near_ref, head, block, blocks, far[0, head], far[1, head], True)
                scores = jnp.where(places[span] < length, raw[span] + bias, masked_score)
                soft = jnp.exp(scores - line)
                soft_ref[span] = soft
                low_rows.append(soft.astype(jnp.bfloat16))
                inner += jnp.sum(soft * soft_grad[span], axis=0, keepdims=True)
            soft_low = jnp.concatenate(low_rows, axis=0)
            grad_rows = []
            near_total = [None] * 3
            far_total = [None] * 2
            for block in range(blocks):
                span = slice(block * tile, (block + 1) * tile)
                grads = soft_ref[span] * (soft_grad[span] - inner)
                grad_rows.append(grads.astype(jnp.bfloat16))
                for other in range(blocks):
                    piece = grads[:, other * tile : (other + 1) * tile]
                    ahead = block - other
                    group, spot = (near_total, 1 - ahead) if abs(ahead) <= 1 else (far_total, int(ahead > 0))
                    group[spot] = piece if group[spot] is None else group[spot] + piece
            for spot in range(3):
                if near_total[spot] is not None:
                    near_sums[head, :, spot * tile : (spot + 1) * tile] += near_total[spot]
            for spot in range(2):
                if far_total[spot] is not None:
                    far_sums[spot, pl.ds(head, 1), :] += jnp.sum(far_total[spot], axis=0, keepdims=True)
            grads_low = jnp.concatenate(grad_rows, axis=0)
            pieces = (
                lax.dot_general(grads_low, keys * mine, (((0,), (0,)), ((), ())), preferred_element_type=jnp.float32),
                low_dot(grads_low, my_queries),
                low_dot(soft_low, my_upper),
            )
            grads_out = [new if old is None else old + new for old, new in zip(grads_out, pieces)]
        rows = pl.ds(pl.multiple_of(seq * slot_len, slot_len), slot_len)
        columns = pl.ds(pl.multiple_of(index * pair, pair), pair)
        for ref, grads in zip((by_query, by_key, by_value), grads_out):
            ref[rows, columns] = grads.astype(jnp.bfloat16)
        return carry

    def token_load(seq, begin):
        rows = pl.ds(pl.multiple_of(seq * slot_len, slot_len), slot_len)
        for index, (ref, target) in enumerate(((tokens, token_in), (mixed_grad, mixed_in))):
            copy = pltpu.make_async_copy(ref.at[rows], target, token_sem.at[index])
            copy.start() if begin else copy.wait()

    def token_store(seq):
        rows = pl.ds(pl.multiple_of(seq * slot_len, slot_len), slot_len)
        return pltpu.make_async_copy(token_buffer, token_out.at[rows], token_sem.at[2])

    def token_task(seq):
        rows = pl.ds(pl.multiple_of(seq * slot_len, slot_len), slot_len)
        token_load(seq, False)
        normed_grad = dot_across(by_query[rows, :], wq[...]) + dot_across(by_key[rows, :], wk[...])
        normed_grad += dot_across(by_value[rows, :], wv[...])
        by_tokens, token_gain = norm_back(token_in[...].astype(jnp.float32), gain[...], normed_grad)
        small_own[0, 0:1] += token_gain
        pl.when(seq > 0)(lambda: token_store(seq - 1).wait())
        token_buffer[...] = (mixed_in[...] + by_tokens).astype(jnp.bfloat16)
        token_store(seq).start()
        pl.when(seq + 1 < seqs)(lambda: token_load(seq + 1, True))

    def close():
        token_store(seqs - 1).wait()
        small_own[0, 8:24, :] = jnp.zeros((16, width), jnp.float32)
        for head in range(heads):
            turned = jnp.concatenate([near_sums[head], jnp.zeros((tile, tile), jnp.float32)], axis=1)
            count = tile // 2
            while count:
                upper = turned[count : 2 * count]
                turned = turned[:count] + pltpu.roll(upper, 4 * tile - count, 1)
                count //= 2
            small_own[0, 8 + head : 9 + head, : 4 * tile] = turned
        small_own[0, 8:24, 2 * tile : 3 * tile] += far_sums[0]
        small_own[0, 8:24, 3 * tile : 4 * tile] += far_sums[1]

    load(0, True)
    heads_load(0, True)
    token_load(0, True)
    spread_bias(lines, near_ref, heads)
    near_sums[...] = jnp.zeros_like(near_sums)
    far_sums[...] = jnp.zeros_like(far_sums)
    small_own[0, 0:8, :] = small[...]
    pl.semaphore_wait(barrier, len(mates))

    last_attend = jobs - 3 * (width // job_rows)
    first_small = slots - 1 - len(turns)
    first_token = first_small - 1 - seqs

    def slot(time, carry):
        for step in range(steps, -1, -1):
            job = time - 1 - step
            pl.when(jnp.logical_and(job >= 0, job < jobs))(functools.partial(advance, step, job))
        for turn in range(len(turns) + 1):
            pl.when(time == first_small + turn)(functools.partial(small_turn, turn))
        begin = jnp.minimum(time * tasks // last_attend, tasks)
        end = jnp.minimum((time + 1) * tasks // last_attend, tasks)
        lax.fori_loop(begin, end, attend, 0)
        pl.when(time < jobs)(functools.partial(compute, time))
        seq = time - first_token
        pl.when(jnp.logical_and(seq >= 0, seq < seqs))(functools.partial(token_task, seq))
        pl.when(time == first_small - 1)(close)
        return carry

    lax.fori_loop(0, slots, slot, 0)


def sum_weights(batch_size, collective, lengths, far, streamed, small, resident):
    hidden, normed = streamed[0], streamed[3]
    tokens, width = normed.shape
    seqs = lengths.shape[0]
    heads = far.shape[1]
    slot_len = tokens // seqs
    pair = 2 * width // heads
    total = 2 * hidden.shape[1] + 4 * width
    jobs = total // job_rows
    dims = batch_dims(batch_size)
    half = unit_rows // 2
    rings = [step_rings(order, dims) for order in orders]
    inboxes = [
        pltpu.VMEM((rings[unit][1 + index], rows, width), jnp.float32)
        for unit, order in enumerate(orders)
        for index, rows in enumerate(stage_rows(order, dims, half))
    ]
    steps = len(rings[0])
    longest = max(max(ring) for ring in rings)
    turns = 1 + sum(size // 2 for _, size in dims.values())
    lines = 24
    low, full = jnp.bfloat16, jnp.float32
    in_vmem = pl.BlockSpec(memory_space=pltpu.VMEM)
    in_smem = pl.BlockSpec(memory_space=pltpu.SMEM)
    anywhere = pl.BlockSpec(memory_space=pl.ANY)
    return pl.pallas_call(
        functools.partial(sums_kernel, dims, jobs),
        out_shape=(
            jax.ShapeDtypeStruct((total, width), full),
            jax.ShapeDtypeStruct((tokens, width), low),
            jax.ShapeDtypeStruct((lines, width), full),
        ),
        in_specs=[in_smem] * 2 + [anywhere] * len(streamed) + [in_vmem] * (1 + len(resident)),
        out_specs=(anywhere, anywhere, in_vmem),
        scratch_shapes=[
            pltpu.VMEM((2, tokens, job_rows), low),
            pltpu.VMEM((2, tokens, width), low),
            pltpu.VMEM((2, job_rows, width), full),
            pltpu.VMEM((steps // 2, 3 * half, width), full),
            pltpu.VMEM((steps, 3 * half, width), full),
            pltpu.VMEM((3, 3 * half, width), full),
            pltpu.VMEM((turns, lines, width), full),
            pltpu.VMEM((turns, lines, width), full),
            pltpu.VMEM((2, 4, slot_len, pair), low),
            pltpu.VMEM((tokens, width), low),
            pltpu.VMEM((tokens, width), low),
            pltpu.VMEM((tokens, width), low),
            pltpu.VMEM((heads, tile, near), full),
            pltpu.VMEM((heads, tile, near), full),
            pltpu.VMEM((2, 16, tile), full),
            pltpu.VMEM((slot_len, slot_len), full),
            pltpu.VMEM((slot_len, width), low),
            pltpu.VMEM((slot_len, width), full),
            pltpu.VMEM((slot_len, width), low),
            *inboxes,
            pltpu.SemaphoreType.DMA((2, 2)),
            pltpu.SemaphoreType.DMA((3 * steps, longest)),
            pltpu.SemaphoreType.DMA((3 * steps, longest)),
            pltpu.SemaphoreType.DMA((3, 2)),
            pltpu.SemaphoreType.DMA((2, turns)),
            pltpu.SemaphoreType.DMA((2, 4)),
            pltpu.SemaphoreType.DMA((3,)),
            pltpu.SemaphoreType.REGULAR((3 * steps,)),
        ],
        compiler_params=pltpu.CompilerParams(
            collective_id=collective, has_side_effects=True, vmem_limit_bytes=66500000
        ),
        name="sum_weights",
    )(lengths, far, *streamed, small, *resident)


tile = 128
near = 3 * tile


def bias_lines(bucket_bias, mirrored):
    buckets, heads = bucket_bias.shape
    spots = jnp.arange(4 * tile, dtype=jnp.int32)
    moved = jnp.where(spots >= near, spots - 4 * tile, spots)
    offset = tile - moved if mirrored else moved - tile
    onehot = offset_onehot(offset, buckets)
    lines = jnp.dot(bucket_bias.T, onehot.T, precision=highest)
    return jnp.pad(lines, ((0, 16 - heads), (0, 0)))


def offset_onehot(offset, buckets):
    spread = jnp.abs(offset)
    far_bucket = 8 + sum(((spread >= step).astype(jnp.int32) for step in far_steps))
    bucket = jnp.where(spread < 8, spread, far_bucket) + jnp.where(offset > 0, buckets // 2, 0)
    return (bucket[:, None] == jnp.arange(buckets, dtype=jnp.int32)[None, :]).astype(jnp.float32)


def spread_bias(lines_ref, near_ref, heads):
    for head in range(heads):
        line = jnp.broadcast_to(lines_ref[head : head + 1, :], (tile, 4 * tile))
        near_ref[head] = pltpu.roll(line, 0, 1, stride=1, stride_axis=0)[:, :near]


def bias_row(near_ref, head, block, blocks, low_far, high_far, mirrored):
    parts = []
    for other in range(blocks):
        ahead = block - other if mirrored else other - block
        if abs(ahead) <= 1:
            spot = 1 - ahead if mirrored else 1 + ahead
            parts.append(near_ref[head, :, spot * tile : (spot + 1) * tile])
        else:
            parts.append(jnp.full((tile, tile), high_far if ahead > 0 else low_far, jnp.float32))
    return jnp.concatenate(parts, axis=1)


def unit_scale(values):
    return lax.rsqrt(jnp.mean(values * values, axis=-1, keepdims=True) + epsilon)


def low_dot(left, right):
    return jnp.dot(left, right, preferred_element_type=jnp.float32)


def dot_across(left, right):
    return lax.dot_general(left, right, (((1,), (1,)), ((), ())), preferred_element_type=jnp.float32)


def forward_kernel(
    lengths, prefixes, far, x_ref, lines_ref, gain_a, wq, wk, wv, wo, gain_f, widen, narrow, gain_z,
    normed_ref, q_ref, k_ref, v_ref, lse_ref, context_ref, mixed_ref, ffn_ref, hidden_ref, output_ref, pooled_ref,
    near_ref, lse_cols,
):
    seq = pl.program_id(0)
    heads = far.shape[1]
    slot_len, width = x_ref.shape
    blocks = slot_len // tile
    pair = 2 * width // heads
    length = lengths[seq]
    pl.when(seq == 0)(lambda: spread_bias(lines_ref, near_ref, heads))
    tokens = x_ref[...].astype(jnp.float32)
    normed = (tokens * unit_scale(tokens) * gain_a[...]).astype(jnp.bfloat16)
    normed_ref[...] = normed
    q_ref[...] = low_dot(normed, wq[...]).astype(jnp.bfloat16)
    k_ref[...] = low_dot(normed, wk[...]).astype(jnp.bfloat16)
    v_ref[...] = low_dot(normed, wv[...]).astype(jnp.bfloat16)
    lanes = lax.broadcasted_iota(jnp.int32, (1, pair), 1)
    valid = lax.broadcasted_iota(jnp.int32, (1, slot_len), 1) < length
    columns = lax.broadcasted_iota(jnp.int32, (tile, tile), 1)

    def attend(index, carry):
        span = pl.ds(pl.multiple_of(index * pair, pair), pair)
        keys = k_ref[:, span]
        queries = q_ref[:, span]
        values = v_ref[:, span]
        total = None
        for side in range(2):
            head = 2 * index + side
            mine = (lanes // (pair // 2) == side).astype(jnp.bfloat16)
            raw = dot_across(queries * mine, keys)
            rows = []
            for block in range(blocks):
                part = slice(block * tile, (block + 1) * tile)
                bias = bias_row(near_ref, head, block, blocks, far[0, head], far[1, head], False)
                scores = jnp.where(valid, raw[part] + bias, masked_score)
                peak = jnp.max(scores, axis=-1, keepdims=True)
                raised = jnp.exp(scores - peak)
                total_raised = jnp.sum(raised, axis=-1, keepdims=True)
                rows.append((raised * (1.0 / total_raised)).astype(jnp.bfloat16))
                lse_cols[part] = jnp.where(columns == head, peak + jnp.log(total_raised), lse_cols[part])
            soft_low = jnp.concatenate(rows, axis=0)
            piece = low_dot(soft_low, values * mine)
            total = piece if total is None else total + piece
        context_ref[:, span] = total.astype(jnp.bfloat16)
        return carry

    lax.fori_loop(0, heads // 2, attend, 0)
    lse_ref[0] = lse_cols[...].T[: lse_ref.shape[1]]
    mixed = tokens + low_dot(context_ref[...], wo[...])
    mixed_ref[...] = mixed
    ffn_in = (mixed * unit_scale(mixed) * gain_f[...]).astype(jnp.bfloat16)
    ffn_ref[...] = ffn_in
    output_ref[...] = mixed

    def feed(index, carry):
        span = pl.ds(pl.multiple_of(index * width, 128), width)
        pre_act = low_dot(ffn_ref[...], widen[:, span])
        hidden = jnp.where(pre_act > 0, pre_act, 0.0).astype(jnp.bfloat16)
        hidden_ref[:, span] = hidden
        output_ref[...] += low_dot(hidden, narrow[span, :])
        return carry

    lax.fori_loop(0, widen.shape[1] // width, feed, 0)
    output = output_ref[...]
    places = lax.broadcasted_iota(jnp.int32, (slot_len, 1), 0)
    mask = jnp.logical_and(places >= prefixes[seq], places < length).astype(jnp.float32)
    count = (length - prefixes[seq]).astype(jnp.float32)
    final = output * unit_scale(output) * gain_z[...]
    pooled_ref[0] = jnp.sum(final * (mask / count), axis=0, keepdims=True)


def run_forward(tokens, lengths, prefixes, far, lines, gains, weights):
    rows, width = tokens.shape
    seqs = lengths.shape[0]
    slot_len = rows // seqs
    heads = far.shape[1]
    wq, wk, wv, wo, widen, narrow = weights
    gain_a, gain_f, gain_z = gains
    ff = widen.shape[1]

    def whole(shape):
        return pl.BlockSpec(shape, lambda n, *_: (0,) * len(shape), pipeline_mode=pl.Buffered(1))

    def block(columns):
        return pl.BlockSpec((slot_len, columns), lambda n, *_: (n, 0))

    square = whole((width, width))
    line = whole((1, width))
    low, full = jnp.bfloat16, jnp.float32

    def shape(columns, kind):
        return jax.ShapeDtypeStruct((rows, columns), kind)

    return pl.pallas_call(
        forward_kernel,
        grid_spec=pltpu.PrefetchScalarGridSpec(
            num_scalar_prefetch=3,
            grid=(seqs,),
            in_specs=[
                block(width), whole((16, 4 * tile)), line, square, square, square, square,
                line, whole((width, ff)), whole((ff, width)), line,
            ],
            out_specs=[
                block(width), block(width), block(width), block(width),
                pl.BlockSpec((1, 16, slot_len), lambda n, *_: (n, 0, 0)),
                block(width), block(width), block(width), block(ff), block(width),
                pl.BlockSpec((1, 1, width), lambda n, *_: (n, 0, 0)),
            ],
            scratch_shapes=[
                pltpu.VMEM((heads, tile, near), jnp.float32),
                pltpu.VMEM((slot_len, tile), jnp.float32),
            ],
        ),
        out_shape=(
            shape(width, low), shape(width, low), shape(width, low), shape(width, low),
            jax.ShapeDtypeStruct((seqs, 16, slot_len), full),
            shape(width, low), shape(width, full), shape(width, low), shape(ff, low), shape(width, full),
            jax.ShapeDtypeStruct((seqs, 1, width), full),
        ),
        compiler_params=pltpu.CompilerParams(vmem_limit_bytes=60000000),
        name="forward",
    )(lengths, prefixes, far, tokens, lines, gain_a[None], wq, wk, wv, wo, gain_f[None], widen, narrow, gain_z[None])


def norm_back(values, gain, upstream):
    inverse = unit_scale(values)
    scaled = upstream * gain
    inner = jnp.mean(scaled * values, axis=-1, keepdims=True)
    by_values = inverse * scaled - values * (inverse * inverse * inverse) * inner
    return by_values, jnp.sum(upstream * values * inverse, axis=0, keepdims=True)


def feed_back_kernel(
    lengths, prefixes, wo, gain_f, widen, narrow, gain_z, mixed_ref, hidden_ref, output_ref, pooled_ref,
    branch_ref, pre_ref, attn_ref, context_ref, mixed_grad, gains_ref, feed_grad,
):
    seq = pl.program_id(0)
    slot_len, width = mixed_ref.shape
    length = lengths[seq]

    def clear():
        gains_ref[...] = jnp.zeros_like(gains_ref)

    pl.when(seq == 0)(clear)
    places = lax.broadcasted_iota(jnp.int32, (slot_len, 1), 0)
    mask = jnp.logical_and(places >= prefixes[seq], places < length).astype(jnp.float32)
    count = (length - prefixes[seq]).astype(jnp.float32)
    final_grad = (mask / count) * pooled_ref[0]
    output_grad, final_gain = norm_back(output_ref[...], gain_z[...], final_grad)
    gains_ref[2:3] += final_gain
    mixed_grad[...] = output_grad
    branch_ref[...] = output_grad.astype(jnp.bfloat16)
    feed_grad[...] = jnp.zeros_like(feed_grad)

    def feed(index, carry):
        span = pl.ds(pl.multiple_of(index * width, 128), width)
        hidden_grad = dot_across(branch_ref[...], narrow[span, :])
        pre_grad = jnp.where(hidden_ref[:, span] > 0, hidden_grad, 0.0).astype(jnp.bfloat16)
        pre_ref[:, span] = pre_grad
        feed_grad[...] += dot_across(pre_grad, widen[:, span])
        return carry

    lax.fori_loop(0, widen.shape[1] // width, feed, 0)
    by_mixed, feed_gain = norm_back(mixed_ref[...], gain_f[...], feed_grad[...])
    gains_ref[1:2] += feed_gain
    total_grad = mixed_grad[...] + by_mixed
    mixed_grad[...] = total_grad
    attn_low = total_grad.astype(jnp.bfloat16)
    attn_ref[...] = attn_low
    context_ref[...] = dot_across(attn_low, wo[...]).astype(jnp.bfloat16)


def whole(shape):
    return pl.BlockSpec(shape, lambda n, *_: (0,) * len(shape), pipeline_mode=pl.Buffered(1))


def run_feed_back(lengths, prefixes, gains, weights, mixed, hidden, output, pooled_grad):
    rows, width = mixed.shape
    seqs = lengths.shape[0]
    slot_len = rows // seqs
    wo, widen, narrow = weights
    ff = widen.shape[1]

    def block(columns):
        return pl.BlockSpec((slot_len, columns), lambda n, *_: (n, 0))

    def shape(columns, kind):
        return jax.ShapeDtypeStruct((rows, columns), kind)

    low, full = jnp.bfloat16, jnp.float32
    return pl.pallas_call(
        feed_back_kernel,
        grid_spec=pltpu.PrefetchScalarGridSpec(
            num_scalar_prefetch=2,
            grid=(seqs,),
            in_specs=[
                whole((width, width)), whole((1, width)), whole((width, ff)), whole((ff, width)), whole((1, width)),
                block(width), block(ff), block(width),
                pl.BlockSpec((1, 1, width), lambda n, *_: (n, 0, 0)),
            ],
            out_specs=[
                block(width), block(ff), block(width), block(width), block(width),
                pl.BlockSpec((8, width), lambda n, *_: (0, 0)),
            ],
            scratch_shapes=[pltpu.VMEM((slot_len, width), jnp.float32)],
        ),
        out_shape=(
            shape(width, low), shape(ff, low), shape(width, low), shape(width, low), shape(width, full),
            jax.ShapeDtypeStruct((8, width), full),
        ),
        compiler_params=pltpu.CompilerParams(vmem_limit_bytes=60000000),
        name="feed_back",
    )(lengths, prefixes, wo, gains[0][None], widen, narrow, gains[1][None], mixed, hidden, output, pooled_grad)


def bucket_sums(offset_sums, shape):
    spots = jnp.arange(4 * tile, dtype=jnp.int32)
    moved = jnp.where(spots >= near, spots - 4 * tile, spots)
    onehot = offset_onehot(tile - moved, shape[0])
    return jnp.dot(onehot.T, offset_sums[: shape[1]].T, precision=highest)


def local(
    batch_size,
    tokens,
    lengths,
    prefixes,
    positives,
    gain_attention,
    query_weight,
    key_weight,
    value_weight,
    output_weight,
    bucket_bias,
    gain_feedforward,
    widen_weight,
    narrow_weight,
    gain_final,
):
    seqs = lengths.shape[1]
    width = tokens.shape[2]
    buckets = bucket_bias.shape[0]
    far = jnp.stack([bucket_bias[buckets // 2 - 1], bucket_bias[buckets - 1]])
    gains = (gain_attention, gain_feedforward, gain_final)
    weights = (query_weight, key_weight, value_weight, output_weight, widen_weight, narrow_weight)
    normed, query, key, value, totals, context, mixed, ffn_in, hidden, output, pooled = run_forward(
        tokens[0], lengths[0], prefixes[0], far, bias_lines(bucket_bias, False), gains, weights
    )
    pooled = pooled[:, 0]
    inverse_pool = lax.rsqrt(jnp.sum(pooled * pooled, axis=-1, keepdims=True) + epsilon)
    unit = pooled * inverse_pool
    gathered = gather_blocks(unit, batch_size, 0).reshape(2 * batch_size * seqs, width)
    total_seqs = gathered.shape[0] // 2
    query_units = gathered[:total_seqs]
    doc_units = gathered[total_seqs:]
    scores = score_scale * jnp.dot(query_units, doc_units.T, precision=highest)
    labels = jnp.arange(total_seqs, dtype=jnp.int32)
    target = (positives[:, None] == labels[None, :]).astype(jnp.float32)
    row_peak = jnp.max(scores, axis=1, keepdims=True)
    row_raised = jnp.exp(scores - row_peak)
    row_sum = jnp.sum(row_raised, axis=1, keepdims=True)
    col_peak = jnp.max(scores, axis=0, keepdims=True)
    col_raised = jnp.exp(scores - col_peak)
    col_sum = jnp.sum(col_raised, axis=0, keepdims=True)
    loss_value = (
        0.5 * jnp.sum(row_peak[:, 0] + jnp.log(row_sum[:, 0]))
        + 0.5 * jnp.sum(col_peak[0] + jnp.log(col_sum[0]))
        - jnp.sum(target * scores)
    )
    score_grad = 0.5 * row_raised / row_sum + 0.5 * col_raised / col_sum - target
    tower = lax.axis_index("tower")
    first_row = lax.axis_index("batch") * seqs
    my_rows = lax.dynamic_slice_in_dim(score_grad, first_row, seqs, 0)
    my_cols = lax.dynamic_slice_in_dim(score_grad, first_row, seqs, 1)
    grad_as_query = score_scale * jnp.dot(my_rows, doc_units, precision=highest)
    grad_as_doc = score_scale * jnp.dot(my_cols.T, query_units, precision=highest)
    grad_unit = jnp.where(tower == 0, grad_as_query, grad_as_doc)
    cubed = inverse_pool * inverse_pool * inverse_pool
    grad_pooled = inverse_pool * grad_unit - pooled * cubed * jnp.sum(
        grad_unit * pooled, axis=-1, keepdims=True
    )
    branch, pre, attn, context_grad, mixed_grad, feed_gains = run_feed_back(
        lengths[0], prefixes[0], gains[1:], weights[3:], mixed, hidden, output, grad_pooled[:, None]
    )
    streamed = (
        hidden, ffn_in, context, normed, branch, pre, attn, query, key, value, context_grad, tokens[0], mixed_grad
    )
    resident = (totals, bias_lines(bucket_bias, True), gain_attention[None], *weights[:3])
    summed, token_gradient, sums = sum_weights(batch_size, 1, lengths[0], far, streamed, feed_gains, resident)
    sum_bucket = bucket_sums(sums[8:, : 4 * tile], bucket_bias.shape)
    ff = hidden.shape[1]
    sum_widen = summed[ff : 2 * ff].reshape(ff // width, width, width)
    sum_widen = sum_widen.transpose(1, 0, 2).reshape(width, ff)
    sum_output, sum_query, sum_key, sum_value = (
        summed[2 * ff + n * width : 2 * ff + (n + 1) * width] for n in range(4)
    )
    return (
        loss_value,
        my_rows,
        token_gradient[None],
        sums[0],
        sum_query,
        sum_key,
        sum_value,
        sum_output,
        sum_bucket,
        sums[1],
        sum_widen,
        summed[:ff],
        sums[2],
    )


def solution(mesh):
    placed = (
        P("tower", "batch", None),
        P("tower", "batch"),
        P("tower", "batch"),
        P(),
        P(),
        P(),
        P(),
        P(),
        P(),
        P(),
        P(),
        P(),
        P(),
        P(),
    )
    return jax.shard_map(
        functools.partial(local, mesh.shape["batch"]),
        mesh=mesh,
        in_specs=placed,
        out_specs=(
            P(),
            P("batch", None),
            P("tower", "batch", None),
            P(),
            P(),
            P(),
            P(),
            P(),
            P(),
            P(),
            P(),
            P(),
            P(),
        ),
        check_vma=False,
    )
```

```python
import functools

import jax
import jax.numpy as jnp
from jax import lax
from jax.experimental import pallas as pl
from jax.experimental.pallas import tpu as pltpu
from jax.sharding import PartitionSpec as P

epsilon = 1e-06
masked_score = -1000000000.0
score_scale = 100.0
far_steps = (12, 16, 23, 32, 46, 64, 91)
highest = lax.Precision.HIGHEST


MESH = pl.DeviceIdType.MESH
job_rows = 384
unit_rows = 128


def batch_dims(size):
    sizes = {16: (2, 2, 4), 64: (4, 4, 4)}[size]
    strides = (1, sizes[0], sizes[0] * sizes[1])
    return dict(zip("xyz", zip(strides, sizes)))


def place():
    return lax.axis_index("tower"), lax.axis_index("batch")


def gather_kernel(groups, block_ref, out_ref, slots, send_sem, recv_sem, mate_sem):
    tower, batch = place()
    barrier = pltpu.get_barrier_semaphore()
    mate = (1 - tower, batch)

    def peer(step):
        return tower, lax.rem(batch + step, groups)

    def greet(step, carry):
        pl.semaphore_signal(barrier, 1, device_id=peer(step), device_id_type=MESH)
        return carry

    lax.fori_loop(1, groups, greet, 0)
    pl.semaphore_signal(barrier, 1, device_id=mate, device_id_type=MESH)
    slots[tower, batch] = block_ref[...]
    pl.semaphore_wait(barrier, groups)

    def copy(step, owner):
        return pltpu.make_async_remote_copy(
            src_ref=block_ref,
            dst_ref=slots.at[tower, owner],
            send_sem=send_sem.at[step],
            recv_sem=recv_sem.at[owner],
            device_id=peer(step),
            device_id_type=MESH,
        )

    def begin(step, carry):
        copy(step, batch).start()
        return carry

    def finish(step, carry):
        copy(step, batch).wait_send()
        copy(step, peer(step)[1]).wait_recv()
        return carry

    lax.fori_loop(1, groups, begin, 0)
    lax.fori_loop(1, groups, finish, 0)
    side = pltpu.make_async_remote_copy(
        src_ref=slots.at[tower],
        dst_ref=slots.at[tower],
        send_sem=mate_sem.at[0],
        recv_sem=mate_sem.at[1],
        device_id=mate,
        device_id_type=MESH,
    )
    side.start()
    side.wait()
    out_ref[...] = slots[...]


def gather_blocks(block, groups, collective):
    whole = (2, groups) + block.shape
    return pl.pallas_call(
        functools.partial(gather_kernel, groups),
        out_shape=jax.ShapeDtypeStruct(whole, jnp.float32),
        in_specs=[pl.BlockSpec(memory_space=pltpu.VMEM)],
        out_specs=pl.BlockSpec(memory_space=pltpu.VMEM),
        scratch_shapes=[
            pltpu.VMEM(whole, jnp.float32),
            pltpu.SemaphoreType.DMA((groups,)),
            pltpu.SemaphoreType.DMA((groups,)),
            pltpu.SemaphoreType.DMA((2,)),
        ],
        compiler_params=pltpu.CompilerParams(collective_id=collective, has_side_effects=True),
        name="gather_blocks",
    )(block)


def both(first, second):
    if first is None:
        return second
    if second is None:
        return first
    return jnp.logical_and(first, second)


def guarded(condition, action):
    if condition is None:
        action()
    else:
        pl.when(condition)(action)


def hands_back(order, dims, index):
    return index == 0 and all(dims[name][1] == 2 for name in order[1:])


def plan_unit(order, dims, coords, batch, rows):
    add, spread = [], []
    start, active, column = 0, None, None
    for index, name in enumerate(order):
        stride, size = dims[name]
        coord = coords[name]
        if size == 4:
            low_side = coord < 2
            inner = jnp.logical_or(coord == 1, coord == 2)
            outer = jnp.logical_not(inner)
            mate = batch + stride * (1 - 2 * lax.rem(coord, 2))
            share = hands_back(order, dims, index)
            sent = rows * 3 // 4 if share else rows
            first = start + jnp.where(low_side, rows // 4, 0) if share else start
            add.append(
                dict(rows=sent, send=first, keep=first, peer=mate, one_way=True,
                     sends=both(active, outer), receives=both(active, inner)))
            spread.append(
                dict(rows=sent, send=first, peer=mate,
                     sends=both(active, inner), receives=both(active, outer)))
            active_inner = both(active, inner)
            bit = coord // 2
            half = rows // 2
            kept = start + bit * half
            other = batch + stride * (3 - 2 * coord)
            add.append(
                dict(rows=half, send=start + (1 - bit) * half, keep=kept, peer=other, one_way=False,
                     sends=active_inner, receives=active_inner))
            spread.append(dict(rows=half, send=kept, peer=other, sends=active_inner, receives=active_inner))
            if share:
                quarter = rows // 4
                last = start + jnp.where(low_side, 0, 3 * quarter)
                add.append(
                    dict(rows=quarter, send=last, keep=last, peer=mate, one_way=True,
                         sends=active_inner, receives=both(active, outer)))
                spread.append(
                    dict(rows=quarter, send=last, peer=mate,
                         sends=both(active, outer), receives=active_inner))
                start, rows = start + coord * quarter, quarter
            else:
                start, rows, active = kept, half, active_inner
            continue
        mate = batch + stride * (1 - 2 * coord)
        if rows > 8:
            rows = rows // 2
            kept = start + coord * rows
            add.append(
                dict(rows=rows, send=start + (1 - coord) * rows, keep=kept, peer=mate, one_way=False,
                     sends=active, receives=active))
            spread.append(dict(rows=rows, send=kept, peer=mate, sends=active, receives=active))
            start = kept
        else:
            add.append(
                dict(rows=rows, send=start, keep=start, peer=mate, one_way=False, sends=active, receives=active,
                     send_side=1 - coord, keep_side=coord))
            spread.append(
                dict(rows=rows, send=start, peer=mate, sends=active, receives=active, send_side=coord))
    return add, spread[::-1]


def plan_shapes(order, dims, rows):
    result = []
    for index, name in enumerate(order):
        if dims[name][1] == 4:
            share = hands_back(order, dims, index)
            result.append((rows * 3 // 4 if share else rows, 1, True))
            result.append((rows // 2, 1, False))
            if share:
                result.append((rows // 4, 1, True))
            rows = rows // 4 if share else rows // 2
        elif rows > 8:
            rows //= 2
            result.append((rows, 1, False))
        else:
            result.append((rows, 2, False))
    return result


def step_rings(shapes):
    steps = 2 + 2 * len(shapes)
    rings = [4] * steps
    for index, (_, _, single) in enumerate(shapes):
        if single:
            first, last = 1 + index, steps - 2 - index
            rings[last] = last - first + 4
    return rings


orders = ("xyz", "yxz", "zxy")


def sums_kernel(dims, jobs, *refs):
    (lengths, far, hidden, ffn_in, context, normed, branch, pre, attn, query, key, value, upstream) = refs[:13]
    (tokens, mixed_grad, small, totals, lines, gain, wq, wk, wv) = refs[13:22]
    (out, token_out, small_out) = refs[22:25]
    (left, right, part, acc, full, mate_in, small_own, small_in, heads_in, by_query, by_key, by_value) = refs[25:37]
    (near_ref, near_sums, far_sums, soft_ref, token_in, mixed_in, token_buffer) = refs[37:44]
    rest = refs[44:]
    half = unit_rows // 2
    shapes = [plan_shapes(order, dims, half) for order in orders]
    counts = [len(shape) for shape in shapes]
    inbox, where = [], 0
    for count in counts:
        inbox.append(rest[where : where + count])
        where += count
    load_sem, right_sem, send_sem, recv_sem, keep_sem, small_sem, heads_sem, token_sem, credit = rest[where:]
    tower, batch = place()
    steps = [2 + 2 * count for count in counts]
    longest = max(steps)
    slots = jobs + longest + 1
    rings = [step_rings(shape) for shape in shapes]
    coords = {name: lax.rem(batch // stride, size) for name, (stride, size) in dims.items()}
    plans = [plan_unit(order, dims, coords, batch, half) for order in orders]
    turned_dims = dict(dims, x=dims["y"], y=dims["x"])
    turned_coords = dict(coords, x=coords["y"], y=coords["x"])
    turned = plan_unit(orders[-1], turned_dims, turned_coords, batch, half)

    def pick(odd, first, second):
        if isinstance(first, int) and isinstance(second, int) and first == second or first is None:
            return first
        if isinstance(first, bool):
            return first
        if getattr(first, "dtype", None) == jnp.bool_:
            return jnp.logical_or(jnp.logical_and(odd, second), jnp.logical_and(jnp.logical_not(odd), first))
        return jnp.where(odd, second, first)

    def plan(unit, job):
        if unit < len(orders) - 1:
            return plans[unit]
        odd = lax.rem(job, 2) == 1
        return tuple(
            [{key: pick(odd, one[key], two[key]) for key in one} for one, two in zip(ones, twos)]
            for ones, twos in zip(plans[unit], turned)
        )

    held, spread_held = acc.shape[0], full.shape[0]
    width = out.shape[1]
    heads = far.shape[1]
    seqs = lengths.shape[0]
    slot_len = tokens.shape[0] // seqs
    pair = 2 * width // heads
    pairs = heads // 2
    tasks = seqs * pairs
    blocks = slot_len // tile

    barrier = pltpu.get_barrier_semaphore()
    mate = (1 - tower, batch)
    mates, turns = [mate], [mate]
    for stride, size in dims.values():
        coord = lax.rem(batch // stride, size)
        near_mate = (tower, batch + stride * (1 - 2 * lax.rem(coord, 2)))
        mates.append(near_mate)
        turns.append(near_mate)
        if size == 4:
            mates.append((tower, batch + stride * (3 - 2 * coord)))
            turns.append((tower, batch + stride * (2 - 4 * (coord // 2))))
            mates.append(turns[-1])
    for other in mates:
        pl.semaphore_signal(barrier, 1, device_id=other, device_id_type=MESH)

    per_narrow = hidden.shape[1] // job_rows
    per_side = width // job_rows
    sources = [(hidden, branch, per_narrow), (ffn_in, pre, per_narrow), (context, attn, per_side)]
    sources += [(normed, grads, per_side) for grads in (by_query, by_key, by_value)]

    def right_place(job):
        past = job - per_narrow
        group = jnp.where(past < 0, 0, 1 + past // per_side)
        fresh = jnp.where(past < 0, job == 0, lax.rem(past, per_side) == 0)
        return lax.rem(group, 2), fresh

    def left_copies(target, job, columns):
        quarter = target.shape[1] // 4
        return [
            pltpu.make_async_copy(
                columns(pl.ds(n * quarter, quarter)), target.at[lax.rem(job, 2), pl.ds(n * quarter, quarter)],
                load_sem.at[lax.rem(job, 2), n],
            )
            for n in range(4)
        ]

    def load(job):
        place_right, fresh = right_place(job)
        first = 0
        for index, (left_ref, right_ref, count) in enumerate(sources):
            local = job - first

            def go(local=local, left_ref=left_ref, right_ref=right_ref, index=index):
                block = lax.rem(local, per_side) if index == 1 else local
                span = pl.ds(pl.multiple_of(block * job_rows, 128), job_rows)
                for copy in left_copies(left, job, lambda rows: left_ref.at[rows, span]):
                    copy.start()

                def go_right():
                    block = local // per_side if index == 1 else 0
                    span = pl.ds(pl.multiple_of(block * width, 128), width)
                    pltpu.make_async_copy(
                        right_ref.at[:, span], right.at[place_right], right_sem.at[place_right]
                    ).start()

                pl.when(fresh)(go_right)

            pl.when(jnp.logical_and(local >= 0, local < count))(go)
            first += count

    def compute(job):
        slot = lax.rem(job, 2)
        place_right, fresh = right_place(job)
        for copy in left_copies(left, job, lambda rows: normed.at[rows, pl.ds(0, job_rows)]):
            copy.wait()
        pl.when(fresh)(
            lambda: pltpu.make_async_copy(attn, right.at[place_right], right_sem.at[place_right]).wait()
        )
        pl.when(job + 1 < jobs)(lambda: load(job + 1))
        part[slot] = lax.dot_general(
            left[slot], right[place_right], (((0,), (0,)), ((), ())), preferred_element_type=jnp.float32
        )

    def side_columns(item, key):
        if key not in item:
            return slice(None)
        return pl.ds(pl.multiple_of(item[key] * (width // 2), 128), width // 2)

    def remote(unit, step, job):
        add, spread = plan(unit, job)
        turn = lax.rem(job, rings[unit][step])
        place_in = lax.rem(job, held)
        sems = dict(
            send_sem=send_sem.at[unit * longest + step, turn],
            recv_sem=recv_sem.at[unit * longest + step, turn],
            device_id_type=MESH,
        )
        base = unit * half
        if step == 0:
            src = part.at[lax.rem(job, 2), pl.ds(pl.multiple_of(unit * unit_rows + (1 - tower) * half, 8), half)]
            dst = mate_in.at[turn, pl.ds(base, half)]
            return pltpu.make_async_remote_copy(src, dst, device_id=(1 - tower, batch), **sems), None, None
        if step == steps[unit] - 1:
            src = full.at[lax.rem(job, spread_held), pl.ds(base, half)]
            first = pl.multiple_of(job * job_rows + unit * unit_rows + tower * half, 8)
            dst = out.at[pl.ds(first, half)]
            return pltpu.make_async_remote_copy(src, dst, device_id=(1 - tower, batch), **sems), None, None
        count = counts[unit]
        item = add[step - 1] if step <= count else spread[step - 1 - count]
        rows = pl.ds(pl.multiple_of(base + item["send"], 8), item["rows"])
        columns = side_columns(item, "send_side")
        if step <= count:
            src, dst = acc.at[place_in, rows, columns], inbox[unit][step - 1].at[turn]
        else:
            src = dst = full.at[lax.rem(job, spread_held), rows, columns]
        copy = pltpu.make_async_remote_copy(src, dst, device_id=(tower, item["peer"]), **sems)
        return copy, item["sends"], item["receives"]

    def keep(unit, job):
        base = unit * half
        first = pl.multiple_of(job * job_rows + unit * unit_rows + tower * half, 8)
        return pltpu.make_async_copy(
            full.at[lax.rem(job, spread_held), pl.ds(base, half)], out.at[pl.ds(first, half)],
            keep_sem.at[unit, lax.rem(job, 2)],
        )

    def one_way(unit, step):
        return 1 <= step <= counts[unit] and shapes[unit][step - 1][2]

    def finish(unit, step, job):
        copy, sends, receives = remote(unit, step, job)
        add, _ = plan(unit, job)
        base = unit * half
        guarded(sends, copy.wait_send)
        turn = lax.rem(job, rings[unit][step])
        place_in = lax.rem(job, held)

        def arrived():
            copy.wait_recv()
            if step == 0:
                own = pl.ds(pl.multiple_of(unit * unit_rows + tower * half, 8), half)
                acc[place_in, pl.ds(base, half)] = part[lax.rem(job, 2), own] + mate_in[turn, pl.ds(base, half)]
            elif step <= counts[unit]:
                item = add[step - 1]
                rows = pl.ds(pl.multiple_of(base + item["keep"], 8), item["rows"])
                columns = side_columns(item, "keep_side")
                total = acc[place_in, rows, columns] + inbox[unit][step - 1][turn]
                if step == counts[unit]:
                    full[lax.rem(job, spread_held), rows, columns] = total
                else:
                    acc[place_in, rows, columns] = total
                if one_way(unit, step):
                    pl.when(job + rings[unit][step] < jobs)(
                        lambda: pl.semaphore_signal(
                            credit.at[unit * longest + step], 1,
                            device_id=(tower, item["peer"]), device_id_type=MESH,
                        )
                    )

        guarded(receives, arrived)
        if step == steps[unit] - 1:
            keep(unit, job).wait()

    def advance(unit, step, job):
        if step > 0:
            finish(unit, step - 1, job)
        if step < steps[unit]:
            copy, sends, _ = remote(unit, step, job)

            def begin():
                if one_way(unit, step):
                    pl.when(job >= rings[unit][step])(
                        lambda: pl.semaphore_wait(credit.at[unit * longest + step], 1)
                    )
                copy.start()

            guarded(sends, begin)
            if step == steps[unit] - 1:
                keep(unit, job).start()

    def small_copy(turn):
        return pltpu.make_async_remote_copy(
            src_ref=small_own.at[turn],
            dst_ref=small_in.at[turn],
            send_sem=small_sem.at[0, turn],
            recv_sem=small_sem.at[1, turn],
            device_id=turns[turn],
            device_id_type=MESH,
        )

    def small_turn(turn):
        if turn > 0:
            small_copy(turn - 1).wait()
            total = small_own[turn - 1] + small_in[turn - 1]
            if turn == len(turns):
                small_out[...] = total
            else:
                small_own[turn] = total
        if turn < len(turns):
            small_copy(turn).start()

    def heads_load(task, begin):
        rows = pl.ds(pl.multiple_of(task // pairs * slot_len, slot_len), slot_len)
        columns = pl.ds(pl.multiple_of(lax.rem(task, pairs) * pair, pair), pair)
        slot = lax.rem(task, 2)
        for index, ref in enumerate((query, key, value, upstream)):
            copy = pltpu.make_async_copy(
                ref.at[rows, columns], heads_in.at[slot, index], heads_sem.at[slot, index]
            )
            copy.start() if begin else copy.wait()

    places = lax.broadcasted_iota(jnp.int32, (slot_len, 1), 0)
    lanes = lax.broadcasted_iota(jnp.int32, (1, pair), 1)

    def attend(task, carry):
        seq, index = task // pairs, lax.rem(task, pairs)
        slot = lax.rem(task, 2)
        heads_load(task, False)
        pl.when(task + 1 < tasks)(lambda: heads_load(task + 1, True))
        queries, keys, values, upper = (heads_in[slot, n] for n in range(4))
        length = lengths[seq]
        grads_out = [None] * 3
        for side in range(2):
            head = 2 * index + side
            mine = (lanes // (pair // 2) == side).astype(jnp.bfloat16)
            my_queries, my_upper = queries * mine, upper * mine
            raw = dot_across(keys, my_queries)
            soft_grad = dot_across(values, my_upper)
            line = totals[seq, pl.ds(head, 1), :]
            inner = jnp.zeros((1, slot_len), jnp.float32)
            low_rows = []
            for block in range(blocks):
                span = slice(block * tile, (block + 1) * tile)
                bias = bias_row(near_ref, head, block, blocks, far[0, head], far[1, head], True)
                scores = jnp.where(places[span] < length, raw[span] + bias, masked_score)
                soft = jnp.exp(scores - line)
                soft_ref[span] = soft
                low_rows.append(soft.astype(jnp.bfloat16))
                inner += jnp.sum(soft * soft_grad[span], axis=0, keepdims=True)
            soft_low = jnp.concatenate(low_rows, axis=0)
            grad_rows = []
            near_total = [None] * 3
            far_total = [None] * 2
            for block in range(blocks):
                span = slice(block * tile, (block + 1) * tile)
                grads = soft_ref[span] * (soft_grad[span] - inner)
                grad_rows.append(grads.astype(jnp.bfloat16))
                for other in range(blocks):
                    piece = grads[:, other * tile : (other + 1) * tile]
                    ahead = block - other
                    group, spot = (near_total, 1 - ahead) if abs(ahead) <= 1 else (far_total, int(ahead > 0))
                    group[spot] = piece if group[spot] is None else group[spot] + piece
            for spot in range(3):
                if near_total[spot] is not None:
                    near_sums[head, :, spot * tile : (spot + 1) * tile] += near_total[spot]
            for spot in range(2):
                if far_total[spot] is not None:
                    far_sums[spot, pl.ds(head, 1), :] += jnp.sum(far_total[spot], axis=0, keepdims=True)
            grads_low = jnp.concatenate(grad_rows, axis=0)
            pieces = (
                lax.dot_general(grads_low, keys * mine, (((0,), (0,)), ((), ())), preferred_element_type=jnp.float32),
                low_dot(grads_low, my_queries),
                low_dot(soft_low, my_upper),
            )
            grads_out = [new if old is None else old + new for old, new in zip(grads_out, pieces)]
        rows = pl.ds(pl.multiple_of(seq * slot_len, slot_len), slot_len)
        columns = pl.ds(pl.multiple_of(index * pair, pair), pair)
        for ref, grads in zip((by_query, by_key, by_value), grads_out):
            ref[rows, columns] = grads.astype(jnp.bfloat16)
        return carry

    def token_load(seq, begin):
        rows = pl.ds(pl.multiple_of(seq * slot_len, slot_len), slot_len)
        for index, (ref, target) in enumerate(((tokens, token_in), (mixed_grad, mixed_in))):
            copy = pltpu.make_async_copy(ref.at[rows], target, token_sem.at[index])
            copy.start() if begin else copy.wait()

    def token_store(seq):
        rows = pl.ds(pl.multiple_of(seq * slot_len, slot_len), slot_len)
        return pltpu.make_async_copy(token_buffer, token_out.at[rows], token_sem.at[2])

    def token_task(seq):
        rows = pl.ds(pl.multiple_of(seq * slot_len, slot_len), slot_len)
        token_load(seq, False)
        normed_grad = dot_across(by_query[rows, :], wq[...]) + dot_across(by_key[rows, :], wk[...])
        normed_grad += dot_across(by_value[rows, :], wv[...])
        by_tokens, token_gain = norm_back(token_in[...].astype(jnp.float32), gain[...], normed_grad)
        small_own[0, 0:1] += token_gain
        pl.when(seq > 0)(lambda: token_store(seq - 1).wait())
        token_buffer[...] = (mixed_in[...] + by_tokens).astype(jnp.bfloat16)
        token_store(seq).start()
        pl.when(seq + 1 < seqs)(lambda: token_load(seq + 1, True))

    def close():
        token_store(seqs - 1).wait()
        small_own[0, 8:24, :] = jnp.zeros((16, width), jnp.float32)
        for head in range(heads):
            turned = jnp.concatenate([near_sums[head], jnp.zeros((tile, tile), jnp.float32)], axis=1)
            count = tile // 2
            while count:
                upper = turned[count : 2 * count]
                turned = turned[:count] + pltpu.roll(upper, 4 * tile - count, 1)
                count //= 2
            small_own[0, 8 + head : 9 + head, : 4 * tile] = turned
        small_own[0, 8:24, 2 * tile : 3 * tile] += far_sums[0]
        small_own[0, 8:24, 3 * tile : 4 * tile] += far_sums[1]

    load(0)
    heads_load(0, True)
    token_load(0, True)
    spread_bias(lines, near_ref, heads)
    near_sums[...] = jnp.zeros_like(near_sums)
    far_sums[...] = jnp.zeros_like(far_sums)
    small_own[0, 0:8, :] = small[...]
    pl.semaphore_wait(barrier, len(mates))

    last_attend = jobs - 3 * (width // job_rows)
    first_small = slots - 1 - len(turns)
    first_token = first_small - 1 - seqs

    def slot(time, carry):
        for unit in range(len(orders)):
            for step in range(steps[unit] + 1):
                job = time - 1 - step
                pl.when(jnp.logical_and(job >= 0, job < jobs))(functools.partial(advance, unit, step, job))
        for turn in range(len(turns) + 1):
            pl.when(time == first_small + turn)(functools.partial(small_turn, turn))
        begin = jnp.minimum(time * tasks // last_attend, tasks)
        end = jnp.minimum((time + 1) * tasks // last_attend, tasks)
        lax.fori_loop(begin, end, attend, 0)
        pl.when(time < jobs)(functools.partial(compute, time))
        seq = time - first_token
        pl.when(jnp.logical_and(seq >= 0, seq < seqs))(functools.partial(token_task, seq))
        pl.when(time == first_small - 1)(close)
        return carry

    lax.fori_loop(0, slots, slot, 0)


def sum_weights(batch_size, collective, lengths, far, streamed, small, resident):
    hidden, normed = streamed[0], streamed[3]
    tokens, width = normed.shape
    seqs = lengths.shape[0]
    heads = far.shape[1]
    slot_len = tokens // seqs
    pair = 2 * width // heads
    total = 2 * hidden.shape[1] + 4 * width
    jobs = total // job_rows
    dims = batch_dims(batch_size)
    half = unit_rows // 2
    shapes = [plan_shapes(order, dims, half) for order in orders]
    rings = [step_rings(shape) for shape in shapes]
    inboxes = [
        pltpu.VMEM((rings[unit][1 + index], rows, width // parts), jnp.float32)
        for unit, shape in enumerate(shapes)
        for index, (rows, parts, _) in enumerate(shape)
    ]
    steps = max(len(ring) for ring in rings)
    longest = max(max(ring) for ring in rings)
    turns = 1 + sum(size // 2 for _, size in dims.values())
    lines = 24
    low, full = jnp.bfloat16, jnp.float32
    in_vmem = pl.BlockSpec(memory_space=pltpu.VMEM)
    in_smem = pl.BlockSpec(memory_space=pltpu.SMEM)
    anywhere = pl.BlockSpec(memory_space=pl.ANY)
    return pl.pallas_call(
        functools.partial(sums_kernel, dims, jobs),
        out_shape=(
            jax.ShapeDtypeStruct((total, width), full),
            jax.ShapeDtypeStruct((tokens, width), low),
            jax.ShapeDtypeStruct((lines, width), full),
        ),
        in_specs=[in_smem] * 2 + [anywhere] * len(streamed) + [in_vmem] * (1 + len(resident)),
        out_specs=(anywhere, anywhere, in_vmem),
        scratch_shapes=[
            pltpu.VMEM((2, tokens, job_rows), low),
            pltpu.VMEM((2, tokens, width), low),
            pltpu.VMEM((2, job_rows, width), full),
            pltpu.VMEM((steps // 2, 3 * half, width), full),
            pltpu.VMEM((steps, 3 * half, width), full),
            pltpu.VMEM((4, 3 * half, width), full),
            pltpu.VMEM((turns, lines, width), full),
            pltpu.VMEM((turns, lines, width), full),
            pltpu.VMEM((2, 4, slot_len, pair), low),
            pltpu.VMEM((tokens, width), low),
            pltpu.VMEM((tokens, width), low),
            pltpu.VMEM((tokens, width), low),
            pltpu.VMEM((heads, tile, near), full),
            pltpu.VMEM((heads, tile, near), full),
            pltpu.VMEM((2, 16, tile), full),
            pltpu.VMEM((slot_len, slot_len), full),
            pltpu.VMEM((slot_len, width), low),
            pltpu.VMEM((slot_len, width), full),
            pltpu.VMEM((slot_len, width), low),
            *inboxes,
            pltpu.SemaphoreType.DMA((2, 4)),
            pltpu.SemaphoreType.DMA((2,)),
            pltpu.SemaphoreType.DMA((3 * steps, longest)),
            pltpu.SemaphoreType.DMA((3 * steps, longest)),
            pltpu.SemaphoreType.DMA((3, 2)),
            pltpu.SemaphoreType.DMA((2, turns)),
            pltpu.SemaphoreType.DMA((2, 4)),
            pltpu.SemaphoreType.DMA((3,)),
            pltpu.SemaphoreType.REGULAR((3 * steps,)),
        ],
        compiler_params=pltpu.CompilerParams(
            collective_id=collective, has_side_effects=True, vmem_limit_bytes=66500000
        ),
        name="sum_weights",
    )(lengths, far, *streamed, small, *resident)


tile = 128
near = 3 * tile


def bias_lines(bucket_bias, mirrored):
    buckets, heads = bucket_bias.shape
    spots = jnp.arange(4 * tile, dtype=jnp.int32)
    moved = jnp.where(spots >= near, spots - 4 * tile, spots)
    offset = tile - moved if mirrored else moved - tile
    onehot = offset_onehot(offset, buckets)
    lines = jnp.dot(bucket_bias.T, onehot.T, precision=highest)
    return jnp.pad(lines, ((0, 16 - heads), (0, 0)))


def offset_onehot(offset, buckets):
    spread = jnp.abs(offset)
    far_bucket = 8 + sum(((spread >= step).astype(jnp.int32) for step in far_steps))
    bucket = jnp.where(spread < 8, spread, far_bucket) + jnp.where(offset > 0, buckets // 2, 0)
    return (bucket[:, None] == jnp.arange(buckets, dtype=jnp.int32)[None, :]).astype(jnp.float32)


def spread_bias(lines_ref, near_ref, heads):
    for head in range(heads):
        line = jnp.broadcast_to(lines_ref[head : head + 1, :], (tile, 4 * tile))
        near_ref[head] = pltpu.roll(line, 0, 1, stride=1, stride_axis=0)[:, :near]


def bias_row(near_ref, head, block, blocks, low_far, high_far, mirrored):
    parts = []
    for other in range(blocks):
        ahead = block - other if mirrored else other - block
        if abs(ahead) <= 1:
            spot = 1 - ahead if mirrored else 1 + ahead
            parts.append(near_ref[head, :, spot * tile : (spot + 1) * tile])
        else:
            parts.append(jnp.full((tile, tile), high_far if ahead > 0 else low_far, jnp.float32))
    return jnp.concatenate(parts, axis=1)


def unit_scale(values):
    return lax.rsqrt(jnp.mean(values * values, axis=-1, keepdims=True) + epsilon)


def low_dot(left, right):
    return jnp.dot(left, right, preferred_element_type=jnp.float32)


def dot_across(left, right):
    return lax.dot_general(left, right, (((1,), (1,)), ((), ())), preferred_element_type=jnp.float32)


def forward_kernel(
    lengths, prefixes, far, x_ref, lines_ref, gain_a, wq, wk, wv, wo, gain_f, widen, narrow, gain_z,
    normed_ref, q_ref, k_ref, v_ref, lse_ref, context_ref, mixed_ref, ffn_ref, hidden_ref, output_ref, pooled_ref,
    near_ref, lse_cols,
):
    seq = pl.program_id(0)
    heads = far.shape[1]
    slot_len, width = x_ref.shape
    blocks = slot_len // tile
    pair = 2 * width // heads
    length = lengths[seq]
    pl.when(seq == 0)(lambda: spread_bias(lines_ref, near_ref, heads))
    tokens = x_ref[...].astype(jnp.float32)
    normed = (tokens * unit_scale(tokens) * gain_a[...]).astype(jnp.bfloat16)
    normed_ref[...] = normed
    q_ref[...] = low_dot(normed, wq[...]).astype(jnp.bfloat16)
    k_ref[...] = low_dot(normed, wk[...]).astype(jnp.bfloat16)
    v_ref[...] = low_dot(normed, wv[...]).astype(jnp.bfloat16)
    lanes = lax.broadcasted_iota(jnp.int32, (1, pair), 1)
    valid = lax.broadcasted_iota(jnp.int32, (1, slot_len), 1) < length
    columns = lax.broadcasted_iota(jnp.int32, (tile, tile), 1)

    def attend(index, carry):
        span = pl.ds(pl.multiple_of(index * pair, pair), pair)
        keys = k_ref[:, span]
        queries = q_ref[:, span]
        values = v_ref[:, span]
        total = None
        for side in range(2):
            head = 2 * index + side
            mine = (lanes // (pair // 2) == side).astype(jnp.bfloat16)
            raw = dot_across(queries * mine, keys)
            rows = []
            for block in range(blocks):
                part = slice(block * tile, (block + 1) * tile)
                bias = bias_row(near_ref, head, block, blocks, far[0, head], far[1, head], False)
                scores = jnp.where(valid, raw[part] + bias, masked_score)
                peak = jnp.max(scores, axis=-1, keepdims=True)
                raised = jnp.exp(scores - peak)
                total_raised = jnp.sum(raised, axis=-1, keepdims=True)
                rows.append((raised * (1.0 / total_raised)).astype(jnp.bfloat16))
                lse_cols[part] = jnp.where(columns == head, peak + jnp.log(total_raised), lse_cols[part])
            soft_low = jnp.concatenate(rows, axis=0)
            piece = low_dot(soft_low, values * mine)
            total = piece if total is None else total + piece
        context_ref[:, span] = total.astype(jnp.bfloat16)
        return carry

    lax.fori_loop(0, heads // 2, attend, 0)
    lse_ref[0] = lse_cols[...].T[: lse_ref.shape[1]]
    mixed = tokens + low_dot(context_ref[...], wo[...])
    mixed_ref[...] = mixed
    ffn_in = (mixed * unit_scale(mixed) * gain_f[...]).astype(jnp.bfloat16)
    ffn_ref[...] = ffn_in
    output_ref[...] = mixed

    def feed(index, carry):
        span = pl.ds(pl.multiple_of(index * width, 128), width)
        pre_act = low_dot(ffn_ref[...], widen[:, span])
        hidden = jnp.where(pre_act > 0, pre_act, 0.0).astype(jnp.bfloat16)
        hidden_ref[:, span] = hidden
        output_ref[...] += low_dot(hidden, narrow[span, :])
        return carry

    lax.fori_loop(0, widen.shape[1] // width, feed, 0)
    output = output_ref[...]
    places = lax.broadcasted_iota(jnp.int32, (slot_len, 1), 0)
    mask = jnp.logical_and(places >= prefixes[seq], places < length).astype(jnp.float32)
    count = (length - prefixes[seq]).astype(jnp.float32)
    final = output * unit_scale(output) * gain_z[...]
    pooled_ref[0] = jnp.sum(final * (mask / count), axis=0, keepdims=True)


def run_forward(tokens, lengths, prefixes, far, lines, gains, weights):
    rows, width = tokens.shape
    seqs = lengths.shape[0]
    slot_len = rows // seqs
    heads = far.shape[1]
    wq, wk, wv, wo, widen, narrow = weights
    gain_a, gain_f, gain_z = gains
    ff = widen.shape[1]

    def whole(shape):
        return pl.BlockSpec(shape, lambda n, *_: (0,) * len(shape), pipeline_mode=pl.Buffered(1))

    def block(columns):
        return pl.BlockSpec((slot_len, columns), lambda n, *_: (n, 0))

    square = whole((width, width))
    line = whole((1, width))
    low, full = jnp.bfloat16, jnp.float32

    def shape(columns, kind):
        return jax.ShapeDtypeStruct((rows, columns), kind)

    return pl.pallas_call(
        forward_kernel,
        grid_spec=pltpu.PrefetchScalarGridSpec(
            num_scalar_prefetch=3,
            grid=(seqs,),
            in_specs=[
                block(width), whole((16, 4 * tile)), line, square, square, square, square,
                line, whole((width, ff)), whole((ff, width)), line,
            ],
            out_specs=[
                block(width), block(width), block(width), block(width),
                pl.BlockSpec((1, 16, slot_len), lambda n, *_: (n, 0, 0)),
                block(width), block(width), block(width), block(ff), block(width),
                pl.BlockSpec((1, 1, width), lambda n, *_: (n, 0, 0)),
            ],
            scratch_shapes=[
                pltpu.VMEM((heads, tile, near), jnp.float32),
                pltpu.VMEM((slot_len, tile), jnp.float32),
            ],
        ),
        out_shape=(
            shape(width, low), shape(width, low), shape(width, low), shape(width, low),
            jax.ShapeDtypeStruct((seqs, 16, slot_len), full),
            shape(width, low), shape(width, full), shape(width, low), shape(ff, low), shape(width, full),
            jax.ShapeDtypeStruct((seqs, 1, width), full),
        ),
        compiler_params=pltpu.CompilerParams(vmem_limit_bytes=60000000),
        name="forward",
    )(lengths, prefixes, far, tokens, lines, gain_a[None], wq, wk, wv, wo, gain_f[None], widen, narrow, gain_z[None])


def norm_back(values, gain, upstream):
    inverse = unit_scale(values)
    scaled = upstream * gain
    inner = jnp.mean(scaled * values, axis=-1, keepdims=True)
    by_values = inverse * scaled - values * (inverse * inverse * inverse) * inner
    return by_values, jnp.sum(upstream * values * inverse, axis=0, keepdims=True)


def feed_back_kernel(
    lengths, prefixes, wo, gain_f, widen, narrow, gain_z, mixed_ref, hidden_ref, output_ref, pooled_ref,
    branch_ref, pre_ref, attn_ref, context_ref, mixed_grad, gains_ref, feed_grad,
):
    seq = pl.program_id(0)
    slot_len, width = mixed_ref.shape
    length = lengths[seq]

    def clear():
        gains_ref[...] = jnp.zeros_like(gains_ref)

    pl.when(seq == 0)(clear)
    places = lax.broadcasted_iota(jnp.int32, (slot_len, 1), 0)
    mask = jnp.logical_and(places >= prefixes[seq], places < length).astype(jnp.float32)
    count = (length - prefixes[seq]).astype(jnp.float32)
    final_grad = (mask / count) * pooled_ref[0]
    output_grad, final_gain = norm_back(output_ref[...], gain_z[...], final_grad)
    gains_ref[2:3] += final_gain
    mixed_grad[...] = output_grad
    branch_ref[...] = output_grad.astype(jnp.bfloat16)
    feed_grad[...] = jnp.zeros_like(feed_grad)

    def feed(index, carry):
        span = pl.ds(pl.multiple_of(index * width, 128), width)
        hidden_grad = dot_across(branch_ref[...], narrow[span, :])
        pre_grad = jnp.where(hidden_ref[:, span] > 0, hidden_grad, 0.0).astype(jnp.bfloat16)
        pre_ref[:, span] = pre_grad
        feed_grad[...] += dot_across(pre_grad, widen[:, span])
        return carry

    lax.fori_loop(0, widen.shape[1] // width, feed, 0)
    by_mixed, feed_gain = norm_back(mixed_ref[...], gain_f[...], feed_grad[...])
    gains_ref[1:2] += feed_gain
    total_grad = mixed_grad[...] + by_mixed
    mixed_grad[...] = total_grad
    attn_low = total_grad.astype(jnp.bfloat16)
    attn_ref[...] = attn_low
    context_ref[...] = dot_across(attn_low, wo[...]).astype(jnp.bfloat16)


def whole(shape):
    return pl.BlockSpec(shape, lambda n, *_: (0,) * len(shape), pipeline_mode=pl.Buffered(1))


def run_feed_back(lengths, prefixes, gains, weights, mixed, hidden, output, pooled_grad):
    rows, width = mixed.shape
    seqs = lengths.shape[0]
    slot_len = rows // seqs
    wo, widen, narrow = weights
    ff = widen.shape[1]

    def block(columns):
        return pl.BlockSpec((slot_len, columns), lambda n, *_: (n, 0))

    def shape(columns, kind):
        return jax.ShapeDtypeStruct((rows, columns), kind)

    low, full = jnp.bfloat16, jnp.float32
    return pl.pallas_call(
        feed_back_kernel,
        grid_spec=pltpu.PrefetchScalarGridSpec(
            num_scalar_prefetch=2,
            grid=(seqs,),
            in_specs=[
                whole((width, width)), whole((1, width)), whole((width, ff)), whole((ff, width)), whole((1, width)),
                block(width), block(ff), block(width),
                pl.BlockSpec((1, 1, width), lambda n, *_: (n, 0, 0)),
            ],
            out_specs=[
                block(width), block(ff), block(width), block(width), block(width),
                pl.BlockSpec((8, width), lambda n, *_: (0, 0)),
            ],
            scratch_shapes=[pltpu.VMEM((slot_len, width), jnp.float32)],
        ),
        out_shape=(
            shape(width, low), shape(ff, low), shape(width, low), shape(width, low), shape(width, full),
            jax.ShapeDtypeStruct((8, width), full),
        ),
        compiler_params=pltpu.CompilerParams(vmem_limit_bytes=60000000),
        name="feed_back",
    )(lengths, prefixes, wo, gains[0][None], widen, narrow, gains[1][None], mixed, hidden, output, pooled_grad)


def bucket_sums(offset_sums, shape):
    spots = jnp.arange(4 * tile, dtype=jnp.int32)
    moved = jnp.where(spots >= near, spots - 4 * tile, spots)
    onehot = offset_onehot(tile - moved, shape[0])
    return jnp.dot(onehot.T, offset_sums[: shape[1]].T, precision=highest)


def local(
    batch_size,
    tokens,
    lengths,
    prefixes,
    positives,
    gain_attention,
    query_weight,
    key_weight,
    value_weight,
    output_weight,
    bucket_bias,
    gain_feedforward,
    widen_weight,
    narrow_weight,
    gain_final,
):
    seqs = lengths.shape[1]
    width = tokens.shape[2]
    buckets = bucket_bias.shape[0]
    far = jnp.stack([bucket_bias[buckets // 2 - 1], bucket_bias[buckets - 1]])
    gains = (gain_attention, gain_feedforward, gain_final)
    weights = (query_weight, key_weight, value_weight, output_weight, widen_weight, narrow_weight)
    normed, query, key, value, totals, context, mixed, ffn_in, hidden, output, pooled = run_forward(
        tokens[0], lengths[0], prefixes[0], far, bias_lines(bucket_bias, False), gains, weights
    )
    pooled = pooled[:, 0]
    inverse_pool = lax.rsqrt(jnp.sum(pooled * pooled, axis=-1, keepdims=True) + epsilon)
    unit = pooled * inverse_pool
    gathered = gather_blocks(unit, batch_size, 0).reshape(2 * batch_size * seqs, width)
    total_seqs = gathered.shape[0] // 2
    query_units = gathered[:total_seqs]
    doc_units = gathered[total_seqs:]
    scores = score_scale * jnp.dot(query_units, doc_units.T, precision=highest)
    labels = jnp.arange(total_seqs, dtype=jnp.int32)
    target = (positives[:, None] == labels[None, :]).astype(jnp.float32)
    row_peak = jnp.max(scores, axis=1, keepdims=True)
    row_raised = jnp.exp(scores - row_peak)
    row_sum = jnp.sum(row_raised, axis=1, keepdims=True)
    col_peak = jnp.max(scores, axis=0, keepdims=True)
    col_raised = jnp.exp(scores - col_peak)
    col_sum = jnp.sum(col_raised, axis=0, keepdims=True)
    loss_value = (
        0.5 * jnp.sum(row_peak[:, 0] + jnp.log(row_sum[:, 0]))
        + 0.5 * jnp.sum(col_peak[0] + jnp.log(col_sum[0]))
        - jnp.sum(target * scores)
    )
    score_grad = 0.5 * row_raised / row_sum + 0.5 * col_raised / col_sum - target
    tower = lax.axis_index("tower")
    first_row = lax.axis_index("batch") * seqs
    my_rows = lax.dynamic_slice_in_dim(score_grad, first_row, seqs, 0)
    my_cols = lax.dynamic_slice_in_dim(score_grad, first_row, seqs, 1)
    grad_as_query = score_scale * jnp.dot(my_rows, doc_units, precision=highest)
    grad_as_doc = score_scale * jnp.dot(my_cols.T, query_units, precision=highest)
    grad_unit = jnp.where(tower == 0, grad_as_query, grad_as_doc)
    cubed = inverse_pool * inverse_pool * inverse_pool
    grad_pooled = inverse_pool * grad_unit - pooled * cubed * jnp.sum(
        grad_unit * pooled, axis=-1, keepdims=True
    )
    branch, pre, attn, context_grad, mixed_grad, feed_gains = run_feed_back(
        lengths[0], prefixes[0], gains[1:], weights[3:], mixed, hidden, output, grad_pooled[:, None]
    )
    streamed = (
        hidden, ffn_in, context, normed, branch, pre, attn, query, key, value, context_grad, tokens[0], mixed_grad
    )
    resident = (totals, bias_lines(bucket_bias, True), gain_attention[None], *weights[:3])
    summed, token_gradient, sums = sum_weights(batch_size, 1, lengths[0], far, streamed, feed_gains, resident)
    sum_bucket = bucket_sums(sums[8:, : 4 * tile], bucket_bias.shape)
    ff = hidden.shape[1]
    sum_widen = summed[ff : 2 * ff].reshape(ff // width, width, width)
    sum_widen = sum_widen.transpose(1, 0, 2).reshape(width, ff)
    sum_output, sum_query, sum_key, sum_value = (
        summed[2 * ff + n * width : 2 * ff + (n + 1) * width] for n in range(4)
    )
    return (
        loss_value,
        my_rows,
        token_gradient[None],
        sums[0],
        sum_query,
        sum_key,
        sum_value,
        sum_output,
        sum_bucket,
        sums[1],
        sum_widen,
        summed[:ff],
        sums[2],
    )


def solution(mesh):
    placed = (
        P("tower", "batch", None),
        P("tower", "batch"),
        P("tower", "batch"),
        P(),
        P(),
        P(),
        P(),
        P(),
        P(),
        P(),
        P(),
        P(),
        P(),
        P(),
    )
    return jax.shard_map(
        functools.partial(local, mesh.shape["batch"]),
        mesh=mesh,
        in_specs=placed,
        out_specs=(
            P(),
            P("batch", None),
            P("tower", "batch", None),
            P(),
            P(),
            P(),
            P(),
            P(),
            P(),
            P(),
            P(),
            P(),
            P(),
        ),
        check_vma=False,
    )
```

```python
import functools

import jax
import jax.numpy as jnp
from jax import lax
from jax.experimental import pallas as pl
from jax.experimental.pallas import tpu as pltpu
from jax.sharding import PartitionSpec as P

epsilon = 1e-06
masked_score = -1000000000.0
score_scale = 100.0
far_steps = (12, 16, 23, 32, 46, 64, 91)
highest = lax.Precision.HIGHEST


MESH = pl.DeviceIdType.MESH
job_rows = 384
unit_rows = 128


def batch_dims(size):
    sizes = {16: (2, 2, 4), 64: (4, 4, 4)}[size]
    strides = (1, sizes[0], sizes[0] * sizes[1])
    return dict(zip("xyz", zip(strides, sizes)))


def place():
    return lax.axis_index("tower"), lax.axis_index("batch")


def gather_kernel(groups, block_ref, out_ref, slots, send_sem, recv_sem, mate_sem):
    tower, batch = place()
    barrier = pltpu.get_barrier_semaphore()
    mate = (1 - tower, batch)

    def peer(step):
        return tower, lax.rem(batch + step, groups)

    def greet(step, carry):
        pl.semaphore_signal(barrier, 1, device_id=peer(step), device_id_type=MESH)
        return carry

    lax.fori_loop(1, groups, greet, 0)
    pl.semaphore_signal(barrier, 1, device_id=mate, device_id_type=MESH)
    slots[tower, batch] = block_ref[...]
    pl.semaphore_wait(barrier, groups)

    def copy(step, owner):
        return pltpu.make_async_remote_copy(
            src_ref=block_ref,
            dst_ref=slots.at[tower, owner],
            send_sem=send_sem.at[step],
            recv_sem=recv_sem.at[owner],
            device_id=peer(step),
            device_id_type=MESH,
        )

    def begin(step, carry):
        copy(step, batch).start()
        return carry

    def finish(step, carry):
        copy(step, batch).wait_send()
        copy(step, peer(step)[1]).wait_recv()
        return carry

    lax.fori_loop(1, groups, begin, 0)
    lax.fori_loop(1, groups, finish, 0)
    side = pltpu.make_async_remote_copy(
        src_ref=slots.at[tower],
        dst_ref=slots.at[tower],
        send_sem=mate_sem.at[0],
        recv_sem=mate_sem.at[1],
        device_id=mate,
        device_id_type=MESH,
    )
    side.start()
    side.wait()
    out_ref[...] = slots[...]


def gather_blocks(block, groups, collective):
    whole = (2, groups) + block.shape
    return pl.pallas_call(
        functools.partial(gather_kernel, groups),
        out_shape=jax.ShapeDtypeStruct(whole, jnp.float32),
        in_specs=[pl.BlockSpec(memory_space=pltpu.VMEM)],
        out_specs=pl.BlockSpec(memory_space=pltpu.VMEM),
        scratch_shapes=[
            pltpu.VMEM(whole, jnp.float32),
            pltpu.SemaphoreType.DMA((groups,)),
            pltpu.SemaphoreType.DMA((groups,)),
            pltpu.SemaphoreType.DMA((2,)),
        ],
        compiler_params=pltpu.CompilerParams(collective_id=collective, has_side_effects=True),
        name="gather_blocks",
    )(block)


def both(first, second):
    if first is None:
        return second
    if second is None:
        return first
    return jnp.logical_and(first, second)


def guarded(condition, action):
    if condition is None:
        action()
    else:
        pl.when(condition)(action)


def hands_back(order, dims, index):
    return index == 0 and all(dims[name][1] == 2 for name in order[1:])


def plan_unit(order, dims, coords, batch, rows):
    add, spread = [], []
    start, active, column = 0, None, None
    for index, name in enumerate(order):
        stride, size = dims[name]
        coord = coords[name]
        if size == 4:
            low_side = coord < 2
            inner = jnp.logical_or(coord == 1, coord == 2)
            outer = jnp.logical_not(inner)
            mate = batch + stride * (1 - 2 * lax.rem(coord, 2))
            share = hands_back(order, dims, index)
            sent = rows * 3 // 4 if share else rows
            first = start + jnp.where(low_side, rows // 4, 0) if share else start
            add.append(
                dict(rows=sent, send=first, keep=first, peer=mate, one_way=True,
                     sends=both(active, outer), receives=both(active, inner)))
            spread.append(
                dict(rows=sent, send=first, peer=mate,
                     sends=both(active, inner), receives=both(active, outer)))
            active_inner = both(active, inner)
            bit = coord // 2
            half = rows // 2
            kept = start + bit * half
            other = batch + stride * (3 - 2 * coord)
            add.append(
                dict(rows=half, send=start + (1 - bit) * half, keep=kept, peer=other, one_way=False,
                     sends=active_inner, receives=active_inner))
            spread.append(dict(rows=half, send=kept, peer=other, sends=active_inner, receives=active_inner))
            if share:
                quarter = rows // 4
                last = start + jnp.where(low_side, 0, 3 * quarter)
                add.append(
                    dict(rows=quarter, send=last, keep=last, peer=mate, one_way=True,
                         sends=active_inner, receives=both(active, outer)))
                spread.append(
                    dict(rows=quarter, send=last, peer=mate,
                         sends=both(active, outer), receives=active_inner))
                start, rows = start + coord * quarter, quarter
            else:
                start, rows, active = kept, half, active_inner
            continue
        mate = batch + stride * (1 - 2 * coord)
        if rows > 8:
            rows = rows // 2
            kept = start + coord * rows
            add.append(
                dict(rows=rows, send=start + (1 - coord) * rows, keep=kept, peer=mate, one_way=False,
                     sends=active, receives=active))
            spread.append(dict(rows=rows, send=kept, peer=mate, sends=active, receives=active))
            start = kept
        else:
            add.append(
                dict(rows=rows, send=start, keep=start, peer=mate, one_way=False, sends=active, receives=active,
                     send_side=1 - coord, keep_side=coord))
            spread.append(
                dict(rows=rows, send=start, peer=mate, sends=active, receives=active, send_side=coord))
    return add, spread[::-1]


def plan_shapes(order, dims, rows):
    result = []
    for index, name in enumerate(order):
        if dims[name][1] == 4:
            share = hands_back(order, dims, index)
            result.append((rows * 3 // 4 if share else rows, 1, True))
            result.append((rows // 2, 1, False))
            if share:
                result.append((rows // 4, 1, True))
            rows = rows // 4 if share else rows // 2
        elif rows > 8:
            rows //= 2
            result.append((rows, 1, False))
        else:
            result.append((rows, 2, False))
    return result


def step_rings(shapes):
    steps = 2 + 2 * len(shapes)
    rings = [4] * steps
    for index, (_, _, single) in enumerate(shapes):
        if single:
            first, last = 1 + index, steps - 2 - index
            rings[last] = last - first + 4
    return rings


orders = ("xyz", "yxz", "zxy")


def sums_kernel(dims, jobs, *refs):
    (lengths, far, hidden, ffn_in, context, normed, branch, pre, attn, query, key, value, upstream) = refs[:13]
    (tokens, mixed_grad, small, totals, lines, gain, wq, wk, wv) = refs[13:22]
    (narrow_out, widen_out, square_out, token_out, small_out) = refs[22:27]
    (left, right, part, acc, full, mate_in, small_own, small_in, heads_in, by_query, by_key, by_value) = refs[27:39]
    (near_ref, near_sums, far_sums, token_in, mixed_in, token_buffer) = refs[39:45]
    rest = refs[45:]
    half = unit_rows // 2
    shapes = [plan_shapes(order, dims, half) for order in orders]
    counts = [len(shape) for shape in shapes]
    inbox, where = [], 0
    for count in counts:
        inbox.append(rest[where : where + count])
        where += count
    load_sem, right_sem, send_sem, recv_sem, keep_sem, small_sem, heads_sem, token_sem, credit = rest[where:]
    tower, batch = place()
    steps = [2 + 2 * count for count in counts]
    longest = max(steps)
    slots = jobs + longest + 1
    rings = [step_rings(shape) for shape in shapes]
    coords = {name: lax.rem(batch // stride, size) for name, (stride, size) in dims.items()}
    plans = [plan_unit(order, dims, coords, batch, half) for order in orders]
    turned_dims = dict(dims, x=dims["y"], y=dims["x"])
    turned_coords = dict(coords, x=coords["y"], y=coords["x"])
    turned = plan_unit(orders[-1], turned_dims, turned_coords, batch, half)

    def pick(odd, first, second):
        if isinstance(first, int) and isinstance(second, int) and first == second or first is None:
            return first
        if isinstance(first, bool):
            return first
        if getattr(first, "dtype", None) == jnp.bool_:
            return jnp.logical_or(jnp.logical_and(odd, second), jnp.logical_and(jnp.logical_not(odd), first))
        return jnp.where(odd, second, first)

    def plan(unit, job):
        if unit < len(orders) - 1:
            return plans[unit]
        odd = lax.rem(job, 2) == 1
        return tuple(
            [{key: pick(odd, one[key], two[key]) for key in one} for one, two in zip(ones, twos)]
            for ones, twos in zip(plans[unit], turned)
        )

    held, spread_held = acc.shape[0], full.shape[0]
    width = narrow_out.shape[1]
    heads = far.shape[1]
    seqs = lengths.shape[0]
    slot_len = tokens.shape[0] // seqs
    pair = 2 * width // heads
    pairs = heads // 2
    tasks = seqs * pairs
    blocks = slot_len // tile

    barrier = pltpu.get_barrier_semaphore()
    mate = (1 - tower, batch)
    mates, turns = [mate], [mate]
    for stride, size in dims.values():
        coord = lax.rem(batch // stride, size)
        near_mate = (tower, batch + stride * (1 - 2 * lax.rem(coord, 2)))
        mates.append(near_mate)
        turns.append(near_mate)
        if size == 4:
            mates.append((tower, batch + stride * (3 - 2 * coord)))
            turns.append((tower, batch + stride * (2 - 4 * (coord // 2))))
            mates.append(turns[-1])
    for other in mates:
        pl.semaphore_signal(barrier, 1, device_id=other, device_id_type=MESH)

    per_narrow = hidden.shape[1] // job_rows
    per_side = width // job_rows
    sources = [(hidden, branch, per_narrow), (ffn_in, pre, per_narrow), (context, attn, per_side)]
    sources += [(normed, grads, per_side) for grads in (by_query, by_key, by_value)]

    def right_place(job):
        past = job - per_narrow
        group = jnp.where(past < 0, 0, 1 + past // per_side)
        fresh = jnp.where(past < 0, job == 0, lax.rem(past, per_side) == 0)
        return lax.rem(group, 2), fresh

    def left_copies(target, job, columns):
        quarter = target.shape[1] // 4
        return [
            pltpu.make_async_copy(
                columns(pl.ds(n * quarter, quarter)), target.at[lax.rem(job, 2), pl.ds(n * quarter, quarter)],
                load_sem.at[lax.rem(job, 2), n],
            )
            for n in range(4)
        ]

    def load(job):
        place_right, fresh = right_place(job)
        first = 0
        for index, (left_ref, right_ref, count) in enumerate(sources):
            local = job - first

            def go(local=local, left_ref=left_ref, right_ref=right_ref, index=index):
                block = lax.rem(local, per_side) if index == 1 else local
                span = pl.ds(pl.multiple_of(block * job_rows, 128), job_rows)
                for copy in left_copies(left, job, lambda rows: left_ref.at[rows, span]):
                    copy.start()

                def go_right():
                    block = local // per_side if index == 1 else 0
                    span = pl.ds(pl.multiple_of(block * width, 128), width)
                    pltpu.make_async_copy(
                        right_ref.at[:, span], right.at[place_right], right_sem.at[place_right]
                    ).start()

                pl.when(fresh)(go_right)

            pl.when(jnp.logical_and(local >= 0, local < count))(go)
            first += count

    def compute(job):
        slot = lax.rem(job, 2)
        place_right, fresh = right_place(job)
        for copy in left_copies(left, job, lambda rows: normed.at[rows, pl.ds(0, job_rows)]):
            copy.wait()
        pl.when(fresh)(
            lambda: pltpu.make_async_copy(attn, right.at[place_right], right_sem.at[place_right]).wait()
        )
        pl.when(job + 1 < jobs)(lambda: load(job + 1))
        part[slot] = lax.dot_general(
            left[slot], right[place_right], (((0,), (0,)), ((), ())), preferred_element_type=jnp.float32
        )

    def side_columns(item, key):
        if key not in item:
            return slice(None)
        return pl.ds(pl.multiple_of(item[key] * (width // 2), 128), width // 2)

    def remote(unit, step, job):
        add, spread = plan(unit, job)
        turn = lax.rem(job, rings[unit][step])
        place_in = lax.rem(job, held)
        sems = dict(
            send_sem=send_sem.at[unit * longest + step, turn],
            recv_sem=recv_sem.at[unit * longest + step, turn],
            device_id_type=MESH,
        )
        base = unit * half
        if step == 0:
            src = part.at[lax.rem(job, 2), pl.ds(pl.multiple_of(unit * unit_rows + (1 - tower) * half, 8), half)]
            dst = mate_in.at[turn, pl.ds(base, half)]
            return pltpu.make_async_remote_copy(src, dst, device_id=(1 - tower, batch), **sems), None, None
        count = counts[unit]
        item = add[step - 1] if step <= count else spread[step - 1 - count]
        rows = pl.ds(pl.multiple_of(base + item["send"], 8), item["rows"])
        columns = side_columns(item, "send_side")
        if step <= count:
            src, dst = acc.at[place_in, rows, columns], inbox[unit][step - 1].at[turn]
        else:
            src = dst = full.at[lax.rem(job, spread_held), rows, columns]
        copy = pltpu.make_async_remote_copy(src, dst, device_id=(tower, item["peer"]), **sems)
        return copy, item["sends"], item["receives"]

    def place_sums(unit, job, action):
        src = full.at[lax.rem(job, spread_held), pl.ds(unit * half, half)]
        first = unit * unit_rows + tower * half

        def at(ref, row, *columns):
            return lambda: action(src, ref.at[(pl.ds(pl.multiple_of(row + first, 8), half), *columns)])

        past = job - per_narrow
        pl.when(past < 0)(at(narrow_out, job * job_rows))
        columns = pl.ds(pl.multiple_of(past // per_side * width, 128), width)
        pl.when(jnp.logical_and(past >= 0, past < per_narrow))(
            at(widen_out, lax.rem(past, per_side) * job_rows, columns)
        )
        pl.when(past >= per_narrow)(at(square_out, (past - per_narrow) * job_rows))

    def last_copy(unit, job, src, dst):
        turn = lax.rem(job, rings[unit][steps[unit] - 1])
        index = unit * longest + steps[unit] - 1
        return pltpu.make_async_remote_copy(
            src, dst, send_sem=send_sem.at[index, turn], recv_sem=recv_sem.at[index, turn],
            device_id=(1 - tower, batch), device_id_type=MESH,
        )

    def begin_last(unit, job):
        def both_ways(src, dst):
            last_copy(unit, job, src, dst).start()
            pltpu.make_async_copy(src, dst, keep_sem.at[unit, lax.rem(job, 2)]).start()

        place_sums(unit, job, both_ways)

    def finish_last(unit, job):
        src = full.at[lax.rem(job, spread_held), pl.ds(unit * half, half)]
        dst = narrow_out.at[pl.ds(0, half)]
        last_copy(unit, job, src, dst).wait()
        pltpu.make_async_copy(src, dst, keep_sem.at[unit, lax.rem(job, 2)]).wait()

    def one_way(unit, step):
        return 1 <= step <= counts[unit] and shapes[unit][step - 1][2]

    def finish(unit, step, job):
        copy, sends, receives = remote(unit, step, job)
        add, _ = plan(unit, job)
        base = unit * half
        guarded(sends, copy.wait_send)
        turn = lax.rem(job, rings[unit][step])
        place_in = lax.rem(job, held)

        def arrived():
            copy.wait_recv()
            if step == 0:
                own = pl.ds(pl.multiple_of(unit * unit_rows + tower * half, 8), half)
                acc[place_in, pl.ds(base, half)] = part[lax.rem(job, 2), own] + mate_in[turn, pl.ds(base, half)]
            elif step <= counts[unit]:
                item = add[step - 1]
                rows = pl.ds(pl.multiple_of(base + item["keep"], 8), item["rows"])
                columns = side_columns(item, "keep_side")
                total = acc[place_in, rows, columns] + inbox[unit][step - 1][turn]
                if step == counts[unit]:
                    full[lax.rem(job, spread_held), rows, columns] = total
                else:
                    acc[place_in, rows, columns] = total
                if one_way(unit, step):
                    pl.when(job + rings[unit][step] < jobs)(
                        lambda: pl.semaphore_signal(
                            credit.at[unit * longest + step], 1,
                            device_id=(tower, item["peer"]), device_id_type=MESH,
                        )
                    )

        guarded(receives, arrived)

    def advance(unit, step, job):
        if step == steps[unit]:
            finish_last(unit, job)
            return
        if step > 0:
            finish(unit, step - 1, job)
        if step == steps[unit] - 1:
            begin_last(unit, job)
            return
        copy, sends, _ = remote(unit, step, job)

        def begin():
            if one_way(unit, step):
                pl.when(job >= rings[unit][step])(
                    lambda: pl.semaphore_wait(credit.at[unit * longest + step], 1)
                )
            copy.start()

        guarded(sends, begin)

    def small_copy(turn):
        return pltpu.make_async_remote_copy(
            src_ref=small_own.at[turn],
            dst_ref=small_in.at[turn],
            send_sem=small_sem.at[0, turn],
            recv_sem=small_sem.at[1, turn],
            device_id=turns[turn],
            device_id_type=MESH,
        )

    def small_turn(turn):
        if turn > 0:
            small_copy(turn - 1).wait()
            total = small_own[turn - 1] + small_in[turn - 1]
            if turn == len(turns):
                small_out[...] = total
            else:
                small_own[turn] = total
        if turn < len(turns):
            small_copy(turn).start()

    def heads_load(task, begin):
        rows = pl.ds(pl.multiple_of(task // pairs * slot_len, slot_len), slot_len)
        columns = pl.ds(pl.multiple_of(lax.rem(task, pairs) * pair, pair), pair)
        slot = lax.rem(task, 2)
        for index, ref in enumerate((query, key, value, upstream)):
            copy = pltpu.make_async_copy(
                ref.at[rows, columns], heads_in.at[slot, index], heads_sem.at[slot, index]
            )
            copy.start() if begin else copy.wait()

    places = lax.broadcasted_iota(jnp.int32, (slot_len, 1), 0)
    lanes = lax.broadcasted_iota(jnp.int32, (1, pair), 1)

    def attend(task, carry):
        seq, index = task // pairs, lax.rem(task, pairs)
        slot = lax.rem(task, 2)
        heads_load(task, False)
        pl.when(task + 1 < tasks)(lambda: heads_load(task + 1, True))
        queries, keys, values, upper = (heads_in[slot, n] for n in range(4))
        length = lengths[seq]
        keys_across = keys.T
        grads_out = [None] * 2
        query_rows = []
        for side in range(2):
            head = 2 * index + side
            mine = (lanes // (pair // 2) == side).astype(jnp.bfloat16)
            my_queries, my_upper = queries * mine, upper * mine
            raw = dot_across(keys, my_queries)
            soft_grad = dot_across(values, my_upper)
            line = totals[seq, pl.ds(head, 1), :]
            soft_columns, grad_columns = [], []
            near_total = [None] * 3
            far_total = [None] * 2
            for column in range(blocks):
                columns = slice(column * tile, (column + 1) * tile)
                scores = []
                for block in range(blocks):
                    rows = slice(block * tile, (block + 1) * tile)
                    bias = bias_tile(near_ref, head, block, column, far[0, head], far[1, head])
                    scores.append(jnp.where(places[rows] < length, raw[rows, columns] + bias, masked_score))
                soft = jnp.exp(jnp.concatenate(scores, axis=0) - line[:, columns])
                soft_columns.append(soft.astype(jnp.bfloat16))
                by_soft = soft_grad[:, columns]
                grads = soft * (by_soft - jnp.sum(soft * by_soft, axis=0, keepdims=True))
                grad_columns.append(grads.astype(jnp.bfloat16))
                for block in range(blocks):
                    piece = grads[block * tile : (block + 1) * tile]
                    ahead = block - column
                    group, spot = (near_total, 1 - ahead) if abs(ahead) <= 1 else (far_total, int(ahead > 0))
                    group[spot] = piece if group[spot] is None else group[spot] + piece
            for spot in range(3):
                if near_total[spot] is not None:
                    near_sums[head, :, spot * tile : (spot + 1) * tile] += near_total[spot]
            for spot in range(2):
                if far_total[spot] is not None:
                    far_sums[spot, pl.ds(head, 1), :] += jnp.sum(far_total[spot], axis=0, keepdims=True)
            soft_low = jnp.concatenate(soft_columns, axis=1)
            grads_low = jnp.concatenate(grad_columns, axis=1)
            half_rows = slice(side * (pair // 2), (side + 1) * (pair // 2))
            query_rows.append(low_dot(keys_across[half_rows], grads_low).astype(jnp.bfloat16))
            pieces = (low_dot(grads_low, my_queries), low_dot(soft_low, my_upper))
            grads_out = [new if old is None else old + new for old, new in zip(grads_out, pieces)]
        rows = pl.ds(pl.multiple_of(seq * slot_len, slot_len), slot_len)
        columns = pl.ds(pl.multiple_of(index * pair, pair), pair)
        by_query[rows, columns] = jnp.concatenate(query_rows, axis=0).T
        for ref, grads in zip((by_key, by_value), grads_out):
            ref[rows, columns] = grads.astype(jnp.bfloat16)
        return carry

    def token_load(seq, begin):
        rows = pl.ds(pl.multiple_of(seq * slot_len, slot_len), slot_len)
        for index, (ref, target) in enumerate(((tokens, token_in), (mixed_grad, mixed_in))):
            copy = pltpu.make_async_copy(ref.at[rows], target, token_sem.at[index])
            copy.start() if begin else copy.wait()

    def token_store(seq):
        rows = pl.ds(pl.multiple_of(seq * slot_len, slot_len), slot_len)
        return pltpu.make_async_copy(token_buffer, token_out.at[rows], token_sem.at[2])

    def token_task(seq):
        rows = pl.ds(pl.multiple_of(seq * slot_len, slot_len), slot_len)
        token_load(seq, False)
        normed_grad = dot_across(by_query[rows, :], wq[...]) + dot_across(by_key[rows, :], wk[...])
        normed_grad += dot_across(by_value[rows, :], wv[...])
        by_tokens, token_gain = norm_back(token_in[...].astype(jnp.float32), gain[...], normed_grad)
        small_own[0, 0:1] += token_gain
        pl.when(seq > 0)(lambda: token_store(seq - 1).wait())
        token_buffer[...] = (mixed_in[...] + by_tokens).astype(jnp.bfloat16)
        token_store(seq).start()
        pl.when(seq + 1 < seqs)(lambda: token_load(seq + 1, True))

    def close():
        token_store(seqs - 1).wait()
        small_own[0, 8:24, :] = jnp.zeros((16, width), jnp.float32)
        for head in range(heads):
            turned = jnp.concatenate([near_sums[head], jnp.zeros((tile, tile), jnp.float32)], axis=1)
            count = tile // 2
            while count:
                upper = turned[count : 2 * count]
                turned = turned[:count] + pltpu.roll(upper, 4 * tile - count, 1)
                count //= 2
            small_own[0, 8 + head : 9 + head, : 4 * tile] = turned
        small_own[0, 8:24, 2 * tile : 3 * tile] += far_sums[0]
        small_own[0, 8:24, 3 * tile : 4 * tile] += far_sums[1]

    load(0)
    heads_load(0, True)
    token_load(0, True)
    spread_bias(lines, near_ref, heads)
    near_sums[...] = jnp.zeros_like(near_sums)
    far_sums[...] = jnp.zeros_like(far_sums)
    small_own[0, 0:8, :] = small[...]
    pl.semaphore_wait(barrier, len(mates))

    last_attend = jobs - 3 * (width // job_rows)
    first_small = slots - 1 - len(turns)
    first_token = first_small - 1 - seqs

    def slot(time, carry):
        for unit in range(len(orders)):
            for step in range(steps[unit] + 1):
                job = time - 1 - step
                pl.when(jnp.logical_and(job >= 0, job < jobs))(functools.partial(advance, unit, step, job))
        for turn in range(len(turns) + 1):
            pl.when(time == first_small + turn)(functools.partial(small_turn, turn))
        begin = jnp.minimum(time * tasks // last_attend, tasks)
        end = jnp.minimum((time + 1) * tasks // last_attend, tasks)
        lax.fori_loop(begin, end, attend, 0)
        pl.when(time < jobs)(functools.partial(compute, time))
        seq = time - first_token
        pl.when(jnp.logical_and(seq >= 0, seq < seqs))(functools.partial(token_task, seq))
        pl.when(time == first_small - 1)(close)
        return carry

    lax.fori_loop(0, slots, slot, 0)


def sum_weights(batch_size, collective, lengths, far, streamed, small, resident):
    hidden, normed = streamed[0], streamed[3]
    tokens, width = normed.shape
    seqs = lengths.shape[0]
    heads = far.shape[1]
    slot_len = tokens // seqs
    pair = 2 * width // heads
    total = 2 * hidden.shape[1] + 4 * width
    jobs = total // job_rows
    dims = batch_dims(batch_size)
    half = unit_rows // 2
    shapes = [plan_shapes(order, dims, half) for order in orders]
    rings = [step_rings(shape) for shape in shapes]
    inboxes = [
        pltpu.VMEM((rings[unit][1 + index], rows, width // parts), jnp.float32)
        for unit, shape in enumerate(shapes)
        for index, (rows, parts, _) in enumerate(shape)
    ]
    steps = max(len(ring) for ring in rings)
    longest = max(max(ring) for ring in rings)
    turns = 1 + sum(size // 2 for _, size in dims.values())
    lines = 24
    low, full = jnp.bfloat16, jnp.float32
    in_vmem = pl.BlockSpec(memory_space=pltpu.VMEM)
    in_smem = pl.BlockSpec(memory_space=pltpu.SMEM)
    anywhere = pl.BlockSpec(memory_space=pl.ANY)
    return pl.pallas_call(
        functools.partial(sums_kernel, dims, jobs),
        out_shape=(
            jax.ShapeDtypeStruct((hidden.shape[1], width), full),
            jax.ShapeDtypeStruct((width, hidden.shape[1]), full),
            jax.ShapeDtypeStruct((4 * width, width), full),
            jax.ShapeDtypeStruct((tokens, width), low),
            jax.ShapeDtypeStruct((lines, width), full),
        ),
        in_specs=[in_smem] * 2 + [anywhere] * len(streamed) + [in_vmem] * (1 + len(resident)),
        out_specs=(anywhere, anywhere, anywhere, anywhere, in_vmem),
        scratch_shapes=[
            pltpu.VMEM((2, tokens, job_rows), low),
            pltpu.VMEM((2, tokens, width), low),
            pltpu.VMEM((2, job_rows, width), full),
            pltpu.VMEM((steps // 2, 3 * half, width), full),
            pltpu.VMEM((steps, 3 * half, width), full),
            pltpu.VMEM((4, 3 * half, width), full),
            pltpu.VMEM((turns, lines, width), full),
            pltpu.VMEM((turns, lines, width), full),
            pltpu.VMEM((2, 4, slot_len, pair), low),
            pltpu.VMEM((tokens, width), low),
            pltpu.VMEM((tokens, width), low),
            pltpu.VMEM((tokens, width), low),
            pltpu.VMEM((heads, tile, near), full),
            pltpu.VMEM((heads, tile, near), full),
            pltpu.VMEM((2, 16, tile), full),
            pltpu.VMEM((slot_len, width), low),
            pltpu.VMEM((slot_len, width), full),
            pltpu.VMEM((slot_len, width), low),
            *inboxes,
            pltpu.SemaphoreType.DMA((2, 4)),
            pltpu.SemaphoreType.DMA((2,)),
            pltpu.SemaphoreType.DMA((3 * steps, longest)),
            pltpu.SemaphoreType.DMA((3 * steps, longest)),
            pltpu.SemaphoreType.DMA((3, 2)),
            pltpu.SemaphoreType.DMA((2, turns)),
            pltpu.SemaphoreType.DMA((2, 4)),
            pltpu.SemaphoreType.DMA((3,)),
            pltpu.SemaphoreType.REGULAR((3 * steps,)),
        ],
        compiler_params=pltpu.CompilerParams(
            collective_id=collective, has_side_effects=True, vmem_limit_bytes=66500000
        ),
        name="sum_weights",
    )(lengths, far, *streamed, small, *resident)


tile = 128
near = 3 * tile


def bias_lines(bucket_bias):
    buckets, heads = bucket_bias.shape
    spots = jnp.arange(4 * tile, dtype=jnp.int32)
    moved = jnp.where(spots >= near, spots - 4 * tile, spots)
    onehot = offset_onehot(tile - moved, buckets)
    lines = jnp.dot(bucket_bias.T, onehot.T, precision=highest)
    return jnp.pad(lines, ((0, 16 - heads), (0, 0)))


def offset_onehot(offset, buckets):
    spread = jnp.abs(offset)
    far_bucket = 8 + sum(((spread >= step).astype(jnp.int32) for step in far_steps))
    bucket = jnp.where(spread < 8, spread, far_bucket) + jnp.where(offset > 0, buckets // 2, 0)
    return (bucket[:, None] == jnp.arange(buckets, dtype=jnp.int32)[None, :]).astype(jnp.float32)


def spread_bias(lines_ref, near_ref, heads):
    for head in range(heads):
        line = jnp.broadcast_to(lines_ref[head : head + 1, :], (tile, 4 * tile))
        near_ref[head] = pltpu.roll(line, 0, 1, stride=1, stride_axis=0)[:, :near]


def bias_tile(near_ref, head, row_block, column_block, low_far, high_far):
    ahead = row_block - column_block
    if abs(ahead) <= 1:
        spot = 1 - ahead
        return near_ref[head, :, spot * tile : (spot + 1) * tile]
    return jnp.full((tile, tile), high_far if ahead > 0 else low_far, jnp.float32)


def unit_scale(values):
    return lax.rsqrt(jnp.mean(values * values, axis=-1, keepdims=True) + epsilon)


def low_dot(left, right):
    return jnp.dot(left, right, preferred_element_type=jnp.float32)


def dot_across(left, right):
    return lax.dot_general(left, right, (((1,), (1,)), ((), ())), preferred_element_type=jnp.float32)


def forward_kernel(
    lengths, prefixes, far, x_ref, lines_ref, gain_a, wq, wk, wv, wo, gain_f, widen_far, narrow_far, gain_z,
    normed_ref, q_ref, k_ref, v_ref, lse_ref, context_ref, mixed_ref, ffn_ref, hidden_ref, output_ref, pooled_ref,
    near_ref, widen, narrow, weight_sem,
):
    seq = pl.program_id(0)
    heads = far.shape[1]
    slot_len, width = x_ref.shape
    blocks = slot_len // tile
    pair = 2 * width // heads
    length = lengths[seq]
    fetches = [
        pltpu.make_async_copy(widen_far, widen, weight_sem.at[0]),
        pltpu.make_async_copy(narrow_far, narrow, weight_sem.at[1]),
    ]

    def first():
        for fetch in fetches:
            fetch.start()
        spread_bias(lines_ref, near_ref, heads)

    pl.when(seq == 0)(first)
    tokens = x_ref[...].astype(jnp.float32)
    normed = (tokens * unit_scale(tokens) * gain_a[...]).astype(jnp.bfloat16)
    normed_ref[...] = normed
    q_ref[...] = low_dot(normed, wq[...]).astype(jnp.bfloat16)
    k_ref[...] = low_dot(normed, wk[...]).astype(jnp.bfloat16)
    v_ref[...] = low_dot(normed, wv[...]).astype(jnp.bfloat16)
    lanes = lax.broadcasted_iota(jnp.int32, (1, pair), 1)
    places = lax.broadcasted_iota(jnp.int32, (slot_len, 1), 0)

    def attend(index, carry):
        span = pl.ds(pl.multiple_of(index * pair, pair), pair)
        keys = k_ref[:, span]
        queries = q_ref[:, span]
        values_across = v_ref[:, span].T
        pieces = []
        for side in range(2):
            head = 2 * index + side
            mine = (lanes // (pair // 2) == side).astype(jnp.bfloat16)
            raw = dot_across(keys, queries * mine)
            soft_columns, lines = [], []
            for column in range(blocks):
                columns = slice(column * tile, (column + 1) * tile)
                scores = []
                for block in range(blocks):
                    rows = slice(block * tile, (block + 1) * tile)
                    bias = bias_tile(near_ref, head, block, column, far[0, head], far[1, head])
                    scores.append(jnp.where(places[rows] < length, raw[rows, columns] + bias, masked_score))
                scores = jnp.concatenate(scores, axis=0)
                peak = jnp.max(scores, axis=0, keepdims=True)
                raised = jnp.exp(scores - peak)
                total = jnp.sum(raised, axis=0, keepdims=True)
                soft_columns.append((raised * (1.0 / total)).astype(jnp.bfloat16))
                lines.append(peak + jnp.log(total))
            lse_ref[0, pl.ds(head, 1), :] = jnp.concatenate(lines, axis=1)
            soft_low = jnp.concatenate(soft_columns, axis=1)
            rows = slice(side * (pair // 2), (side + 1) * (pair // 2))
            pieces.append(low_dot(values_across[rows], soft_low).astype(jnp.bfloat16))
        context_ref[:, span] = jnp.concatenate(pieces, axis=0).T
        return carry

    lax.fori_loop(0, heads // 2, attend, 0)
    mixed = tokens + low_dot(context_ref[...], wo[...])
    mixed_ref[...] = mixed
    ffn_in = (mixed * unit_scale(mixed) * gain_f[...]).astype(jnp.bfloat16)
    ffn_ref[...] = ffn_in
    output_ref[...] = mixed
    pl.when(seq == 0)(lambda: [fetch.wait() for fetch in fetches] and None)

    def feed(index, carry):
        span = pl.ds(pl.multiple_of(index * width, 128), width)
        pre_act = low_dot(ffn_ref[...], widen[:, span])
        hidden = jnp.where(pre_act > 0, pre_act, 0.0).astype(jnp.bfloat16)
        hidden_ref[:, span] = hidden
        output_ref[...] += low_dot(hidden, narrow[span, :])
        return carry

    lax.fori_loop(0, widen.shape[1] // width, feed, 0)
    output = output_ref[...]
    mask = jnp.logical_and(places >= prefixes[seq], places < length).astype(jnp.float32)
    count = (length - prefixes[seq]).astype(jnp.float32)
    final = output * unit_scale(output) * gain_z[...]
    pooled_ref[0] = jnp.sum(final * (mask / count), axis=0, keepdims=True)


def run_forward(tokens, lengths, prefixes, far, lines, gains, weights):
    rows, width = tokens.shape
    seqs = lengths.shape[0]
    slot_len = rows // seqs
    heads = far.shape[1]
    wq, wk, wv, wo, widen, narrow = weights
    gain_a, gain_f, gain_z = gains
    ff = widen.shape[1]

    def whole(shape):
        return pl.BlockSpec(shape, lambda n, *_: (0,) * len(shape), pipeline_mode=pl.Buffered(1))

    def block(columns):
        return pl.BlockSpec((slot_len, columns), lambda n, *_: (n, 0))

    square = whole((width, width))
    line = whole((1, width))
    low, full = jnp.bfloat16, jnp.float32

    def shape(columns, kind):
        return jax.ShapeDtypeStruct((rows, columns), kind)

    return pl.pallas_call(
        forward_kernel,
        grid_spec=pltpu.PrefetchScalarGridSpec(
            num_scalar_prefetch=3,
            grid=(seqs,),
            in_specs=[
                block(width), whole((16, 4 * tile)), line, square, square, square, square,
                line, pl.BlockSpec(memory_space=pl.ANY), pl.BlockSpec(memory_space=pl.ANY), line,
            ],
            out_specs=[
                block(width), block(width), block(width), block(width),
                pl.BlockSpec((1, 16, slot_len), lambda n, *_: (n, 0, 0)),
                block(width), block(width), block(width), block(ff), block(width),
                pl.BlockSpec((1, 1, width), lambda n, *_: (n, 0, 0)),
            ],
            scratch_shapes=[
                pltpu.VMEM((heads, tile, near), jnp.float32),
                pltpu.VMEM((width, ff), low),
                pltpu.VMEM((ff, width), low),
                pltpu.SemaphoreType.DMA((2,)),
            ],
        ),
        out_shape=(
            shape(width, low), shape(width, low), shape(width, low), shape(width, low),
            jax.ShapeDtypeStruct((seqs, 16, slot_len), full),
            shape(width, low), shape(width, full), shape(width, low), shape(ff, low), shape(width, full),
            jax.ShapeDtypeStruct((seqs, 1, width), full),
        ),
        compiler_params=pltpu.CompilerParams(vmem_limit_bytes=60000000),
        name="forward",
    )(lengths, prefixes, far, tokens, lines, gain_a[None], wq, wk, wv, wo, gain_f[None], widen, narrow, gain_z[None])


def norm_back(values, gain, upstream):
    inverse = unit_scale(values)
    scaled = upstream * gain
    inner = jnp.mean(scaled * values, axis=-1, keepdims=True)
    by_values = inverse * scaled - values * (inverse * inverse * inverse) * inner
    return by_values, jnp.sum(upstream * values * inverse, axis=0, keepdims=True)


def feed_back_kernel(
    lengths, prefixes, wo, gain_f, widen, narrow, gain_z, mixed_ref, hidden_ref, output_ref, pooled_ref,
    branch_ref, pre_ref, attn_ref, context_ref, mixed_grad, gains_ref, feed_grad,
):
    seq = pl.program_id(0)
    slot_len, width = mixed_ref.shape
    length = lengths[seq]

    def clear():
        gains_ref[...] = jnp.zeros_like(gains_ref)

    pl.when(seq == 0)(clear)
    places = lax.broadcasted_iota(jnp.int32, (slot_len, 1), 0)
    mask = jnp.logical_and(places >= prefixes[seq], places < length).astype(jnp.float32)
    count = (length - prefixes[seq]).astype(jnp.float32)
    final_grad = (mask / count) * pooled_ref[0]
    output_grad, final_gain = norm_back(output_ref[...], gain_z[...], final_grad)
    gains_ref[2:3] += final_gain
    mixed_grad[...] = output_grad
    branch_ref[...] = output_grad.astype(jnp.bfloat16)
    feed_grad[...] = jnp.zeros_like(feed_grad)

    def feed(index, carry):
        span = pl.ds(pl.multiple_of(index * width, 128), width)
        hidden_grad = dot_across(branch_ref[...], narrow[span, :])
        pre_grad = jnp.where(hidden_ref[:, span] > 0, hidden_grad, 0.0).astype(jnp.bfloat16)
        pre_ref[:, span] = pre_grad
        feed_grad[...] += dot_across(pre_grad, widen[:, span])
        return carry

    lax.fori_loop(0, widen.shape[1] // width, feed, 0)
    by_mixed, feed_gain = norm_back(mixed_ref[...], gain_f[...], feed_grad[...])
    gains_ref[1:2] += feed_gain
    total_grad = mixed_grad[...] + by_mixed
    mixed_grad[...] = total_grad
    attn_low = total_grad.astype(jnp.bfloat16)
    attn_ref[...] = attn_low
    context_ref[...] = dot_across(attn_low, wo[...]).astype(jnp.bfloat16)


def whole(shape):
    return pl.BlockSpec(shape, lambda n, *_: (0,) * len(shape), pipeline_mode=pl.Buffered(1))


def run_feed_back(lengths, prefixes, gains, weights, mixed, hidden, output, pooled_grad):
    rows, width = mixed.shape
    seqs = lengths.shape[0]
    slot_len = rows // seqs
    wo, widen, narrow = weights
    ff = widen.shape[1]

    def block(columns):
        return pl.BlockSpec((slot_len, columns), lambda n, *_: (n, 0))

    def shape(columns, kind):
        return jax.ShapeDtypeStruct((rows, columns), kind)

    low, full = jnp.bfloat16, jnp.float32
    return pl.pallas_call(
        feed_back_kernel,
        grid_spec=pltpu.PrefetchScalarGridSpec(
            num_scalar_prefetch=2,
            grid=(seqs,),
            in_specs=[
                whole((width, width)), whole((1, width)), whole((width, ff)), whole((ff, width)), whole((1, width)),
                block(width), block(ff), block(width),
                pl.BlockSpec((1, 1, width), lambda n, *_: (n, 0, 0)),
            ],
            out_specs=[
                block(width), block(ff), block(width), block(width), block(width),
                pl.BlockSpec((8, width), lambda n, *_: (0, 0)),
            ],
            scratch_shapes=[pltpu.VMEM((slot_len, width), jnp.float32)],
        ),
        out_shape=(
            shape(width, low), shape(ff, low), shape(width, low), shape(width, low), shape(width, full),
            jax.ShapeDtypeStruct((8, width), full),
        ),
        compiler_params=pltpu.CompilerParams(vmem_limit_bytes=60000000),
        name="feed_back",
    )(lengths, prefixes, wo, gains[0][None], widen, narrow, gains[1][None], mixed, hidden, output, pooled_grad)


def bucket_sums(offset_sums, shape):
    spots = jnp.arange(4 * tile, dtype=jnp.int32)
    moved = jnp.where(spots >= near, spots - 4 * tile, spots)
    onehot = offset_onehot(tile - moved, shape[0])
    return jnp.dot(onehot.T, offset_sums[: shape[1]].T, precision=highest)


def local(
    batch_size,
    tokens,
    lengths,
    prefixes,
    positives,
    gain_attention,
    query_weight,
    key_weight,
    value_weight,
    output_weight,
    bucket_bias,
    gain_feedforward,
    widen_weight,
    narrow_weight,
    gain_final,
):
    seqs = lengths.shape[1]
    width = tokens.shape[2]
    buckets = bucket_bias.shape[0]
    far = jnp.stack([bucket_bias[buckets // 2 - 1], bucket_bias[buckets - 1]])
    gains = (gain_attention, gain_feedforward, gain_final)
    weights = (query_weight, key_weight, value_weight, output_weight, widen_weight, narrow_weight)
    lines = bias_lines(bucket_bias)
    normed, query, key, value, totals, context, mixed, ffn_in, hidden, output, pooled = run_forward(
        tokens[0], lengths[0], prefixes[0], far, lines, gains, weights
    )
    pooled = pooled[:, 0]
    inverse_pool = lax.rsqrt(jnp.sum(pooled * pooled, axis=-1, keepdims=True) + epsilon)
    unit = pooled * inverse_pool
    gathered = gather_blocks(unit, batch_size, 0).reshape(2 * batch_size * seqs, width)
    total_seqs = gathered.shape[0] // 2
    query_units = gathered[:total_seqs]
    doc_units = gathered[total_seqs:]
    scores = score_scale * jnp.dot(query_units, doc_units.T, precision=highest)
    labels = jnp.arange(total_seqs, dtype=jnp.int32)
    target = (positives[:, None] == labels[None, :]).astype(jnp.float32)
    row_peak = jnp.max(scores, axis=1, keepdims=True)
    row_raised = jnp.exp(scores - row_peak)
    row_sum = jnp.sum(row_raised, axis=1, keepdims=True)
    col_peak = jnp.max(scores, axis=0, keepdims=True)
    col_raised = jnp.exp(scores - col_peak)
    col_sum = jnp.sum(col_raised, axis=0, keepdims=True)
    loss_value = (
        0.5 * jnp.sum(row_peak[:, 0] + jnp.log(row_sum[:, 0]))
        + 0.5 * jnp.sum(col_peak[0] + jnp.log(col_sum[0]))
        - jnp.sum(target * scores)
    )
    score_grad = 0.5 * row_raised / row_sum + 0.5 * col_raised / col_sum - target
    tower = lax.axis_index("tower")
    first_row = lax.axis_index("batch") * seqs
    my_rows = lax.dynamic_slice_in_dim(score_grad, first_row, seqs, 0)
    my_cols = lax.dynamic_slice_in_dim(score_grad, first_row, seqs, 1)
    grad_as_query = score_scale * jnp.dot(my_rows, doc_units, precision=highest)
    grad_as_doc = score_scale * jnp.dot(my_cols.T, query_units, precision=highest)
    grad_unit = jnp.where(tower == 0, grad_as_query, grad_as_doc)
    cubed = inverse_pool * inverse_pool * inverse_pool
    grad_pooled = inverse_pool * grad_unit - pooled * cubed * jnp.sum(
        grad_unit * pooled, axis=-1, keepdims=True
    )
    branch, pre, attn, context_grad, mixed_grad, feed_gains = run_feed_back(
        lengths[0], prefixes[0], gains[1:], weights[3:], mixed, hidden, output, grad_pooled[:, None]
    )
    streamed = (
        hidden, ffn_in, context, normed, branch, pre, attn, query, key, value, context_grad, tokens[0], mixed_grad
    )
    resident = (totals, lines, gain_attention[None], *weights[:3])
    sum_narrow, sum_widen, squares, token_gradient, sums = sum_weights(batch_size, 1, lengths[0], far, streamed, feed_gains, resident)
    sum_bucket = bucket_sums(sums[8:, : 4 * tile], bucket_bias.shape)
    sum_output, sum_query, sum_key, sum_value = (squares[n * width : (n + 1) * width] for n in range(4))
    return (
        loss_value,
        my_rows,
        token_gradient[None],
        sums[0],
        sum_query,
        sum_key,
        sum_value,
        sum_output,
        sum_bucket,
        sums[1],
        sum_widen,
        sum_narrow,
        sums[2],
    )


def solution(mesh):
    placed = (
        P("tower", "batch", None),
        P("tower", "batch"),
        P("tower", "batch"),
        P(),
        P(),
        P(),
        P(),
        P(),
        P(),
        P(),
        P(),
        P(),
        P(),
        P(),
    )
    return jax.shard_map(
        functools.partial(local, mesh.shape["batch"]),
        mesh=mesh,
        in_specs=placed,
        out_specs=(
            P(),
            P("batch", None),
            P("tower", "batch", None),
            P(),
            P(),
            P(),
            P(),
            P(),
            P(),
            P(),
            P(),
            P(),
            P(),
        ),
        check_vma=False,
    )
```

```python
import functools

import jax
import jax.numpy as jnp
from jax import lax
from jax.experimental import pallas as pl
from jax.experimental.pallas import tpu as pltpu
from jax.sharding import PartitionSpec as P

epsilon = 1e-06
masked_score = -1000000000.0
score_scale = 100.0
far_steps = (12, 16, 23, 32, 46, 64, 91)
highest = lax.Precision.HIGHEST


MESH = pl.DeviceIdType.MESH
job_rows = 384
unit_rows = 128


def batch_dims(size):
    sizes = {16: (2, 2, 4), 64: (4, 4, 4)}[size]
    strides = (1, sizes[0], sizes[0] * sizes[1])
    return dict(zip("xyz", zip(strides, sizes)))


def place():
    return lax.axis_index("tower"), lax.axis_index("batch")


def gather_peer(groups, step):
    tower, batch = place()
    return tower, lax.rem(batch + step, groups)


def greet_all(groups):
    tower, batch = place()
    barrier = pltpu.get_barrier_semaphore()

    def greet(step, carry):
        pl.semaphore_signal(barrier, 1, device_id=gather_peer(groups, step), device_id_type=MESH)
        return carry

    lax.fori_loop(1, groups, greet, 0)
    pl.semaphore_signal(barrier, 1, device_id=(1 - tower, batch), device_id_type=MESH)


def gather_units(groups, block_ref, out_ref, slots, send_sem, recv_sem, mate_sem):
    tower, batch = place()
    slots[tower, batch] = block_ref[...]
    pl.semaphore_wait(pltpu.get_barrier_semaphore(), groups)

    def copy(step, owner):
        return pltpu.make_async_remote_copy(
            src_ref=block_ref,
            dst_ref=slots.at[tower, owner],
            send_sem=send_sem.at[step],
            recv_sem=recv_sem.at[owner],
            device_id=gather_peer(groups, step),
            device_id_type=MESH,
        )

    def begin(step, carry):
        copy(step, batch).start()
        return carry

    def finish(step, carry):
        copy(step, batch).wait_send()
        copy(step, gather_peer(groups, step)[1]).wait_recv()
        return carry

    lax.fori_loop(1, groups, begin, 0)
    lax.fori_loop(1, groups, finish, 0)
    side = pltpu.make_async_remote_copy(
        src_ref=slots.at[tower],
        dst_ref=slots.at[tower],
        send_sem=mate_sem.at[0],
        recv_sem=mate_sem.at[1],
        device_id=(1 - tower, batch),
        device_id_type=MESH,
    )
    side.start()
    side.wait()
    out_ref[...] = slots[...]


def both(first, second):
    if first is None:
        return second
    if second is None:
        return first
    return jnp.logical_and(first, second)


def guarded(condition, action):
    if condition is None:
        action()
    else:
        pl.when(condition)(action)


def hands_back(order, dims, index):
    return index == 0 and all(dims[name][1] == 2 for name in order[1:])


def plan_unit(order, dims, coords, batch, rows):
    add, spread = [], []
    start, active, column = 0, None, None
    for index, name in enumerate(order):
        stride, size = dims[name]
        coord = coords[name]
        if size == 4:
            low_side = coord < 2
            inner = jnp.logical_or(coord == 1, coord == 2)
            outer = jnp.logical_not(inner)
            mate = batch + stride * (1 - 2 * lax.rem(coord, 2))
            share = hands_back(order, dims, index)
            sent = rows * 3 // 4 if share else rows
            first = start + jnp.where(low_side, rows // 4, 0) if share else start
            add.append(
                dict(rows=sent, send=first, keep=first, peer=mate, one_way=True,
                     sends=both(active, outer), receives=both(active, inner)))
            spread.append(
                dict(rows=sent, send=first, peer=mate,
                     sends=both(active, inner), receives=both(active, outer)))
            active_inner = both(active, inner)
            bit = coord // 2
            half = rows // 2
            kept = start + bit * half
            other = batch + stride * (3 - 2 * coord)
            add.append(
                dict(rows=half, send=start + (1 - bit) * half, keep=kept, peer=other, one_way=False,
                     sends=active_inner, receives=active_inner))
            spread.append(dict(rows=half, send=kept, peer=other, sends=active_inner, receives=active_inner))
            if share:
                quarter = rows // 4
                last = start + jnp.where(low_side, 0, 3 * quarter)
                add.append(
                    dict(rows=quarter, send=last, keep=last, peer=mate, one_way=True,
                         sends=active_inner, receives=both(active, outer)))
                spread.append(
                    dict(rows=quarter, send=last, peer=mate,
                         sends=both(active, outer), receives=active_inner))
                start, rows = start + coord * quarter, quarter
            else:
                start, rows, active = kept, half, active_inner
            continue
        mate = batch + stride * (1 - 2 * coord)
        if rows > 8:
            rows = rows // 2
            kept = start + coord * rows
            add.append(
                dict(rows=rows, send=start + (1 - coord) * rows, keep=kept, peer=mate, one_way=False,
                     sends=active, receives=active))
            spread.append(dict(rows=rows, send=kept, peer=mate, sends=active, receives=active))
            start = kept
        else:
            add.append(
                dict(rows=rows, send=start, keep=start, peer=mate, one_way=False, sends=active, receives=active,
                     send_side=1 - coord, keep_side=coord))
            spread.append(
                dict(rows=rows, send=start, peer=mate, sends=active, receives=active, send_side=coord))
    return add, spread[::-1]


def plan_shapes(order, dims, rows):
    result = []
    for index, name in enumerate(order):
        if dims[name][1] == 4:
            share = hands_back(order, dims, index)
            result.append((rows * 3 // 4 if share else rows, 1, True))
            result.append((rows // 2, 1, False))
            if share:
                result.append((rows // 4, 1, True))
            rows = rows // 4 if share else rows // 2
        elif rows > 8:
            rows //= 2
            result.append((rows, 1, False))
        else:
            result.append((rows, 2, False))
    return result


def step_rings(shapes):
    steps = 2 + 2 * len(shapes)
    rings = [4] * steps
    for index, (_, _, single) in enumerate(shapes):
        if single:
            first, last = 1 + index, steps - 2 - index
            rings[last] = last - first + 4
    return rings


orders = ("xyz", "yxz", "zxy")


def sums_kernel(dims, jobs, *refs):
    (lengths, table, hidden, ffn_in, context, normed, branch, pre, attn, query, key, value, upstream) = refs[:13]
    (tokens, mixed_grad, small, totals, bias_ref, gain, wq, wk, wv) = refs[13:22]
    (narrow_out, widen_out, square_out, token_out, small_out) = refs[22:27]
    (left, right, part, acc, full, mate_in, small_own, small_in, heads_in, by_query, by_key, by_value) = refs[27:39]
    (near_ref, near_sums, far_sums, token_in, mixed_in, token_buffer) = refs[39:45]
    rest = refs[45:]
    half = unit_rows // 2
    shapes = [plan_shapes(order, dims, half) for order in orders]
    counts = [len(shape) for shape in shapes]
    inbox, where = [], 0
    for count in counts:
        inbox.append(rest[where : where + count])
        where += count
    load_sem, right_sem, send_sem, recv_sem, keep_sem, small_sem, heads_sem, token_sem, credit = rest[where:]
    tower, batch = place()
    steps = [2 + 2 * count for count in counts]
    longest = max(steps)
    slots = jobs + longest + 1
    rings = [step_rings(shape) for shape in shapes]
    coords = {name: lax.rem(batch // stride, size) for name, (stride, size) in dims.items()}
    plans = [plan_unit(order, dims, coords, batch, half) for order in orders]
    turned_dims = dict(dims, x=dims["y"], y=dims["x"])
    turned_coords = dict(coords, x=coords["y"], y=coords["x"])
    turned = plan_unit(orders[-1], turned_dims, turned_coords, batch, half)

    def pick(odd, first, second):
        if isinstance(first, int) and isinstance(second, int) and first == second or first is None:
            return first
        if isinstance(first, bool):
            return first
        if getattr(first, "dtype", None) == jnp.bool_:
            return jnp.logical_or(jnp.logical_and(odd, second), jnp.logical_and(jnp.logical_not(odd), first))
        return jnp.where(odd, second, first)

    def plan(unit, job):
        if unit < len(orders) - 1:
            return plans[unit]
        odd = lax.rem(job, 2) == 1
        return tuple(
            [{key: pick(odd, one[key], two[key]) for key in one} for one, two in zip(ones, twos)]
            for ones, twos in zip(plans[unit], turned)
        )

    held, spread_held = acc.shape[0], full.shape[0]
    width = narrow_out.shape[1]
    heads = table.shape[1]
    seqs = lengths.shape[0]
    slot_len = tokens.shape[0] // seqs
    pair = 2 * width // heads
    group = heads_in.shape[3]
    pairs = width // group
    tasks = seqs * pairs
    blocks = slot_len // tile

    barrier = pltpu.get_barrier_semaphore()
    mate = (1 - tower, batch)
    mates, turns = [mate], [mate]
    for stride, size in dims.values():
        coord = lax.rem(batch // stride, size)
        near_mate = (tower, batch + stride * (1 - 2 * lax.rem(coord, 2)))
        mates.append(near_mate)
        turns.append(near_mate)
        if size == 4:
            mates.append((tower, batch + stride * (3 - 2 * coord)))
            turns.append((tower, batch + stride * (2 - 4 * (coord // 2))))
            mates.append(turns[-1])
    for other in mates:
        pl.semaphore_signal(barrier, 1, device_id=other, device_id_type=MESH)

    per_narrow = hidden.shape[1] // job_rows
    per_side = width // job_rows
    sources = [(hidden, branch, per_narrow), (ffn_in, pre, per_narrow), (context, attn, per_side)]
    sources += [(normed, grads, per_side) for grads in (by_query, by_key, by_value)]

    def right_place(job):
        past = job - per_narrow
        group = jnp.where(past < 0, 0, 1 + past // per_side)
        fresh = jnp.where(past < 0, job == 0, lax.rem(past, per_side) == 0)
        return lax.rem(group, 2), fresh

    def left_copies(target, job, columns):
        quarter = target.shape[1] // 4
        return [
            pltpu.make_async_copy(
                columns(pl.ds(n * quarter, quarter)), target.at[lax.rem(job, 2), pl.ds(n * quarter, quarter)],
                load_sem.at[lax.rem(job, 2), n],
            )
            for n in range(4)
        ]

    def load(job):
        place_right, fresh = right_place(job)
        first = 0
        for index, (left_ref, right_ref, count) in enumerate(sources):
            local = job - first

            def go(local=local, left_ref=left_ref, right_ref=right_ref, index=index):
                block = lax.rem(local, per_side) if index == 1 else local
                span = pl.ds(pl.multiple_of(block * job_rows, 128), job_rows)
                for copy in left_copies(left, job, lambda rows: left_ref.at[rows, span]):
                    copy.start()

                def go_right():
                    block = local // per_side if index == 1 else 0
                    span = pl.ds(pl.multiple_of(block * width, 128), width)
                    pltpu.make_async_copy(
                        right_ref.at[:, span], right.at[place_right], right_sem.at[place_right]
                    ).start()

                pl.when(fresh)(go_right)

            pl.when(jnp.logical_and(local >= 0, local < count))(go)
            first += count

    def compute(job):
        slot = lax.rem(job, 2)
        place_right, fresh = right_place(job)
        for copy in left_copies(left, job, lambda rows: normed.at[rows, pl.ds(0, job_rows)]):
            copy.wait()
        pl.when(fresh)(
            lambda: pltpu.make_async_copy(attn, right.at[place_right], right_sem.at[place_right]).wait()
        )
        pl.when(job + 1 < jobs)(lambda: load(job + 1))
        part[slot] = lax.dot_general(
            left[slot], right[place_right], (((0,), (0,)), ((), ())), preferred_element_type=jnp.float32
        )

    def side_columns(item, key):
        if key not in item:
            return slice(None)
        return pl.ds(pl.multiple_of(item[key] * (width // 2), 128), width // 2)

    def remote(unit, step, job):
        add, spread = plan(unit, job)
        turn = lax.rem(job, rings[unit][step])
        place_in = lax.rem(job, held)
        sems = dict(
            send_sem=send_sem.at[unit * longest + step, turn],
            recv_sem=recv_sem.at[unit * longest + step, turn],
            device_id_type=MESH,
        )
        base = unit * half
        if step == 0:
            src = part.at[lax.rem(job, 2), pl.ds(pl.multiple_of(unit * unit_rows + (1 - tower) * half, 8), half)]
            dst = mate_in.at[turn, pl.ds(base, half)]
            return pltpu.make_async_remote_copy(src, dst, device_id=(1 - tower, batch), **sems), None, None
        count = counts[unit]
        item = add[step - 1] if step <= count else spread[step - 1 - count]
        rows = pl.ds(pl.multiple_of(base + item["send"], 8), item["rows"])
        columns = side_columns(item, "send_side")
        if step <= count:
            src, dst = acc.at[place_in, rows, columns], inbox[unit][step - 1].at[turn]
        else:
            src = dst = full.at[lax.rem(job, spread_held), rows, columns]
        copy = pltpu.make_async_remote_copy(src, dst, device_id=(tower, item["peer"]), **sems)
        return copy, item["sends"], item["receives"]

    def place_sums(unit, job, action):
        src = full.at[lax.rem(job, spread_held), pl.ds(unit * half, half)]
        first = unit * unit_rows + tower * half

        def at(ref, row, *columns):
            return lambda: action(src, ref.at[(pl.ds(pl.multiple_of(row + first, 8), half), *columns)])

        past = job - per_narrow
        pl.when(past < 0)(at(narrow_out, job * job_rows))
        columns = pl.ds(pl.multiple_of(past // per_side * width, 128), width)
        pl.when(jnp.logical_and(past >= 0, past < per_narrow))(
            at(widen_out, lax.rem(past, per_side) * job_rows, columns)
        )
        pl.when(past >= per_narrow)(at(square_out, (past - per_narrow) * job_rows))

    def last_copy(unit, job, src, dst):
        turn = lax.rem(job, rings[unit][steps[unit] - 1])
        index = unit * longest + steps[unit] - 1
        return pltpu.make_async_remote_copy(
            src, dst, send_sem=send_sem.at[index, turn], recv_sem=recv_sem.at[index, turn],
            device_id=(1 - tower, batch), device_id_type=MESH,
        )

    def begin_last(unit, job):
        def both_ways(src, dst):
            last_copy(unit, job, src, dst).start()
            pltpu.make_async_copy(src, dst, keep_sem.at[unit, lax.rem(job, 2)]).start()

        place_sums(unit, job, both_ways)

    def finish_last(unit, job):
        src = full.at[lax.rem(job, spread_held), pl.ds(unit * half, half)]
        dst = narrow_out.at[pl.ds(0, half)]
        last_copy(unit, job, src, dst).wait()
        pltpu.make_async_copy(src, dst, keep_sem.at[unit, lax.rem(job, 2)]).wait()

    def one_way(unit, step):
        return 1 <= step <= counts[unit] and shapes[unit][step - 1][2]

    def finish(unit, step, job):
        copy, sends, receives = remote(unit, step, job)
        add, _ = plan(unit, job)
        base = unit * half
        guarded(sends, copy.wait_send)
        turn = lax.rem(job, rings[unit][step])
        place_in = lax.rem(job, held)

        def arrived():
            copy.wait_recv()
            if step == 0:
                own = pl.ds(pl.multiple_of(unit * unit_rows + tower * half, 8), half)
                acc[place_in, pl.ds(base, half)] = part[lax.rem(job, 2), own] + mate_in[turn, pl.ds(base, half)]
            elif step <= counts[unit]:
                item = add[step - 1]
                rows = pl.ds(pl.multiple_of(base + item["keep"], 8), item["rows"])
                columns = side_columns(item, "keep_side")
                total = acc[place_in, rows, columns] + inbox[unit][step - 1][turn]
                if step == counts[unit]:
                    full[lax.rem(job, spread_held), rows, columns] = total
                else:
                    acc[place_in, rows, columns] = total
                if one_way(unit, step):
                    pl.when(job + rings[unit][step] < jobs)(
                        lambda: pl.semaphore_signal(
                            credit.at[unit * longest + step], 1,
                            device_id=(tower, item["peer"]), device_id_type=MESH,
                        )
                    )

        guarded(receives, arrived)

    def advance(unit, step, job):
        if step == steps[unit]:
            finish_last(unit, job)
            return
        if step > 0:
            finish(unit, step - 1, job)
        if step == steps[unit] - 1:
            begin_last(unit, job)
            return
        copy, sends, _ = remote(unit, step, job)

        def begin():
            if one_way(unit, step):
                pl.when(job >= rings[unit][step])(
                    lambda: pl.semaphore_wait(credit.at[unit * longest + step], 1)
                )
            copy.start()

        guarded(sends, begin)

    def small_copy(turn):
        return pltpu.make_async_remote_copy(
            src_ref=small_own.at[turn],
            dst_ref=small_in.at[turn],
            send_sem=small_sem.at[0, turn],
            recv_sem=small_sem.at[1, turn],
            device_id=turns[turn],
            device_id_type=MESH,
        )

    def small_turn(turn):
        if turn > 0:
            small_copy(turn - 1).wait()
            total = small_own[turn - 1] + small_in[turn - 1]
            if turn == len(turns):
                small_out[...] = total
            else:
                small_own[turn] = total
        if turn < len(turns):
            small_copy(turn).start()

    def heads_load(task, begin):
        rows = pl.ds(pl.multiple_of(task // pairs * slot_len, slot_len), slot_len)
        columns = pl.ds(pl.multiple_of(lax.rem(task, pairs) * group, group), group)
        slot = lax.rem(task, 2)
        for index, ref in enumerate((query, key, value, upstream)):
            copy = pltpu.make_async_copy(
                ref.at[rows, columns], heads_in.at[slot, index], heads_sem.at[slot, index]
            )
            copy.start() if begin else copy.wait()

    places = lax.broadcasted_iota(jnp.int32, (slot_len, 1), 0)
    lanes = lax.broadcasted_iota(jnp.int32, (1, pair), 1)

    def attend(task, carry):
        seq, index = task // pairs, lax.rem(task, pairs)
        slot = lax.rem(task, 2)
        heads_load(task, False)
        pl.when(task + 1 < tasks)(lambda: heads_load(task + 1, True))
        for inside in range(group // pair):
            attend_pair(seq, index * (group // pair) + inside, slot, inside)
        return carry

    def attend_pair(seq, index, slot, inside):
        span = slice(inside * pair, (inside + 1) * pair)
        queries, keys, values, upper = (heads_in[slot, n, :, span] for n in range(4))
        length = lengths[seq]
        keys_across = keys.T
        grads_out = [None] * 2
        query_rows = []
        for side in range(2):
            head = 2 * index + side
            mine = (lanes // (pair // 2) == side).astype(jnp.bfloat16)
            my_queries, my_upper = queries * mine, upper * mine
            raw = dot_across(keys, my_queries)
            soft_grad = dot_across(values, my_upper)
            line = totals[seq, pl.ds(head, 1), :]
            soft_columns, grad_columns = [], []
            near_total = [None] * 3
            far_total = [None] * 2
            for column in range(blocks):
                columns = slice(column * tile, (column + 1) * tile)
                scores = []
                for block in range(blocks):
                    rows = slice(block * tile, (block + 1) * tile)
                    bias = bias_tile(near_ref, head, block, column, *far_bias(table, head))
                    scores.append(jnp.where(places[rows] < length, raw[rows, columns] + bias, masked_score))
                soft = jnp.exp(jnp.concatenate(scores, axis=0) - line[:, columns])
                soft_columns.append(soft.astype(jnp.bfloat16))
                by_soft = soft_grad[:, columns]
                grads = soft * (by_soft - jnp.sum(soft * by_soft, axis=0, keepdims=True))
                grad_columns.append(grads.astype(jnp.bfloat16))
                for block in range(blocks):
                    piece = grads[block * tile : (block + 1) * tile]
                    ahead = block - column
                    group, spot = (near_total, 1 - ahead) if abs(ahead) <= 1 else (far_total, int(ahead > 0))
                    group[spot] = piece if group[spot] is None else group[spot] + piece
            for spot in range(3):
                if near_total[spot] is not None:
                    near_sums[head, :, spot * tile : (spot + 1) * tile] += near_total[spot]
            for spot in range(2):
                if far_total[spot] is not None:
                    far_sums[spot, pl.ds(head, 1), :] += jnp.sum(far_total[spot], axis=0, keepdims=True)
            soft_low = jnp.concatenate(soft_columns, axis=1)
            grads_low = jnp.concatenate(grad_columns, axis=1)
            half_rows = slice(side * (pair // 2), (side + 1) * (pair // 2))
            query_rows.append(low_dot(keys_across[half_rows], grads_low).astype(jnp.bfloat16))
            pieces = (low_dot(grads_low, my_queries), low_dot(soft_low, my_upper))
            grads_out = [new if old is None else old + new for old, new in zip(grads_out, pieces)]
        rows = pl.ds(pl.multiple_of(seq * slot_len, slot_len), slot_len)
        columns = pl.ds(pl.multiple_of(index * pair, pair), pair)
        by_query[rows, columns] = jnp.concatenate(query_rows, axis=0).T
        for ref, grads in zip((by_key, by_value), grads_out):
            ref[rows, columns] = grads.astype(jnp.bfloat16)

    def token_load(seq, begin):
        rows = pl.ds(pl.multiple_of(seq * slot_len, slot_len), slot_len)
        for index, (ref, target) in enumerate(((tokens, token_in), (mixed_grad, mixed_in))):
            copy = pltpu.make_async_copy(ref.at[rows], target, token_sem.at[index])
            copy.start() if begin else copy.wait()

    def token_store(seq):
        rows = pl.ds(pl.multiple_of(seq * slot_len, slot_len), slot_len)
        return pltpu.make_async_copy(token_buffer, token_out.at[rows], token_sem.at[2])

    def token_task(seq):
        rows = pl.ds(pl.multiple_of(seq * slot_len, slot_len), slot_len)
        token_load(seq, False)
        normed_grad = dot_across(by_query[rows, :], wq[...]) + dot_across(by_key[rows, :], wk[...])
        normed_grad += dot_across(by_value[rows, :], wv[...])
        by_tokens, token_gain = norm_back(token_in[...].astype(jnp.float32), gain[...][None], normed_grad)
        small_own[0, 0:1] += token_gain
        pl.when(seq > 0)(lambda: token_store(seq - 1).wait())
        token_buffer[...] = (mixed_in[...] + by_tokens).astype(jnp.bfloat16)
        token_store(seq).start()
        pl.when(seq + 1 < seqs)(lambda: token_load(seq + 1, True))

    def close():
        token_store(seqs - 1).wait()
        small_own[0, 8:24, :] = jnp.zeros((16, width), jnp.float32)
        for head in range(heads):
            turned = jnp.concatenate([near_sums[head], jnp.zeros((tile, tile), jnp.float32)], axis=1)
            count = tile // 2
            while count:
                upper = turned[count : 2 * count]
                turned = turned[:count] + pltpu.roll(upper, 4 * tile - count, 1)
                count //= 2
            small_own[0, 8 + head : 9 + head, : 4 * tile] = turned
        small_own[0, 8:24, 2 * tile : 3 * tile] += far_sums[0]
        small_own[0, 8:24, 3 * tile : 4 * tile] += far_sums[1]

    load(0)
    heads_load(0, True)
    token_load(0, True)
    spread_bias(bias_ref, near_ref, heads)
    near_sums[...] = jnp.zeros_like(near_sums)
    far_sums[...] = jnp.zeros_like(far_sums)
    small_own[0, 0:8, :] = small[...]
    pl.semaphore_wait(barrier, len(mates))

    last_attend = jobs - 3 * (width // job_rows) - 1
    first_small = slots - 1 - len(turns)
    first_token = first_small - 1 - seqs

    def slot(time, carry):
        for unit in range(len(orders)):
            for step in range(steps[unit] + 1):
                job = time - 1 - step
                pl.when(jnp.logical_and(job >= 0, job < jobs))(functools.partial(advance, unit, step, job))
        for turn in range(len(turns) + 1):
            pl.when(time == first_small + turn)(functools.partial(small_turn, turn))
        begin = jnp.minimum(time * tasks // last_attend, tasks)
        end = jnp.minimum((time + 1) * tasks // last_attend, tasks)
        pl.when(time < jobs)(functools.partial(compute, time))
        lax.fori_loop(begin, end, attend, 0)
        seq = time - first_token
        pl.when(jnp.logical_and(seq >= 0, seq < seqs))(functools.partial(token_task, seq))
        pl.when(time == first_small - 1)(close)
        return carry

    lax.fori_loop(0, slots, slot, 0)


def sum_weights(batch_size, collective, lengths, bucket_bias, streamed, small, resident):
    hidden, normed = streamed[0], streamed[3]
    tokens, width = normed.shape
    seqs = lengths.shape[0]
    heads = bucket_bias.shape[1]
    slot_len = tokens // seqs
    pair = 2 * width // heads
    total = 2 * hidden.shape[1] + 4 * width
    jobs = total // job_rows
    dims = batch_dims(batch_size)
    half = unit_rows // 2
    shapes = [plan_shapes(order, dims, half) for order in orders]
    rings = [step_rings(shape) for shape in shapes]
    inboxes = [
        pltpu.VMEM((rings[unit][1 + index], rows, width // parts), jnp.float32)
        for unit, shape in enumerate(shapes)
        for index, (rows, parts, _) in enumerate(shape)
    ]
    steps = max(len(ring) for ring in rings)
    longest = max(max(ring) for ring in rings)
    turns = 1 + sum(size // 2 for _, size in dims.values())
    lines = 24
    low, full = jnp.bfloat16, jnp.float32
    in_vmem = pl.BlockSpec(memory_space=pltpu.VMEM)
    in_smem = pl.BlockSpec(memory_space=pltpu.SMEM)
    anywhere = pl.BlockSpec(memory_space=pl.ANY)
    return pl.pallas_call(
        functools.partial(sums_kernel, dims, jobs),
        out_shape=(
            jax.ShapeDtypeStruct((hidden.shape[1], width), full),
            jax.ShapeDtypeStruct((width, hidden.shape[1]), full),
            jax.ShapeDtypeStruct((4 * width, width), full),
            jax.ShapeDtypeStruct((tokens, width), low),
            jax.ShapeDtypeStruct((lines, width), full),
        ),
        in_specs=[in_smem] * 2 + [anywhere] * len(streamed) + [in_vmem] * (1 + len(resident)),
        out_specs=(anywhere, anywhere, anywhere, anywhere, in_vmem),
        scratch_shapes=[
            pltpu.VMEM((2, tokens, job_rows), low),
            pltpu.VMEM((2, tokens, width), low),
            pltpu.VMEM((2, job_rows, width), full),
            pltpu.VMEM((steps // 2, 3 * half, width), full),
            pltpu.VMEM((steps, 3 * half, width), full),
            pltpu.VMEM((4, 3 * half, width), full),
            pltpu.VMEM((turns, lines, width), full),
            pltpu.VMEM((turns, lines, width), full),
            pltpu.VMEM((2, 4, slot_len, 1 * pair), low),
            pltpu.VMEM((tokens, width), low),
            pltpu.VMEM((tokens, width), low),
            pltpu.VMEM((tokens, width), low),
            pltpu.VMEM((heads, tile, near), full),
            pltpu.VMEM((heads, tile, near), full),
            pltpu.VMEM((2, 16, tile), full),
            pltpu.VMEM((slot_len, width), low),
            pltpu.VMEM((slot_len, width), full),
            pltpu.VMEM((slot_len, width), low),
            *inboxes,
            pltpu.SemaphoreType.DMA((2, 4)),
            pltpu.SemaphoreType.DMA((2,)),
            pltpu.SemaphoreType.DMA((3 * steps, longest)),
            pltpu.SemaphoreType.DMA((3 * steps, longest)),
            pltpu.SemaphoreType.DMA((3, 2)),
            pltpu.SemaphoreType.DMA((2, turns)),
            pltpu.SemaphoreType.DMA((2, 4)),
            pltpu.SemaphoreType.DMA((3,)),
            pltpu.SemaphoreType.REGULAR((3 * steps,)),
        ],
        compiler_params=pltpu.CompilerParams(
            collective_id=collective, has_side_effects=True, vmem_limit_bytes=66500000
        ),
        name="sum_weights",
    )(lengths, bucket_bias, *streamed, small, *resident)


tile = 128
near = 3 * tile


def offset_onehot(buckets):
    spots = lax.broadcasted_iota(jnp.int32, (buckets, 4 * tile), 1)
    labels = lax.broadcasted_iota(jnp.int32, (buckets, 4 * tile), 0)
    offset = tile - jnp.where(spots >= near, spots - 4 * tile, spots)
    spread = jnp.abs(offset)
    far_bucket = 8 + sum(((spread >= step).astype(jnp.int32) for step in far_steps))
    bucket = jnp.where(spread < 8, spread, far_bucket) + jnp.where(offset > 0, buckets // 2, 0)
    return (bucket == labels).astype(jnp.float32)


def spread_bias(bias_ref, near_ref, heads):
    lines = lax.dot_general(
        bias_ref[...], offset_onehot(bias_ref.shape[0]), (((0,), (0,)), ((), ())),
        precision=highest, preferred_element_type=jnp.float32,
    )
    for head in range(heads):
        line = jnp.broadcast_to(lines[head : head + 1, :], (tile, 4 * tile))
        near_ref[head] = pltpu.roll(line, 0, 1, stride=1, stride_axis=0)[:, :near]


def far_bias(table, head):
    buckets = table.shape[0]
    return table[buckets // 2 - 1, head], table[buckets - 1, head]


def bias_tile(near_ref, head, row_block, column_block, low_far, high_far):
    ahead = row_block - column_block
    if abs(ahead) <= 1:
        spot = 1 - ahead
        return near_ref[head, :, spot * tile : (spot + 1) * tile]
    return jnp.full((tile, tile), high_far if ahead > 0 else low_far, jnp.float32)


def unit_scale(values):
    return lax.rsqrt(jnp.mean(values * values, axis=-1, keepdims=True) + epsilon)


def low_dot(left, right):
    return jnp.dot(left, right, preferred_element_type=jnp.float32)


def dot_across(left, right):
    return lax.dot_general(left, right, (((1,), (1,)), ((), ())), preferred_element_type=jnp.float32)


def forward_kernel(
    groups, lengths, prefixes, table, x_ref, bias_ref, gain_a, wq, wk, wv, wo, gain_f, widen_far, narrow_far, gain_z,
    normed_ref, q_ref, k_ref, v_ref, lse_ref, context_ref, mixed_ref, ffn_ref, hidden_ref, output_ref, pooled_ref, units_ref,
    near_ref, widen, narrow, weight_sem, slots, block_ref, send_sem, recv_sem, mate_sem,
):
    seq = pl.program_id(0)
    heads = table.shape[1]
    slot_len, width = x_ref.shape
    blocks = slot_len // tile
    pair = 2 * width // heads
    length = lengths[seq]
    fetches = [
        pltpu.make_async_copy(widen_far, widen, weight_sem.at[0]),
        pltpu.make_async_copy(narrow_far, narrow, weight_sem.at[1]),
    ]

    def first():
        greet_all(groups)
        for fetch in fetches:
            fetch.start()
        spread_bias(bias_ref, near_ref, heads)

    pl.when(seq == 0)(first)
    tokens = x_ref[...].astype(jnp.float32)
    normed = (tokens * unit_scale(tokens) * gain_a[...][None]).astype(jnp.bfloat16)
    normed_ref[...] = normed
    q_ref[...] = low_dot(normed, wq[...]).astype(jnp.bfloat16)
    k_ref[...] = low_dot(normed, wk[...]).astype(jnp.bfloat16)
    v_ref[...] = low_dot(normed, wv[...]).astype(jnp.bfloat16)
    lanes = lax.broadcasted_iota(jnp.int32, (1, pair), 1)
    places = lax.broadcasted_iota(jnp.int32, (slot_len, 1), 0)

    def attend(index, carry):
        span = pl.ds(pl.multiple_of(index * pair, pair), pair)
        keys = k_ref[:, span]
        queries = q_ref[:, span]
        values_across = v_ref[:, span].T
        pieces = []
        for side in range(2):
            head = 2 * index + side
            mine = (lanes // (pair // 2) == side).astype(jnp.bfloat16)
            raw = dot_across(keys, queries * mine)
            soft_columns, lines = [], []
            for column in range(blocks):
                columns = slice(column * tile, (column + 1) * tile)
                scores = []
                for block in range(blocks):
                    rows = slice(block * tile, (block + 1) * tile)
                    bias = bias_tile(near_ref, head, block, column, *far_bias(table, head))
                    scores.append(jnp.where(places[rows] < length, raw[rows, columns] + bias, masked_score))
                scores = jnp.concatenate(scores, axis=0)
                peak = jnp.max(scores, axis=0, keepdims=True)
                raised = jnp.exp(scores - peak)
                total = jnp.sum(raised, axis=0, keepdims=True)
                soft_columns.append((raised * (1.0 / total)).astype(jnp.bfloat16))
                lines.append(peak + jnp.log(total))
            lse_ref[0, pl.ds(head, 1), :] = jnp.concatenate(lines, axis=1)
            soft_low = jnp.concatenate(soft_columns, axis=1)
            rows = slice(side * (pair // 2), (side + 1) * (pair // 2))
            pieces.append(low_dot(values_across[rows], soft_low).astype(jnp.bfloat16))
        context_ref[:, span] = jnp.concatenate(pieces, axis=0).T
        return carry

    lax.fori_loop(0, heads // 2, attend, 0, unroll=True)
    mixed = tokens + low_dot(context_ref[...], wo[...])
    mixed_ref[...] = mixed
    ffn_in = (mixed * unit_scale(mixed) * gain_f[...][None]).astype(jnp.bfloat16)
    ffn_ref[...] = ffn_in
    output_ref[...] = mixed
    pl.when(seq == 0)(lambda: [fetch.wait() for fetch in fetches] and None)

    def feed(index, carry):
        span = pl.ds(pl.multiple_of(index * width, 128), width)
        pre_act = low_dot(ffn_ref[...], widen[:, span])
        hidden = jnp.where(pre_act > 0, pre_act, 0.0).astype(jnp.bfloat16)
        hidden_ref[:, span] = hidden
        output_ref[...] += low_dot(hidden, narrow[span, :])
        return carry

    lax.fori_loop(0, widen.shape[1] // width, feed, 0, unroll=True)
    output = output_ref[...]
    mask = jnp.logical_and(places >= prefixes[seq], places < length).astype(jnp.float32)
    count = (length - prefixes[seq]).astype(jnp.float32)
    final = output * unit_scale(output) * gain_z[...][None]
    pooled_ref[pl.ds(seq, 1), :] = jnp.sum(final * (mask / count), axis=0, keepdims=True)

    def last():
        pooled = pooled_ref[...]
        block_ref[...] = pooled * lax.rsqrt(jnp.sum(pooled * pooled, axis=-1, keepdims=True) + epsilon)
        gather_units(groups, block_ref, units_ref, slots, send_sem, recv_sem, mate_sem)

    pl.when(seq == pl.num_programs(0) - 1)(last)


def run_forward(groups, collective, tokens, lengths, prefixes, bucket_bias, gains, weights):
    rows, width = tokens.shape
    seqs = lengths.shape[0]
    slot_len = rows // seqs
    heads = bucket_bias.shape[1]
    wq, wk, wv, wo, widen, narrow = weights
    gain_a, gain_f, gain_z = gains
    ff = widen.shape[1]
    units = (2, groups, seqs, width)

    def whole(shape):
        return pl.BlockSpec(shape, lambda n, *_: (0,) * len(shape), pipeline_mode=pl.Buffered(1))

    def block(columns):
        return pl.BlockSpec((slot_len, columns), lambda n, *_: (n, 0))

    square = whole((width, width))
    line = whole((width,))
    low, full = jnp.bfloat16, jnp.float32

    def shape(columns, kind):
        return jax.ShapeDtypeStruct((rows, columns), kind)

    return pl.pallas_call(
        functools.partial(forward_kernel, groups),
        grid_spec=pltpu.PrefetchScalarGridSpec(
            num_scalar_prefetch=3,
            grid=(seqs,),
            in_specs=[
                block(width), whole(bucket_bias.shape), line, square, square, square, square,
                line, pl.BlockSpec(memory_space=pl.ANY), pl.BlockSpec(memory_space=pl.ANY), line,
            ],
            out_specs=[
                block(width), block(width), block(width), block(width),
                pl.BlockSpec((1, 16, slot_len), lambda n, *_: (n, 0, 0)),
                block(width), block(width), block(width), block(ff), block(width),
                pl.BlockSpec((seqs, width), lambda n, *_: (0, 0)),
                pl.BlockSpec(units, lambda n, *_: (0, 0, 0, 0)),
            ],
            scratch_shapes=[
                pltpu.VMEM((heads, tile, near), jnp.float32),
                pltpu.VMEM((width, ff), low),
                pltpu.VMEM((ff, width), low),
                pltpu.SemaphoreType.DMA((2,)),
                pltpu.VMEM(units, full),
                pltpu.VMEM((seqs, width), full),
                pltpu.SemaphoreType.DMA((groups,)),
                pltpu.SemaphoreType.DMA((groups,)),
                pltpu.SemaphoreType.DMA((2,)),
            ],
        ),
        out_shape=(
            shape(width, low), shape(width, low), shape(width, low), shape(width, low),
            jax.ShapeDtypeStruct((seqs, 16, slot_len), full),
            shape(width, low), shape(width, full), shape(width, low), shape(ff, low), shape(width, full),
            jax.ShapeDtypeStruct((seqs, width), full),
            jax.ShapeDtypeStruct(units, full),
        ),
        compiler_params=pltpu.CompilerParams(
            collective_id=collective, has_side_effects=True, vmem_limit_bytes=60000000
        ),
        name="forward",
    )(lengths, prefixes, bucket_bias, tokens, bucket_bias, gain_a, wq, wk, wv, wo, gain_f, widen, narrow, gain_z)


def norm_back(values, gain, upstream):
    inverse = unit_scale(values)
    scaled = upstream * gain
    inner = jnp.mean(scaled * values, axis=-1, keepdims=True)
    by_values = inverse * scaled - values * (inverse * inverse * inverse) * inner
    return by_values, jnp.sum(upstream * values * inverse, axis=0, keepdims=True)


def exact_dot(left, right, left_dim, right_dim):
    return lax.dot_general(
        left, right, (((left_dim,), (right_dim,)), ((), ())),
        precision=highest, preferred_element_type=jnp.float32,
    )


def contrast(units_ref, pooled_ref, positives_ref, loss_ref, rows_ref, pooled_grad):
    tower, batch = place()
    _, groups, seqs, width = units_ref.shape
    count = groups * seqs
    queries = units_ref[0].reshape(count, width)
    docs = units_ref[1].reshape(count, width)
    scores = score_scale * exact_dot(queries, docs, 1, 1)
    labels = lax.broadcasted_iota(jnp.int32, (count, count), 1)
    target = (positives_ref[...] == labels).astype(jnp.float32)
    row_peak = jnp.max(scores, axis=1, keepdims=True)
    row_raised = jnp.exp(scores - row_peak)
    row_sum = jnp.sum(row_raised, axis=1, keepdims=True)
    column_peak = jnp.max(scores, axis=0, keepdims=True)
    column_raised = jnp.exp(scores - column_peak)
    column_sum = jnp.sum(column_raised, axis=0, keepdims=True)
    loss = 0.5 * jnp.sum(row_peak + jnp.log(row_sum), axis=0, keepdims=True)
    loss += 0.5 * jnp.sum(column_peak + jnp.log(column_sum), axis=1, keepdims=True)
    loss_ref[...] = loss - jnp.sum(jnp.sum(target * scores, axis=1, keepdims=True), axis=0, keepdims=True)
    grad = 0.5 * row_raised / row_sum + 0.5 * column_raised / column_sum - target
    mine = lax.broadcasted_iota(jnp.int32, (8, count), 0) + batch * seqs
    spots = lax.broadcasted_iota(jnp.int32, (8, count), 1)
    select = (mine == spots).astype(jnp.float32)
    my_rows = exact_dot(select, grad, 1, 0)
    my_columns = exact_dot(select, grad, 1, 1)
    rows_ref[...] = my_rows[:seqs]
    as_query = exact_dot(my_rows, docs, 1, 0)
    as_doc = exact_dot(my_columns, queries, 1, 0)
    unit_grad = (score_scale * jnp.where(tower == 0, as_query, as_doc))[:seqs]
    pooled = pooled_ref[...]
    inverse = lax.rsqrt(jnp.sum(pooled * pooled, axis=-1, keepdims=True) + epsilon)
    cubed = inverse * inverse * inverse
    pooled_grad[:seqs] = inverse * unit_grad - pooled * cubed * jnp.sum(unit_grad * pooled, axis=-1, keepdims=True)


def feed_back_kernel(
    lengths, prefixes, wo, gain_f, widen, narrow, gain_z, mixed_ref, hidden_ref, output_ref, pooled_ref,
    units_ref, positives_ref,
    branch_ref, pre_ref, attn_ref, context_ref, mixed_grad, gains_ref, loss_ref, rows_ref, feed_grad, pooled_grad,
):
    seq = pl.program_id(0)
    slot_len, width = mixed_ref.shape
    length = lengths[seq]

    def clear():
        gains_ref[...] = jnp.zeros_like(gains_ref)
        contrast(units_ref, pooled_ref, positives_ref, loss_ref, rows_ref, pooled_grad)

    pl.when(seq == 0)(clear)
    places = lax.broadcasted_iota(jnp.int32, (slot_len, 1), 0)
    mask = jnp.logical_and(places >= prefixes[seq], places < length).astype(jnp.float32)
    count = (length - prefixes[seq]).astype(jnp.float32)
    final_grad = (mask / count) * pooled_grad[pl.ds(seq, 1), :]
    output_grad, final_gain = norm_back(output_ref[...], gain_z[...][None], final_grad)
    gains_ref[2:3] += final_gain
    mixed_grad[...] = output_grad
    branch_ref[...] = output_grad.astype(jnp.bfloat16)
    feed_grad[...] = jnp.zeros_like(feed_grad)

    def feed(index, carry):
        span = pl.ds(pl.multiple_of(index * 2 * width, 128), 2 * width)
        hidden_grad = dot_across(branch_ref[...], narrow[span, :])
        pre_grad = jnp.where(hidden_ref[:, span] > 0, hidden_grad, 0.0).astype(jnp.bfloat16)
        pre_ref[:, span] = pre_grad
        feed_grad[...] += dot_across(pre_grad, widen[:, span])
        return carry

    lax.fori_loop(0, widen.shape[1] // (2 * width), feed, 0, unroll=True)
    by_mixed, feed_gain = norm_back(mixed_ref[...], gain_f[...][None], feed_grad[...])
    gains_ref[1:2] += feed_gain
    total_grad = mixed_grad[...] + by_mixed
    mixed_grad[...] = total_grad
    attn_low = total_grad.astype(jnp.bfloat16)
    attn_ref[...] = attn_low
    context_ref[...] = dot_across(attn_low, wo[...]).astype(jnp.bfloat16)


def whole(shape):
    return pl.BlockSpec(shape, lambda n, *_: (0,) * len(shape), pipeline_mode=pl.Buffered(1))


def run_feed_back(lengths, prefixes, gains, weights, mixed, hidden, output, pooled, units, positives):
    rows, width = mixed.shape
    seqs = lengths.shape[0]
    slot_len = rows // seqs
    wo, widen, narrow = weights
    ff = widen.shape[1]
    count = positives.shape[0]

    def block(columns):
        return pl.BlockSpec((slot_len, columns), lambda n, *_: (n, 0))

    def shape(columns, kind):
        return jax.ShapeDtypeStruct((rows, columns), kind)

    low, full = jnp.bfloat16, jnp.float32
    return pl.pallas_call(
        feed_back_kernel,
        grid_spec=pltpu.PrefetchScalarGridSpec(
            num_scalar_prefetch=2,
            grid=(seqs,),
            in_specs=[
                whole((width, width)), whole((width,)), whole((width, ff)), whole((ff, width)), whole((width,)),
                block(width), block(ff), block(width),
                whole(pooled.shape), whole(units.shape), whole((count, 1)),
            ],
            out_specs=[
                block(width), block(ff), block(width), block(width), block(width),
                pl.BlockSpec((8, width), lambda n, *_: (0, 0)),
                pl.BlockSpec((1, 1), lambda n, *_: (0, 0)),
                pl.BlockSpec((seqs, count), lambda n, *_: (0, 0)),
            ],
            scratch_shapes=[pltpu.VMEM((slot_len, width), jnp.float32), pltpu.VMEM((8, width), jnp.float32)],
        ),
        out_shape=(
            shape(width, low), shape(ff, low), shape(width, low), shape(width, low), shape(width, full),
            jax.ShapeDtypeStruct((8, width), full),
            jax.ShapeDtypeStruct((1, 1), full),
            jax.ShapeDtypeStruct((seqs, count), full),
        ),
        compiler_params=pltpu.CompilerParams(vmem_limit_bytes=60000000),
        name="feed_back",
    )(
        lengths, prefixes, wo, gains[0], widen, narrow, gains[1], mixed, hidden, output, pooled, units,
        positives[:, None],
    )


def bucket_sums(offset_sums, shape):
    return jnp.dot(offset_onehot(shape[0]), offset_sums[: shape[1]].T, precision=highest)


def local(
    batch_size,
    tokens,
    lengths,
    prefixes,
    positives,
    gain_attention,
    query_weight,
    key_weight,
    value_weight,
    output_weight,
    bucket_bias,
    gain_feedforward,
    widen_weight,
    narrow_weight,
    gain_final,
):
    seqs = lengths.shape[1]
    width = tokens.shape[2]
    gains = (gain_attention, gain_feedforward, gain_final)
    weights = (query_weight, key_weight, value_weight, output_weight, widen_weight, narrow_weight)
    normed, query, key, value, totals, context, mixed, ffn_in, hidden, output, pooled, units = run_forward(
        batch_size, 0, tokens[0], lengths[0], prefixes[0], bucket_bias, gains, weights
    )
    branch, pre, attn, context_grad, mixed_grad, feed_gains, loss, my_rows = run_feed_back(
        lengths[0], prefixes[0], gains[1:], weights[3:], mixed, hidden, output, pooled, units, positives
    )
    streamed = (
        hidden, ffn_in, context, normed, branch, pre, attn, query, key, value, context_grad, tokens[0], mixed_grad
    )
    resident = (totals, bucket_bias, gain_attention, *weights[:3])
    sum_narrow, sum_widen, squares, token_gradient, sums = sum_weights(batch_size, 1, lengths[0], bucket_bias, streamed, feed_gains, resident)
    sum_bucket = bucket_sums(sums[8:, : 4 * tile], bucket_bias.shape)
    sum_output, sum_query, sum_key, sum_value = (squares[n * width : (n + 1) * width] for n in range(4))
    return (
        loss[0, 0],
        my_rows,
        token_gradient[None],
        sums[0],
        sum_query,
        sum_key,
        sum_value,
        sum_output,
        sum_bucket,
        sums[1],
        sum_widen,
        sum_narrow,
        sums[2],
    )


def solution(mesh):
    placed = (
        P("tower", "batch", None),
        P("tower", "batch"),
        P("tower", "batch"),
        P(),
        P(),
        P(),
        P(),
        P(),
        P(),
        P(),
        P(),
        P(),
        P(),
        P(),
    )
    return jax.shard_map(
        functools.partial(local, mesh.shape["batch"]),
        mesh=mesh,
        in_specs=placed,
        out_specs=(
            P(),
            P("batch", None),
            P("tower", "batch", None),
            P(),
            P(),
            P(),
            P(),
            P(),
            P(),
            P(),
            P(),
            P(),
            P(),
        ),
        check_vma=False,
    )
```

```python
import functools

import jax
import jax.numpy as jnp
from jax import lax
from jax.experimental import pallas as pl
from jax.experimental.pallas import tpu as pltpu
from jax.sharding import PartitionSpec as P

epsilon = 1e-06
masked_score = -1000000000.0
score_scale = 100.0
far_steps = (12, 16, 23, 32, 46, 64, 91)
highest = lax.Precision.HIGHEST


MESH = pl.DeviceIdType.MESH
job_rows = 384
unit_rows = 128


def batch_dims(size):
    sizes = {16: (2, 2, 4), 64: (4, 4, 4)}[size]
    strides = (1, sizes[0], sizes[0] * sizes[1])
    return dict(zip("xyz", zip(strides, sizes)))


def place():
    return lax.axis_index("tower"), lax.axis_index("batch")


def gather_peer(groups, step):
    tower, batch = place()
    return tower, lax.rem(batch + step, groups)


def greet_all(groups):
    tower, batch = place()
    barrier = pltpu.get_barrier_semaphore()

    def greet(step, carry):
        pl.semaphore_signal(barrier, 1, device_id=gather_peer(groups, step), device_id_type=MESH)
        return carry

    lax.fori_loop(1, groups, greet, 0)
    pl.semaphore_signal(barrier, 1, device_id=(1 - tower, batch), device_id_type=MESH)


def gather_units(groups, block_ref, out_ref, slots, send_sem, recv_sem, mate_sem):
    tower, batch = place()
    slots[tower, batch] = block_ref[...]
    pl.semaphore_wait(pltpu.get_barrier_semaphore(), groups)

    def copy(step, owner):
        return pltpu.make_async_remote_copy(
            src_ref=block_ref,
            dst_ref=slots.at[tower, owner],
            send_sem=send_sem.at[step],
            recv_sem=recv_sem.at[owner],
            device_id=gather_peer(groups, step),
            device_id_type=MESH,
        )

    def begin(step, carry):
        copy(step, batch).start()
        return carry

    def finish(step, carry):
        copy(step, batch).wait_send()
        copy(step, gather_peer(groups, step)[1]).wait_recv()
        return carry

    lax.fori_loop(1, groups, begin, 0)
    lax.fori_loop(1, groups, finish, 0)
    side = pltpu.make_async_remote_copy(
        src_ref=slots.at[tower],
        dst_ref=slots.at[tower],
        send_sem=mate_sem.at[0],
        recv_sem=mate_sem.at[1],
        device_id=(1 - tower, batch),
        device_id_type=MESH,
    )
    side.start()
    side.wait()
    out_ref[...] = slots[...]


def both(first, second):
    if first is None:
        return second
    if second is None:
        return first
    return jnp.logical_and(first, second)


def guarded(condition, action):
    if condition is None:
        action()
    else:
        pl.when(condition)(action)


def hands_back(order, dims, index):
    return index == 0 and all(dims[name][1] == 2 for name in order[1:])


def plan_unit(order, dims, coords, batch, rows):
    add, spread = [], []
    start, active, column = 0, None, None
    for index, name in enumerate(order):
        stride, size = dims[name]
        coord = coords[name]
        if size == 4:
            low_side = coord < 2
            inner = jnp.logical_or(coord == 1, coord == 2)
            outer = jnp.logical_not(inner)
            mate = batch + stride * (1 - 2 * lax.rem(coord, 2))
            share = hands_back(order, dims, index)
            sent = rows * 3 // 4 if share else rows
            first = start + jnp.where(low_side, rows // 4, 0) if share else start
            add.append(
                dict(rows=sent, send=first, keep=first, peer=mate, one_way=True,
                     sends=both(active, outer), receives=both(active, inner)))
            spread.append(
                dict(rows=sent, send=first, peer=mate,
                     sends=both(active, inner), receives=both(active, outer)))
            active_inner = both(active, inner)
            bit = coord // 2
            half = rows // 2
            kept = start + bit * half
            other = batch + stride * (3 - 2 * coord)
            add.append(
                dict(rows=half, send=start + (1 - bit) * half, keep=kept, peer=other, one_way=False,
                     sends=active_inner, receives=active_inner))
            spread.append(dict(rows=half, send=kept, peer=other, sends=active_inner, receives=active_inner))
            if share:
                quarter = rows // 4
                last = start + jnp.where(low_side, 0, 3 * quarter)
                add.append(
                    dict(rows=quarter, send=last, keep=last, peer=mate, one_way=True,
                         sends=active_inner, receives=both(active, outer)))
                spread.append(
                    dict(rows=quarter, send=last, peer=mate,
                         sends=both(active, outer), receives=active_inner))
                start, rows = start + coord * quarter, quarter
            else:
                start, rows, active = kept, half, active_inner
            continue
        mate = batch + stride * (1 - 2 * coord)
        if rows > 8:
            rows = rows // 2
            kept = start + coord * rows
            add.append(
                dict(rows=rows, send=start + (1 - coord) * rows, keep=kept, peer=mate, one_way=False,
                     sends=active, receives=active))
            spread.append(dict(rows=rows, send=kept, peer=mate, sends=active, receives=active))
            start = kept
        else:
            add.append(
                dict(rows=rows, send=start, keep=start, peer=mate, one_way=False, sends=active, receives=active,
                     send_side=1 - coord, keep_side=coord))
            spread.append(
                dict(rows=rows, send=start, peer=mate, sends=active, receives=active, send_side=coord))
    return add, spread[::-1]


def plan_shapes(order, dims, rows):
    result = []
    for index, name in enumerate(order):
        if dims[name][1] == 4:
            share = hands_back(order, dims, index)
            result.append((rows * 3 // 4 if share else rows, 1, True))
            result.append((rows // 2, 1, False))
            if share:
                result.append((rows // 4, 1, True))
            rows = rows // 4 if share else rows // 2
        elif rows > 8:
            rows //= 2
            result.append((rows, 1, False))
        else:
            result.append((rows, 2, False))
    return result


def step_rings(shapes):
    steps = 2 + 2 * len(shapes)
    rings = [4] * steps
    for index, (_, _, single) in enumerate(shapes):
        if single:
            first, last = 1 + index, steps - 2 - index
            rings[last] = last - first + 4
    return rings


orders = ("xyz", "yxz", "zxy")


def sums_kernel(dims, jobs, *refs):
    (lengths, table, hidden, ffn_in, context, normed, branch, pre, attn, query, key, value, upstream) = refs[:13]
    (tokens, mixed_grad, small, totals, bias_ref, gain, wq, wk, wv) = refs[13:22]
    (narrow_out, widen_out, square_out, token_out, small_out) = refs[22:27]
    (left, right, part, acc, full, mate_in, small_own, small_in, heads_in, by_query, by_key, by_value) = refs[27:39]
    (near_ref, near_sums, far_sums, token_in, mixed_in, token_buffer) = refs[39:45]
    rest = refs[45:]
    half = unit_rows // 2
    shapes = [plan_shapes(order, dims, half) for order in orders]
    counts = [len(shape) for shape in shapes]
    inbox, where = [], 0
    for count in counts:
        inbox.append(rest[where : where + count])
        where += count
    load_sem, right_sem, send_sem, recv_sem, keep_sem, small_sem, heads_sem, token_sem, credit = rest[where:]
    tower, batch = place()
    steps = [2 + 2 * count for count in counts]
    longest = max(steps)
    slots = jobs + longest + 1
    rings = [step_rings(shape) for shape in shapes]
    coords = {name: lax.rem(batch // stride, size) for name, (stride, size) in dims.items()}
    plans = [plan_unit(order, dims, coords, batch, half) for order in orders]
    turned_dims = dict(dims, x=dims["y"], y=dims["x"])
    turned_coords = dict(coords, x=coords["y"], y=coords["x"])
    turned = plan_unit(orders[-1], turned_dims, turned_coords, batch, half)

    def pick(odd, first, second):
        if isinstance(first, int) and isinstance(second, int) and first == second or first is None:
            return first
        if isinstance(first, bool):
            return first
        if getattr(first, "dtype", None) == jnp.bool_:
            return jnp.logical_or(jnp.logical_and(odd, second), jnp.logical_and(jnp.logical_not(odd), first))
        return jnp.where(odd, second, first)

    def plan(unit, job):
        if unit < len(orders) - 1:
            return plans[unit]
        odd = lax.rem(job, 2) == 1
        return tuple(
            [{key: pick(odd, one[key], two[key]) for key in one} for one, two in zip(ones, twos)]
            for ones, twos in zip(plans[unit], turned)
        )

    held, spread_held = acc.shape[0], full.shape[0]
    width = narrow_out.shape[1]
    heads = table.shape[0]
    seqs = lengths.shape[0]
    slot_len = tokens.shape[0] // seqs
    pair = 2 * width // heads
    group = heads_in.shape[3]
    pairs = width // group
    tasks = seqs * pairs
    blocks = slot_len // tile

    barrier = pltpu.get_barrier_semaphore()
    mate = (1 - tower, batch)
    mates, turns = [mate], [mate]
    for stride, size in dims.values():
        coord = lax.rem(batch // stride, size)
        near_mate = (tower, batch + stride * (1 - 2 * lax.rem(coord, 2)))
        mates.append(near_mate)
        turns.append(near_mate)
        if size == 4:
            mates.append((tower, batch + stride * (3 - 2 * coord)))
            turns.append((tower, batch + stride * (2 - 4 * (coord // 2))))
            mates.append(turns[-1])
    for other in mates:
        pl.semaphore_signal(barrier, 1, device_id=other, device_id_type=MESH)

    per_narrow = hidden.shape[1] // job_rows
    per_side = width // job_rows
    sources = [(hidden, branch, per_narrow), (ffn_in, pre, per_narrow), (context, attn, per_side)]
    sources += [(normed, grads, per_side) for grads in (by_query, by_key, by_value)]

    def right_place(job):
        past = job - per_narrow
        group = jnp.where(past < 0, 0, 1 + past // per_side)
        fresh = jnp.where(past < 0, job == 0, lax.rem(past, per_side) == 0)
        return lax.rem(group, 2), fresh

    def left_copies(target, job, columns):
        quarter = target.shape[1] // 4
        return [
            pltpu.make_async_copy(
                columns(pl.ds(n * quarter, quarter)), target.at[lax.rem(job, 2), pl.ds(n * quarter, quarter)],
                load_sem.at[lax.rem(job, 2), n],
            )
            for n in range(4)
        ]

    def load(job):
        place_right, fresh = right_place(job)
        first = 0
        for index, (left_ref, right_ref, count) in enumerate(sources):
            local = job - first

            def go(local=local, left_ref=left_ref, right_ref=right_ref, index=index):
                block = lax.rem(local, per_side) if index == 1 else local
                span = pl.ds(pl.multiple_of(block * job_rows, 128), job_rows)
                for copy in left_copies(left, job, lambda rows: left_ref.at[rows, span]):
                    copy.start()

                def go_right():
                    block = local // per_side if index == 1 else 0
                    span = pl.ds(pl.multiple_of(block * width, 128), width)
                    pltpu.make_async_copy(
                        right_ref.at[:, span], right.at[place_right], right_sem.at[place_right]
                    ).start()

                pl.when(fresh)(go_right)

            pl.when(jnp.logical_and(local >= 0, local < count))(go)
            first += count

    def compute(job):
        slot = lax.rem(job, 2)
        place_right, fresh = right_place(job)
        for copy in left_copies(left, job, lambda rows: normed.at[rows, pl.ds(0, job_rows)]):
            copy.wait()
        pl.when(fresh)(
            lambda: pltpu.make_async_copy(attn, right.at[place_right], right_sem.at[place_right]).wait()
        )
        pl.when(job + 1 < jobs)(lambda: load(job + 1))
        part[lax.rem(job, 3)] = lax.dot_general(
            left[slot], right[place_right], (((0,), (0,)), ((), ())), preferred_element_type=jnp.float32
        )

    def side_columns(item, key):
        if key not in item:
            return slice(None)
        return pl.ds(pl.multiple_of(item[key] * (width // 2), 128), width // 2)

    def remote(unit, step, job):
        add, spread = plan(unit, job)
        turn = lax.rem(job, rings[unit][step])
        place_in = lax.rem(job, held)
        sems = dict(
            send_sem=send_sem.at[unit * longest + step, turn],
            recv_sem=recv_sem.at[unit * longest + step, turn],
            device_id_type=MESH,
        )
        base = unit * half
        if step == 0:
            src = part.at[lax.rem(job, 3), pl.ds(pl.multiple_of(unit * unit_rows + (1 - tower) * half, 8), half)]
            dst = mate_in.at[turn, pl.ds(base, half)]
            return pltpu.make_async_remote_copy(src, dst, device_id=(1 - tower, batch), **sems), None, None
        count = counts[unit]
        item = add[step - 1] if step <= count else spread[step - 1 - count]
        rows = pl.ds(pl.multiple_of(base + item["send"], 8), item["rows"])
        columns = side_columns(item, "send_side")
        if step <= count:
            src, dst = acc.at[place_in, rows, columns], inbox[unit][step - 1].at[turn]
        else:
            src = dst = full.at[lax.rem(job, spread_held), rows, columns]
        copy = pltpu.make_async_remote_copy(src, dst, device_id=(tower, item["peer"]), **sems)
        return copy, item["sends"], item["receives"]

    def place_sums(unit, job, action):
        src = full.at[lax.rem(job, spread_held), pl.ds(unit * half, half)]
        first = unit * unit_rows + tower * half

        def at(ref, row, *columns):
            return lambda: action(src, ref.at[(pl.ds(pl.multiple_of(row + first, 8), half), *columns)])

        past = job - per_narrow
        pl.when(past < 0)(at(narrow_out, job * job_rows))
        columns = pl.ds(pl.multiple_of(past // per_side * width, 128), width)
        pl.when(jnp.logical_and(past >= 0, past < per_narrow))(
            at(widen_out, lax.rem(past, per_side) * job_rows, columns)
        )
        pl.when(past >= per_narrow)(at(square_out, (past - per_narrow) * job_rows))

    def last_copy(unit, job, src, dst):
        turn = lax.rem(job, rings[unit][steps[unit] - 1])
        index = unit * longest + steps[unit] - 1
        return pltpu.make_async_remote_copy(
            src, dst, send_sem=send_sem.at[index, turn], recv_sem=recv_sem.at[index, turn],
            device_id=(1 - tower, batch), device_id_type=MESH,
        )

    def begin_last(unit, job):
        def both_ways(src, dst):
            last_copy(unit, job, src, dst).start()
            pltpu.make_async_copy(src, dst, keep_sem.at[unit, lax.rem(job, 2)]).start()

        place_sums(unit, job, both_ways)

    def finish_last(unit, job):
        src = full.at[lax.rem(job, spread_held), pl.ds(unit * half, half)]
        dst = narrow_out.at[pl.ds(0, half)]
        last_copy(unit, job, src, dst).wait()
        pltpu.make_async_copy(src, dst, keep_sem.at[unit, lax.rem(job, 2)]).wait()

    def one_way(unit, step):
        return 1 <= step <= counts[unit] and shapes[unit][step - 1][2]

    def finish(unit, step, job):
        copy, sends, receives = remote(unit, step, job)
        add, _ = plan(unit, job)
        base = unit * half
        guarded(sends, copy.wait_send)
        turn = lax.rem(job, rings[unit][step])
        place_in = lax.rem(job, held)

        def arrived():
            copy.wait_recv()
            if step == 0:
                own = pl.ds(pl.multiple_of(unit * unit_rows + tower * half, 8), half)
                acc[place_in, pl.ds(base, half)] = part[lax.rem(job, 3), own] + mate_in[turn, pl.ds(base, half)]
            elif step <= counts[unit]:
                item = add[step - 1]
                rows = pl.ds(pl.multiple_of(base + item["keep"], 8), item["rows"])
                columns = side_columns(item, "keep_side")
                total = acc[place_in, rows, columns] + inbox[unit][step - 1][turn]
                if step == counts[unit]:
                    full[lax.rem(job, spread_held), rows, columns] = total
                else:
                    acc[place_in, rows, columns] = total
                if one_way(unit, step):
                    pl.when(job + rings[unit][step] < jobs)(
                        lambda: pl.semaphore_signal(
                            credit.at[unit * longest + step], 1,
                            device_id=(tower, item["peer"]), device_id_type=MESH,
                        )
                    )

        guarded(receives, arrived)

    def advance(unit, step, job):
        if step == steps[unit]:
            finish_last(unit, job)
            return
        if step > 0:
            finish(unit, step - 1, job)
        if step == steps[unit] - 1:
            begin_last(unit, job)
            return
        copy, sends, _ = remote(unit, step, job)

        def begin():
            if one_way(unit, step):
                pl.when(job >= rings[unit][step])(
                    lambda: pl.semaphore_wait(credit.at[unit * longest + step], 1)
                )
            copy.start()

        guarded(sends, begin)

    def small_copy(turn):
        return pltpu.make_async_remote_copy(
            src_ref=small_own.at[turn],
            dst_ref=small_in.at[turn],
            send_sem=small_sem.at[0, turn],
            recv_sem=small_sem.at[1, turn],
            device_id=turns[turn],
            device_id_type=MESH,
        )

    def small_turn(turn):
        if turn > 0:
            small_copy(turn - 1).wait()
            total = small_own[turn - 1] + small_in[turn - 1]
            if turn == len(turns):
                small_out[0:8] = total[0:8]
                small_out[8:, 0:16] = exact_dot(offset_onehot(table.shape[1]), total[8:24, : 4 * tile], 1, 1)
            else:
                small_own[turn] = total
        if turn < len(turns):
            small_copy(turn).start()

    def heads_load(task, begin):
        rows = pl.ds(pl.multiple_of(task // pairs * slot_len, slot_len), slot_len)
        columns = pl.ds(pl.multiple_of(lax.rem(task, pairs) * group, group), group)
        slot = lax.rem(task, 2)
        for index, ref in enumerate((query, key, value, upstream)):
            copy = pltpu.make_async_copy(
                ref.at[rows, columns], heads_in.at[slot, index], heads_sem.at[slot, index]
            )
            copy.start() if begin else copy.wait()

    places = lax.broadcasted_iota(jnp.int32, (slot_len, 1), 0)
    lanes = lax.broadcasted_iota(jnp.int32, (1, pair), 1)

    def attend(task, carry):
        seq, index = task // pairs, lax.rem(task, pairs)
        slot = lax.rem(task, 2)
        heads_load(task, False)
        pl.when(task + 1 < tasks)(lambda: heads_load(task + 1, True))
        for inside in range(group // pair):
            attend_pair(seq, index * (group // pair) + inside, slot, inside)
        return carry

    def attend_pair(seq, index, slot, inside):
        span = slice(inside * pair, (inside + 1) * pair)
        queries, keys, values, upper = (heads_in[slot, n, :, span] for n in range(4))
        length = lengths[seq]
        keys_across = keys.T
        grads_out = [None] * 2
        query_rows = []
        for side in range(2):
            head = 2 * index + side
            mine = (lanes // (pair // 2) == side).astype(jnp.bfloat16)
            my_queries, my_upper = queries * mine, upper * mine
            raw = dot_across(keys, my_queries)
            soft_grad = dot_across(values, my_upper)
            line = totals[seq, pl.ds(head, 1), :]
            soft_columns, grad_columns = [], []
            near_total = [None] * 3
            far_total = [None] * 2
            for column in range(blocks):
                columns = slice(column * tile, (column + 1) * tile)
                scores = []
                for block in range(blocks):
                    rows = slice(block * tile, (block + 1) * tile)
                    bias = bias_tile(near_ref, head, block, column, *far_bias(table, head))
                    scores.append(jnp.where(places[rows] < length, raw[rows, columns] + bias, masked_score))
                soft = jnp.exp(jnp.concatenate(scores, axis=0) - line[:, columns])
                soft_columns.append(soft.astype(jnp.bfloat16))
                by_soft = soft_grad[:, columns]
                grads = soft * (by_soft - jnp.sum(soft * by_soft, axis=0, keepdims=True))
                grad_columns.append(grads.astype(jnp.bfloat16))
                for block in range(blocks):
                    piece = grads[block * tile : (block + 1) * tile]
                    ahead = block - column
                    group, spot = (near_total, 1 - ahead) if abs(ahead) <= 1 else (far_total, int(ahead > 0))
                    group[spot] = piece if group[spot] is None else group[spot] + piece
            for spot in range(3):
                if near_total[spot] is not None:
                    near_sums[head, :, spot * tile : (spot + 1) * tile] += near_total[spot]
            for spot in range(2):
                if far_total[spot] is not None:
                    far_sums[spot, pl.ds(head, 1), :] += jnp.sum(far_total[spot], axis=0, keepdims=True)
            soft_low = jnp.concatenate(soft_columns, axis=1)
            grads_low = jnp.concatenate(grad_columns, axis=1)
            half_rows = slice(side * (pair // 2), (side + 1) * (pair // 2))
            query_rows.append(low_dot(keys_across[half_rows], grads_low).astype(jnp.bfloat16))
            pieces = (low_dot(grads_low, my_queries), low_dot(soft_low, my_upper))
            grads_out = [new if old is None else old + new for old, new in zip(grads_out, pieces)]
        rows = pl.ds(pl.multiple_of(seq * slot_len, slot_len), slot_len)
        columns = pl.ds(pl.multiple_of(index * pair, pair), pair)
        by_query[rows, columns] = jnp.concatenate(query_rows, axis=0).T
        for ref, grads in zip((by_key, by_value), grads_out):
            ref[rows, columns] = grads.astype(jnp.bfloat16)

    def token_load(seq, begin):
        rows = pl.ds(pl.multiple_of(seq * slot_len, slot_len), slot_len)
        for index, (ref, target) in enumerate(((tokens, token_in), (mixed_grad, mixed_in))):
            copy = pltpu.make_async_copy(ref.at[rows], target, token_sem.at[index])
            copy.start() if begin else copy.wait()

    def token_store(seq):
        rows = pl.ds(pl.multiple_of(seq * slot_len, slot_len), slot_len)
        return pltpu.make_async_copy(token_buffer, token_out.at[rows], token_sem.at[2])

    def token_task(seq):
        rows = pl.ds(pl.multiple_of(seq * slot_len, slot_len), slot_len)
        token_load(seq, False)
        normed_grad = dot_across(by_query[rows, :], wq[...]) + dot_across(by_key[rows, :], wk[...])
        normed_grad += dot_across(by_value[rows, :], wv[...])
        by_tokens, token_gain = norm_back(token_in[...].astype(jnp.float32), gain[...][None], normed_grad)
        small_own[0, 0:1] += token_gain
        pl.when(seq > 0)(lambda: token_store(seq - 1).wait())
        token_buffer[...] = (mixed_in[...] + by_tokens).astype(jnp.bfloat16)
        token_store(seq).start()
        pl.when(seq + 1 < seqs)(lambda: token_load(seq + 1, True))

    def close():
        token_store(seqs - 1).wait()
        small_own[0, 8:24, :] = jnp.zeros((16, width), jnp.float32)
        for head in range(heads):
            turned = jnp.concatenate([near_sums[head], jnp.zeros((tile, tile), jnp.float32)], axis=1)
            count = tile // 2
            while count:
                upper = turned[count : 2 * count]
                turned = turned[:count] + pltpu.roll(upper, 4 * tile - count, 1)
                count //= 2
            small_own[0, 8 + head : 9 + head, : 4 * tile] = turned
        small_own[0, 8:24, 2 * tile : 3 * tile] += far_sums[0]
        small_own[0, 8:24, 3 * tile : 4 * tile] += far_sums[1]

    load(0)
    heads_load(0, True)
    token_load(0, True)
    small_own[0, 0:8, :] = small[...]
    compute(jnp.int32(0))
    pl.semaphore_wait(barrier, len(mates))

    last_attend = jobs - 3 * (width // job_rows) - 1
    first_token = last_attend + 1
    first_attend = 5
    first_small = slots - 1 - len(turns)

    def prepare():
        spread_bias(bias_ref, near_ref, heads)
        near_sums[...] = jnp.zeros_like(near_sums)
        far_sums[...] = jnp.zeros_like(far_sums)

    def products(time):
        pl.when(time < jobs)(functools.partial(compute, time))
        pl.when(time == 2)(prepare)

    def attention(time):
        past = jnp.maximum(time - first_attend, 0)
        span = last_attend - first_attend
        begin = jnp.minimum(past * tasks // span, tasks)
        end = jnp.where(time < first_attend, 0, jnp.minimum((past + 1) * tasks // span, tasks))
        lax.fori_loop(begin, end, attend, 0)

    def token_part(time):
        seq = time - first_token
        pl.when(jnp.logical_and(seq >= 0, seq < seqs))(functools.partial(token_task, seq))
        pl.when(time == first_token + seqs)(close)
        for turn in range(len(turns) + 1):
            pl.when(time == first_small + turn)(functools.partial(small_turn, turn))

    def slot(time, carry):
        for unit, work in ((2, products), (0, attention), (1, token_part)):
            for step in range(steps[unit] + 1):
                job = time - 1 - step
                pl.when(jnp.logical_and(job >= 0, job < jobs))(functools.partial(advance, unit, step, job))
            work(time)
        return carry

    lax.fori_loop(1, slots, slot, 0)


def sum_weights(batch_size, collective, lengths, bucket_bias, streamed, small, resident):
    hidden, normed = streamed[0], streamed[3]
    tokens, width = normed.shape
    seqs = lengths.shape[0]
    heads = bucket_bias.shape[0]
    slot_len = tokens // seqs
    pair = 2 * width // heads
    total = 2 * hidden.shape[1] + 4 * width
    jobs = total // job_rows
    dims = batch_dims(batch_size)
    half = unit_rows // 2
    shapes = [plan_shapes(order, dims, half) for order in orders]
    rings = [step_rings(shape) for shape in shapes]
    inboxes = [
        pltpu.VMEM((rings[unit][1 + index], rows, width // parts), jnp.float32)
        for unit, shape in enumerate(shapes)
        for index, (rows, parts, _) in enumerate(shape)
    ]
    steps = max(len(ring) for ring in rings)
    longest = max(max(ring) for ring in rings)
    turns = 1 + sum(size // 2 for _, size in dims.values())
    lines = 24
    low, full = jnp.bfloat16, jnp.float32
    in_vmem = pl.BlockSpec(memory_space=pltpu.VMEM)
    in_smem = pl.BlockSpec(memory_space=pltpu.SMEM)
    anywhere = pl.BlockSpec(memory_space=pl.ANY)
    return pl.pallas_call(
        functools.partial(sums_kernel, dims, jobs),
        out_shape=(
            jax.ShapeDtypeStruct((hidden.shape[1], width), full),
            jax.ShapeDtypeStruct((width, hidden.shape[1]), full),
            jax.ShapeDtypeStruct((4 * width, width), full),
            jax.ShapeDtypeStruct((tokens, width), low),
            jax.ShapeDtypeStruct((8 + bucket_bias.shape[1], width), full),
        ),
        in_specs=[in_smem] * 2 + [anywhere] * len(streamed) + [in_vmem] * (1 + len(resident)),
        out_specs=(anywhere, anywhere, anywhere, anywhere, in_vmem),
        scratch_shapes=[
            pltpu.VMEM((2, tokens, job_rows), low),
            pltpu.VMEM((2, tokens, width), low),
            pltpu.VMEM((3, job_rows, width), full),
            pltpu.VMEM((steps // 2, 3 * half, width), full),
            pltpu.VMEM((steps, 3 * half, width), full),
            pltpu.VMEM((4, 3 * half, width), full),
            pltpu.VMEM((turns, lines, width), full),
            pltpu.VMEM((turns, lines, width), full),
            pltpu.VMEM((2, 4, slot_len, 1 * pair), low),
            pltpu.VMEM((tokens, width), low),
            pltpu.VMEM((tokens, width), low),
            pltpu.VMEM((tokens, width), low),
            pltpu.VMEM((heads, tile, near), full),
            pltpu.VMEM((heads, tile, near), full),
            pltpu.VMEM((2, 16, tile), full),
            pltpu.VMEM((slot_len, width), low),
            pltpu.VMEM((slot_len, width), full),
            pltpu.VMEM((slot_len, width), low),
            *inboxes,
            pltpu.SemaphoreType.DMA((2, 4)),
            pltpu.SemaphoreType.DMA((2,)),
            pltpu.SemaphoreType.DMA((3 * steps, longest)),
            pltpu.SemaphoreType.DMA((3 * steps, longest)),
            pltpu.SemaphoreType.DMA((3, 2)),
            pltpu.SemaphoreType.DMA((2, turns)),
            pltpu.SemaphoreType.DMA((2, 4)),
            pltpu.SemaphoreType.DMA((3,)),
            pltpu.SemaphoreType.REGULAR((3 * steps,)),
        ],
        compiler_params=pltpu.CompilerParams(
            collective_id=collective, has_side_effects=True, vmem_limit_bytes=66500000
        ),
        name="sum_weights",
    )(lengths, bucket_bias, *streamed, small, *resident)


tile = 128
near = 3 * tile


def offset_onehot(buckets):
    spots = lax.broadcasted_iota(jnp.int32, (buckets, 4 * tile), 1)
    labels = lax.broadcasted_iota(jnp.int32, (buckets, 4 * tile), 0)
    offset = tile - jnp.where(spots >= near, spots - 4 * tile, spots)
    spread = jnp.abs(offset)
    far_bucket = 8 + sum(((spread >= step).astype(jnp.int32) for step in far_steps))
    bucket = jnp.where(spread < 8, spread, far_bucket) + jnp.where(offset > 0, buckets // 2, 0)
    return (bucket == labels).astype(jnp.float32)


def spread_bias(bias_ref, near_ref, heads):
    lines = exact_dot(bias_ref[...], offset_onehot(bias_ref.shape[1]), 1, 0)
    for head in range(heads):
        line = jnp.broadcast_to(lines[head : head + 1, :], (tile, 4 * tile))
        near_ref[head] = pltpu.roll(line, 0, 1, stride=1, stride_axis=0)[:, :near]


def far_bias(table, head):
    buckets = table.shape[1]
    return table[head, buckets // 2 - 1], table[head, buckets - 1]


def bias_tile(near_ref, head, row_block, column_block, low_far, high_far):
    ahead = row_block - column_block
    if abs(ahead) <= 1:
        spot = 1 - ahead
        return near_ref[head, :, spot * tile : (spot + 1) * tile]
    return jnp.full((tile, tile), high_far if ahead > 0 else low_far, jnp.float32)


def unit_scale(values):
    return lax.rsqrt(jnp.mean(values * values, axis=-1, keepdims=True) + epsilon)


def low_dot(left, right):
    return jnp.dot(left, right, preferred_element_type=jnp.float32)


def dot_across(left, right):
    return lax.dot_general(left, right, (((1,), (1,)), ((), ())), preferred_element_type=jnp.float32)


def forward_kernel(
    groups, lengths, prefixes, table, x_ref, bias_ref, gain_a, wq, wk, wv, wo, gain_f, widen_far, narrow_far, gain_z,
    normed_ref, q_ref, k_ref, v_ref, lse_ref, context_ref, mixed_ref, ffn_ref, hidden_ref, output_ref, pooled_ref, units_ref,
    near_ref, widen, narrow, weight_sem, slots, block_ref, send_sem, recv_sem, mate_sem,
):
    seq = pl.program_id(0)
    heads = table.shape[0]
    slot_len, width = x_ref.shape
    blocks = slot_len // tile
    pair = 2 * width // heads
    length = lengths[seq]
    fetches = [
        pltpu.make_async_copy(widen_far, widen, weight_sem.at[0]),
        pltpu.make_async_copy(narrow_far, narrow, weight_sem.at[1]),
    ]

    def first():
        greet_all(groups)
        for fetch in fetches:
            fetch.start()
        spread_bias(bias_ref, near_ref, heads)

    pl.when(seq == 0)(first)
    tokens = x_ref[...].astype(jnp.float32)
    normed = (tokens * unit_scale(tokens) * gain_a[...][None]).astype(jnp.bfloat16)
    normed_ref[...] = normed
    q_ref[...] = low_dot(normed, wq[...]).astype(jnp.bfloat16)
    k_ref[...] = low_dot(normed, wk[...]).astype(jnp.bfloat16)
    v_ref[...] = low_dot(normed, wv[...]).astype(jnp.bfloat16)
    lanes = lax.broadcasted_iota(jnp.int32, (1, pair), 1)
    places = lax.broadcasted_iota(jnp.int32, (slot_len, 1), 0)

    def attend(index, carry):
        span = pl.ds(pl.multiple_of(index * pair, pair), pair)
        keys = k_ref[:, span]
        queries = q_ref[:, span]
        values_across = v_ref[:, span].T
        pieces = []
        for side in range(2):
            head = 2 * index + side
            mine = (lanes // (pair // 2) == side).astype(jnp.bfloat16)
            raw = dot_across(keys, queries * mine)
            soft_columns, lines = [], []
            for column in range(blocks):
                columns = slice(column * tile, (column + 1) * tile)
                scores = []
                for block in range(blocks):
                    rows = slice(block * tile, (block + 1) * tile)
                    bias = bias_tile(near_ref, head, block, column, *far_bias(table, head))
                    scores.append(jnp.where(places[rows] < length, raw[rows, columns] + bias, masked_score))
                scores = jnp.concatenate(scores, axis=0)
                peak = jnp.max(scores, axis=0, keepdims=True)
                raised = jnp.exp(scores - peak)
                total = jnp.sum(raised, axis=0, keepdims=True)
                soft_columns.append((raised * (1.0 / total)).astype(jnp.bfloat16))
                lines.append(peak + jnp.log(total))
            lse_ref[0, pl.ds(head, 1), :] = jnp.concatenate(lines, axis=1)
            soft_low = jnp.concatenate(soft_columns, axis=1)
            rows = slice(side * (pair // 2), (side + 1) * (pair // 2))
            pieces.append(low_dot(values_across[rows], soft_low).astype(jnp.bfloat16))
        context_ref[:, span] = jnp.concatenate(pieces, axis=0).T
        return carry

    lax.fori_loop(0, heads // 2, attend, 0, unroll=True)
    mixed = tokens + low_dot(context_ref[...], wo[...])
    mixed_ref[...] = mixed
    ffn_in = (mixed * unit_scale(mixed) * gain_f[...][None]).astype(jnp.bfloat16)
    ffn_ref[...] = ffn_in
    output_ref[...] = mixed
    pl.when(seq == 0)(lambda: [fetch.wait() for fetch in fetches] and None)

    def feed(index, carry):
        span = pl.ds(pl.multiple_of(index * width, 128), width)
        pre_act = low_dot(ffn_ref[...], widen[:, span])
        hidden = jnp.where(pre_act > 0, pre_act, 0.0).astype(jnp.bfloat16)
        hidden_ref[:, span] = hidden
        output_ref[...] += low_dot(hidden, narrow[span, :])
        return carry

    lax.fori_loop(0, widen.shape[1] // width, feed, 0, unroll=True)
    output = output_ref[...]
    mask = jnp.logical_and(places >= prefixes[seq], places < length).astype(jnp.float32)
    count = (length - prefixes[seq]).astype(jnp.float32)
    final = output * unit_scale(output) * gain_z[...][None]
    pooled_ref[pl.ds(seq, 1), :] = jnp.sum(final * (mask / count), axis=0, keepdims=True)

    def last():
        pooled = pooled_ref[...]
        block_ref[...] = pooled * lax.rsqrt(jnp.sum(pooled * pooled, axis=-1, keepdims=True) + epsilon)
        gather_units(groups, block_ref, units_ref, slots, send_sem, recv_sem, mate_sem)

    pl.when(seq == pl.num_programs(0) - 1)(last)


def run_forward(groups, collective, tokens, lengths, prefixes, bucket_bias, gains, weights):
    rows, width = tokens.shape
    seqs = lengths.shape[0]
    slot_len = rows // seqs
    heads = bucket_bias.shape[0]
    wq, wk, wv, wo, widen, narrow = weights
    gain_a, gain_f, gain_z = gains
    ff = widen.shape[1]
    units = (2, groups, seqs, width)

    def whole(shape):
        return pl.BlockSpec(shape, lambda n, *_: (0,) * len(shape), pipeline_mode=pl.Buffered(1))

    def block(columns):
        return pl.BlockSpec((slot_len, columns), lambda n, *_: (n, 0))

    square = whole((width, width))
    line = whole((width,))
    low, full = jnp.bfloat16, jnp.float32

    def shape(columns, kind):
        return jax.ShapeDtypeStruct((rows, columns), kind)

    return pl.pallas_call(
        functools.partial(forward_kernel, groups),
        grid_spec=pltpu.PrefetchScalarGridSpec(
            num_scalar_prefetch=3,
            grid=(seqs,),
            in_specs=[
                block(width), whole(bucket_bias.shape), line, square, square, square, square,
                line, pl.BlockSpec(memory_space=pl.ANY), pl.BlockSpec(memory_space=pl.ANY), line,
            ],
            out_specs=[
                block(width), block(width), block(width), block(width),
                pl.BlockSpec((1, 16, slot_len), lambda n, *_: (n, 0, 0)),
                block(width), block(width), block(width), block(ff), block(width),
                pl.BlockSpec((seqs, width), lambda n, *_: (0, 0)),
                pl.BlockSpec(units, lambda n, *_: (0, 0, 0, 0)),
            ],
            scratch_shapes=[
                pltpu.VMEM((heads, tile, near), jnp.float32),
                pltpu.VMEM((width, ff), low),
                pltpu.VMEM((ff, width), low),
                pltpu.SemaphoreType.DMA((2,)),
                pltpu.VMEM(units, full),
                pltpu.VMEM((seqs, width), full),
                pltpu.SemaphoreType.DMA((groups,)),
                pltpu.SemaphoreType.DMA((groups,)),
                pltpu.SemaphoreType.DMA((2,)),
            ],
        ),
        out_shape=(
            shape(width, low), shape(width, low), shape(width, low), shape(width, low),
            jax.ShapeDtypeStruct((seqs, 16, slot_len), full),
            shape(width, low), shape(width, full), shape(width, low), shape(ff, low), shape(width, full),
            jax.ShapeDtypeStruct((seqs, width), full),
            jax.ShapeDtypeStruct(units, full),
        ),
        compiler_params=pltpu.CompilerParams(
            collective_id=collective, has_side_effects=True, vmem_limit_bytes=60000000
        ),
        name="forward",
    )(lengths, prefixes, bucket_bias, tokens, bucket_bias, gain_a, wq, wk, wv, wo, gain_f, widen, narrow, gain_z)


def norm_back(values, gain, upstream):
    inverse = unit_scale(values)
    scaled = upstream * gain
    inner = jnp.mean(scaled * values, axis=-1, keepdims=True)
    by_values = inverse * scaled - values * (inverse * inverse * inverse) * inner
    return by_values, jnp.sum(upstream * values * inverse, axis=0, keepdims=True)


def exact_dot(left, right, left_dim, right_dim):
    return lax.dot_general(
        left, right, (((left_dim,), (right_dim,)), ((), ())),
        precision=highest, preferred_element_type=jnp.float32,
    )


def contrast(units_ref, pooled_ref, positives_ref, loss_ref, rows_ref, pooled_grad):
    tower, batch = place()
    _, groups, seqs, width = units_ref.shape
    count = groups * seqs
    queries = units_ref[0].reshape(count, width)
    docs = units_ref[1].reshape(count, width)
    scores = score_scale * exact_dot(queries, docs, 1, 1)
    labels = lax.broadcasted_iota(jnp.int32, (count, count), 1)
    target = (positives_ref[...] == labels).astype(jnp.float32)
    row_peak = jnp.max(scores, axis=1, keepdims=True)
    row_raised = jnp.exp(scores - row_peak)
    row_sum = jnp.sum(row_raised, axis=1, keepdims=True)
    column_peak = jnp.max(scores, axis=0, keepdims=True)
    column_raised = jnp.exp(scores - column_peak)
    column_sum = jnp.sum(column_raised, axis=0, keepdims=True)
    loss = 0.5 * jnp.sum(row_peak + jnp.log(row_sum), axis=0, keepdims=True)
    loss += 0.5 * jnp.sum(column_peak + jnp.log(column_sum), axis=1, keepdims=True)
    loss_ref[...] = loss - jnp.sum(jnp.sum(target * scores, axis=1, keepdims=True), axis=0, keepdims=True)
    grad = 0.5 * row_raised / row_sum + 0.5 * column_raised / column_sum - target
    mine = lax.broadcasted_iota(jnp.int32, (8, count), 0) + batch * seqs
    spots = lax.broadcasted_iota(jnp.int32, (8, count), 1)
    select = (mine == spots).astype(jnp.float32)
    my_rows = exact_dot(select, grad, 1, 0)
    my_columns = exact_dot(select, grad, 1, 1)
    rows_ref[...] = my_rows[:seqs]
    as_query = exact_dot(my_rows, docs, 1, 0)
    as_doc = exact_dot(my_columns, queries, 1, 0)
    unit_grad = (score_scale * jnp.where(tower == 0, as_query, as_doc))[:seqs]
    pooled = pooled_ref[...]
    inverse = lax.rsqrt(jnp.sum(pooled * pooled, axis=-1, keepdims=True) + epsilon)
    cubed = inverse * inverse * inverse
    pooled_grad[:seqs] = inverse * unit_grad - pooled * cubed * jnp.sum(unit_grad * pooled, axis=-1, keepdims=True)


def feed_back_kernel(
    lengths, prefixes, wo, gain_f, widen, narrow, gain_z, mixed_ref, hidden_ref, output_ref, pooled_ref,
    units_ref, positives_ref,
    branch_ref, pre_ref, attn_ref, context_ref, mixed_grad, gains_ref, loss_ref, rows_ref, feed_grad, pooled_grad,
):
    seq = pl.program_id(0)
    slot_len, width = mixed_ref.shape
    length = lengths[seq]

    def clear():
        gains_ref[...] = jnp.zeros_like(gains_ref)
        contrast(units_ref, pooled_ref, positives_ref, loss_ref, rows_ref, pooled_grad)

    pl.when(seq == 0)(clear)
    places = lax.broadcasted_iota(jnp.int32, (slot_len, 1), 0)
    mask = jnp.logical_and(places >= prefixes[seq], places < length).astype(jnp.float32)
    count = (length - prefixes[seq]).astype(jnp.float32)
    final_grad = (mask / count) * pooled_grad[pl.ds(seq, 1), :]
    output_grad, final_gain = norm_back(output_ref[...], gain_z[...][None], final_grad)
    gains_ref[2:3] += final_gain
    mixed_grad[...] = output_grad
    branch_ref[...] = output_grad.astype(jnp.bfloat16)
    feed_grad[...] = jnp.zeros_like(feed_grad)

    def feed(index, carry):
        span = pl.ds(pl.multiple_of(index * 2 * width, 128), 2 * width)
        hidden_grad = dot_across(branch_ref[...], narrow[span, :])
        pre_grad = jnp.where(hidden_ref[:, span] > 0, hidden_grad, 0.0).astype(jnp.bfloat16)
        pre_ref[:, span] = pre_grad
        feed_grad[...] += dot_across(pre_grad, widen[:, span])
        return carry

    lax.fori_loop(0, widen.shape[1] // (2 * width), feed, 0, unroll=True)
    by_mixed, feed_gain = norm_back(mixed_ref[...], gain_f[...][None], feed_grad[...])
    gains_ref[1:2] += feed_gain
    total_grad = mixed_grad[...] + by_mixed
    mixed_grad[...] = total_grad
    attn_low = total_grad.astype(jnp.bfloat16)
    attn_ref[...] = attn_low
    context_ref[...] = dot_across(attn_low, wo[...]).astype(jnp.bfloat16)


def whole(shape):
    return pl.BlockSpec(shape, lambda n, *_: (0,) * len(shape), pipeline_mode=pl.Buffered(1))


def run_feed_back(lengths, prefixes, gains, weights, mixed, hidden, output, pooled, units, positives):
    rows, width = mixed.shape
    seqs = lengths.shape[0]
    slot_len = rows // seqs
    wo, widen, narrow = weights
    ff = widen.shape[1]
    count = positives.shape[0]

    def block(columns):
        return pl.BlockSpec((slot_len, columns), lambda n, *_: (n, 0))

    def shape(columns, kind):
        return jax.ShapeDtypeStruct((rows, columns), kind)

    low, full = jnp.bfloat16, jnp.float32
    return pl.pallas_call(
        feed_back_kernel,
        grid_spec=pltpu.PrefetchScalarGridSpec(
            num_scalar_prefetch=2,
            grid=(seqs,),
            in_specs=[
                whole((width, width)), whole((width,)), whole((width, ff)), whole((ff, width)), whole((width,)),
                block(width), block(ff), block(width),
                whole(pooled.shape), whole(units.shape), whole((count, 1)),
            ],
            out_specs=[
                block(width), block(ff), block(width), block(width), block(width),
                pl.BlockSpec((8, width), lambda n, *_: (0, 0)),
                pl.BlockSpec((1, 1), lambda n, *_: (0, 0)),
                pl.BlockSpec((seqs, count), lambda n, *_: (0, 0)),
            ],
            scratch_shapes=[pltpu.VMEM((slot_len, width), jnp.float32), pltpu.VMEM((8, width), jnp.float32)],
        ),
        out_shape=(
            shape(width, low), shape(ff, low), shape(width, low), shape(width, low), shape(width, full),
            jax.ShapeDtypeStruct((8, width), full),
            jax.ShapeDtypeStruct((1, 1), full),
            jax.ShapeDtypeStruct((seqs, count), full),
        ),
        compiler_params=pltpu.CompilerParams(vmem_limit_bytes=60000000),
        name="feed_back",
    )(
        lengths, prefixes, wo, gains[0], widen, narrow, gains[1], mixed, hidden, output, pooled, units,
        positives[:, None],
    )


def local(
    batch_size,
    tokens,
    lengths,
    prefixes,
    positives,
    gain_attention,
    query_weight,
    key_weight,
    value_weight,
    output_weight,
    bucket_bias,
    gain_feedforward,
    widen_weight,
    narrow_weight,
    gain_final,
):
    seqs = lengths.shape[1]
    width = tokens.shape[2]
    gains = (gain_attention, gain_feedforward, gain_final)
    weights = (query_weight, key_weight, value_weight, output_weight, widen_weight, narrow_weight)
    normed, query, key, value, totals, context, mixed, ffn_in, hidden, output, pooled, units = run_forward(
        batch_size, 0, tokens[0], lengths[0], prefixes[0], bucket_bias.T, gains, weights
    )
    branch, pre, attn, context_grad, mixed_grad, feed_gains, loss, my_rows = run_feed_back(
        lengths[0], prefixes[0], gains[1:], weights[3:], mixed, hidden, output, pooled, units, positives
    )
    streamed = (
        hidden, ffn_in, context, normed, branch, pre, attn, query, key, value, context_grad, tokens[0], mixed_grad
    )
    resident = (totals, bucket_bias.T, gain_attention, *weights[:3])
    sum_narrow, sum_widen, squares, token_gradient, sums = sum_weights(batch_size, 1, lengths[0], bucket_bias.T, streamed, feed_gains, resident)
    sum_bucket = sums[8:, : bucket_bias.shape[1]]
    sum_output, sum_query, sum_key, sum_value = (squares[n * width : (n + 1) * width] for n in range(4))
    return (
        loss[0, 0],
        my_rows,
        token_gradient[None],
        sums[0],
        sum_query,
        sum_key,
        sum_value,
        sum_output,
        sum_bucket,
        sums[1],
        sum_widen,
        sum_narrow,
        sums[2],
    )


def solution(mesh):
    placed = (
        P("tower", "batch", None),
        P("tower", "batch"),
        P("tower", "batch"),
        P(),
        P(),
        P(),
        P(),
        P(),
        P(),
        P(),
        P(),
        P(),
        P(),
        P(),
    )
    return jax.shard_map(
        functools.partial(local, mesh.shape["batch"]),
        mesh=mesh,
        in_specs=placed,
        out_specs=(
            P(),
            P("batch", None),
            P("tower", "batch", None),
            P(),
            P(),
            P(),
            P(),
            P(),
            P(),
            P(),
            P(),
            P(),
            P(),
        ),
        check_vma=False,
    )
```

```python
import functools

import jax
import jax.numpy as jnp
from jax import lax
from jax.experimental import pallas as pl
from jax.experimental.pallas import tpu as pltpu
from jax.sharding import PartitionSpec as P

epsilon = 1e-06
masked_score = -1000000000.0
score_scale = 100.0
far_steps = (12, 16, 23, 32, 46, 64, 91)
highest = lax.Precision.HIGHEST


MESH = pl.DeviceIdType.MESH
job_rows = 384
unit_rows = 128


def batch_dims(size):
    sizes = {16: (2, 2, 4), 64: (4, 4, 4)}[size]
    strides = (1, sizes[0], sizes[0] * sizes[1])
    return dict(zip("xyz", zip(strides, sizes)))


def place():
    return lax.axis_index("tower"), lax.axis_index("batch")


def gather_peer(groups, step):
    tower, batch = place()
    return tower, lax.rem(batch + step, groups)


def greet_all(groups):
    tower, batch = place()
    barrier = pltpu.get_barrier_semaphore()

    def greet(step, carry):
        pl.semaphore_signal(barrier, 1, device_id=gather_peer(groups, step), device_id_type=MESH)
        return carry

    lax.fori_loop(1, groups, greet, 0)
    pl.semaphore_signal(barrier, 1, device_id=(1 - tower, batch), device_id_type=MESH)


def gather_units(groups, block_ref, out_ref, slots, send_sem, recv_sem, mate_sem):
    tower, batch = place()
    slots[tower, batch] = block_ref[...]
    pl.semaphore_wait(pltpu.get_barrier_semaphore(), groups)

    def copy(step, owner):
        return pltpu.make_async_remote_copy(
            src_ref=block_ref,
            dst_ref=slots.at[tower, owner],
            send_sem=send_sem.at[step],
            recv_sem=recv_sem.at[owner],
            device_id=gather_peer(groups, step),
            device_id_type=MESH,
        )

    def begin(step, carry):
        copy(step, batch).start()
        return carry

    def finish(step, carry):
        copy(step, batch).wait_send()
        copy(step, gather_peer(groups, step)[1]).wait_recv()
        return carry

    lax.fori_loop(1, groups, begin, 0)
    lax.fori_loop(1, groups, finish, 0)
    side = pltpu.make_async_remote_copy(
        src_ref=slots.at[tower],
        dst_ref=slots.at[tower],
        send_sem=mate_sem.at[0],
        recv_sem=mate_sem.at[1],
        device_id=(1 - tower, batch),
        device_id_type=MESH,
    )
    side.start()
    side.wait()
    out_ref[...] = slots[...]


def both(first, second):
    if first is None:
        return second
    if second is None:
        return first
    return jnp.logical_and(first, second)


def guarded(condition, action):
    if condition is None:
        action()
    else:
        pl.when(condition)(action)


def hands_back(order, dims, index):
    return index == 0 and all(dims[name][1] == 2 for name in order[1:])


def plan_unit(order, dims, coords, batch, rows):
    add, spread = [], []
    start, active, column = 0, None, None
    for index, name in enumerate(order):
        stride, size = dims[name]
        coord = coords[name]
        if size == 4:
            low_side = coord < 2
            inner = jnp.logical_or(coord == 1, coord == 2)
            outer = jnp.logical_not(inner)
            mate = batch + stride * (1 - 2 * lax.rem(coord, 2))
            share = hands_back(order, dims, index)
            sent = rows * 3 // 4 if share else rows
            first = start + jnp.where(low_side, rows // 4, 0) if share else start
            add.append(
                dict(rows=sent, send=first, keep=first, peer=mate, one_way=True,
                     sends=both(active, outer), receives=both(active, inner)))
            spread.append(
                dict(rows=sent, send=first, peer=mate,
                     sends=both(active, inner), receives=both(active, outer)))
            active_inner = both(active, inner)
            bit = coord // 2
            half = rows // 2
            kept = start + bit * half
            other = batch + stride * (3 - 2 * coord)
            add.append(
                dict(rows=half, send=start + (1 - bit) * half, keep=kept, peer=other, one_way=False,
                     sends=active_inner, receives=active_inner))
            spread.append(dict(rows=half, send=kept, peer=other, sends=active_inner, receives=active_inner))
            if share:
                quarter = rows // 4
                last = start + jnp.where(low_side, 0, 3 * quarter)
                add.append(
                    dict(rows=quarter, send=last, keep=last, peer=mate, one_way=True,
                         sends=active_inner, receives=both(active, outer)))
                spread.append(
                    dict(rows=quarter, send=last, peer=mate,
                         sends=both(active, outer), receives=active_inner))
                start, rows = start + coord * quarter, quarter
            else:
                start, rows, active = kept, half, active_inner
            continue
        mate = batch + stride * (1 - 2 * coord)
        if rows > 8:
            rows = rows // 2
            kept = start + coord * rows
            add.append(
                dict(rows=rows, send=start + (1 - coord) * rows, keep=kept, peer=mate, one_way=False,
                     sends=active, receives=active))
            spread.append(dict(rows=rows, send=kept, peer=mate, sends=active, receives=active))
            start = kept
        else:
            add.append(
                dict(rows=rows, send=start, keep=start, peer=mate, one_way=False, sends=active, receives=active,
                     send_side=1 - coord, keep_side=coord))
            spread.append(
                dict(rows=rows, send=start, peer=mate, sends=active, receives=active, send_side=coord))
    return add, spread[::-1]


def plan_shapes(order, dims, rows):
    result = []
    for index, name in enumerate(order):
        if dims[name][1] == 4:
            share = hands_back(order, dims, index)
            result.append((rows * 3 // 4 if share else rows, 1, True))
            result.append((rows // 2, 1, False))
            if share:
                result.append((rows // 4, 1, True))
            rows = rows // 4 if share else rows // 2
        elif rows > 8:
            rows //= 2
            result.append((rows, 1, False))
        else:
            result.append((rows, 2, False))
    return result


def step_rings(shapes):
    steps = 2 + 2 * len(shapes)
    rings = [4] * steps
    for index, (_, _, single) in enumerate(shapes):
        if single:
            first, last = 1 + index, steps - 2 - index
            rings[last] = last - first + 4
    return rings


orders = ("xyz", "yxz", "zxy")


def sums_kernel(dims, jobs, *refs):
    (lengths, table, hidden, ffn_in, context, normed, branch, pre, attn, query, key, value, upstream) = refs[:13]
    (tokens, mixed_grad, small, totals, bias_ref, gain, wq, wk, wv) = refs[13:22]
    (narrow_out, widen_out, square_out, token_out, small_out) = refs[22:27]
    (left, right, part, acc, full, mate_in, small_own, small_in, heads_in, by_query, by_key, by_value) = refs[27:39]
    (near_ref, near_sums, far_sums, token_in, mixed_in, token_buffer) = refs[39:45]
    rest = refs[45:]
    half = unit_rows // 2
    shapes = [plan_shapes(order, dims, half) for order in orders]
    counts = [len(shape) for shape in shapes]
    inbox, where = [], 0
    for count in counts:
        inbox.append(rest[where : where + count])
        where += count
    load_sem, right_sem, send_sem, recv_sem, keep_sem, small_sem, heads_sem, token_sem, credit = rest[where:]
    tower, batch = place()
    steps = [2 + 2 * count for count in counts]
    longest = max(steps)
    slots = jobs + longest + 1
    rings = [step_rings(shape) for shape in shapes]
    coords = {name: lax.rem(batch // stride, size) for name, (stride, size) in dims.items()}
    plans = [plan_unit(order, dims, coords, batch, half) for order in orders]
    turned_dims = dict(dims, x=dims["y"], y=dims["x"])
    turned_coords = dict(coords, x=coords["y"], y=coords["x"])
    turned = plan_unit(orders[-1], turned_dims, turned_coords, batch, half)

    def pick(odd, first, second):
        if isinstance(first, int) and isinstance(second, int) and first == second or first is None:
            return first
        if isinstance(first, bool):
            return first
        if getattr(first, "dtype", None) == jnp.bool_:
            return jnp.logical_or(jnp.logical_and(odd, second), jnp.logical_and(jnp.logical_not(odd), first))
        return jnp.where(odd, second, first)

    def plan(unit, job):
        if unit < len(orders) - 1:
            return plans[unit]
        odd = lax.rem(job, 2) == 1
        return tuple(
            [{key: pick(odd, one[key], two[key]) for key in one} for one, two in zip(ones, twos)]
            for ones, twos in zip(plans[unit], turned)
        )

    held, spread_held = acc.shape[0], full.shape[0]
    width = narrow_out.shape[1]
    heads = table.shape[0]
    seqs = lengths.shape[0]
    slot_len = tokens.shape[0] // seqs
    pair = 2 * width // heads
    group = heads_in.shape[3]
    pairs = width // group
    tasks = seqs * pairs
    blocks = slot_len // tile

    barrier = pltpu.get_barrier_semaphore()
    mate = (1 - tower, batch)
    mates, turns = [mate], [mate]
    for stride, size in dims.values():
        coord = lax.rem(batch // stride, size)
        near_mate = (tower, batch + stride * (1 - 2 * lax.rem(coord, 2)))
        mates.append(near_mate)
        turns.append(near_mate)
        if size == 4:
            mates.append((tower, batch + stride * (3 - 2 * coord)))
            turns.append((tower, batch + stride * (2 - 4 * (coord // 2))))
            mates.append(turns[-1])
    for other in mates:
        pl.semaphore_signal(barrier, 1, device_id=other, device_id_type=MESH)

    per_narrow = hidden.shape[1] // job_rows
    per_side = width // job_rows
    sources = [(hidden, branch, per_narrow), (ffn_in, pre, per_narrow), (context, attn, per_side)]
    sources += [(normed, grads, per_side) for grads in (by_query, by_key, by_value)]

    def right_place(job):
        past = job - per_narrow
        group = jnp.where(past < 0, 0, 1 + past // per_side)
        fresh = jnp.where(past < 0, job == 0, lax.rem(past, per_side) == 0)
        return lax.rem(group, 2), fresh

    def left_copies(target, job, columns):
        quarter = target.shape[1] // 4
        return [
            pltpu.make_async_copy(
                columns(pl.ds(n * quarter, quarter)), target.at[lax.rem(job, 2), pl.ds(n * quarter, quarter)],
                load_sem.at[lax.rem(job, 2), n],
            )
            for n in range(4)
        ]

    def load(job):
        place_right, fresh = right_place(job)
        first = 0
        for index, (left_ref, right_ref, count) in enumerate(sources):
            local = job - first

            def go(local=local, left_ref=left_ref, right_ref=right_ref, index=index):
                block = lax.rem(local, per_side) if index == 1 else local
                span = pl.ds(pl.multiple_of(block * job_rows, 128), job_rows)
                for copy in left_copies(left, job, lambda rows: left_ref.at[rows, span]):
                    copy.start()

                def go_right():
                    block = local // per_side if index == 1 else 0
                    span = pl.ds(pl.multiple_of(block * width, 128), width)
                    pltpu.make_async_copy(
                        right_ref.at[:, span], right.at[place_right], right_sem.at[place_right]
                    ).start()

                pl.when(fresh)(go_right)

            pl.when(jnp.logical_and(local >= 0, local < count))(go)
            first += count

    def compute(job):
        slot = lax.rem(job, 2)
        place_right, fresh = right_place(job)
        for copy in left_copies(left, job, lambda rows: normed.at[rows, pl.ds(0, job_rows)]):
            copy.wait()
        pl.when(fresh)(
            lambda: pltpu.make_async_copy(attn, right.at[place_right], right_sem.at[place_right]).wait()
        )
        pl.when(job + 1 < jobs)(lambda: load(job + 1))
        part[lax.rem(job, 3)] = lax.dot_general(
            left[slot], right[place_right], (((0,), (0,)), ((), ())), preferred_element_type=jnp.float32
        )

    def side_columns(item, key):
        if key not in item:
            return slice(None)
        return pl.ds(pl.multiple_of(item[key] * (width // 2), 128), width // 2)

    def remote(unit, step, job):
        add, spread = plan(unit, job)
        turn = lax.rem(job, rings[unit][step])
        place_in = lax.rem(job, held)
        sems = dict(
            send_sem=send_sem.at[unit * longest + step, turn],
            recv_sem=recv_sem.at[unit * longest + step, turn],
            device_id_type=MESH,
        )
        base = unit * half
        if step == 0:
            src = part.at[lax.rem(job, 3), pl.ds(pl.multiple_of(unit * unit_rows + (1 - tower) * half, 8), half)]
            dst = mate_in.at[turn, pl.ds(base, half)]
            return pltpu.make_async_remote_copy(src, dst, device_id=(1 - tower, batch), **sems), None, None
        count = counts[unit]
        item = add[step - 1] if step <= count else spread[step - 1 - count]
        rows = pl.ds(pl.multiple_of(base + item["send"], 8), item["rows"])
        columns = side_columns(item, "send_side")
        if step <= count:
            src, dst = acc.at[place_in, rows, columns], inbox[unit][step - 1].at[turn]
        else:
            src = dst = full.at[lax.rem(job, spread_held), rows, columns]
        copy = pltpu.make_async_remote_copy(src, dst, device_id=(tower, item["peer"]), **sems)
        return copy, item["sends"], item["receives"]

    def place_sums(unit, job, action):
        src = full.at[lax.rem(job, spread_held), pl.ds(unit * half, half)]
        first = unit * unit_rows + tower * half

        def at(ref, row, *columns):
            return lambda: action(src, ref.at[(pl.ds(pl.multiple_of(row + first, 8), half), *columns)])

        past = job - per_narrow
        pl.when(past < 0)(at(narrow_out, job * job_rows))
        columns = pl.ds(pl.multiple_of(past // per_side * width, 128), width)
        pl.when(jnp.logical_and(past >= 0, past < per_narrow))(
            at(widen_out, lax.rem(past, per_side) * job_rows, columns)
        )
        pl.when(past >= per_narrow)(at(square_out, (past - per_narrow) * job_rows))

    def last_copy(unit, job, src, dst):
        turn = lax.rem(job, rings[unit][steps[unit] - 1])
        index = unit * longest + steps[unit] - 1
        return pltpu.make_async_remote_copy(
            src, dst, send_sem=send_sem.at[index, turn], recv_sem=recv_sem.at[index, turn],
            device_id=(1 - tower, batch), device_id_type=MESH,
        )

    def begin_last(unit, job):
        def both_ways(src, dst):
            last_copy(unit, job, src, dst).start()
            pltpu.make_async_copy(src, dst, keep_sem.at[unit, lax.rem(job, 2)]).start()

        place_sums(unit, job, both_ways)

    def finish_last(unit, job):
        src = full.at[lax.rem(job, spread_held), pl.ds(unit * half, half)]
        dst = narrow_out.at[pl.ds(0, half)]
        last_copy(unit, job, src, dst).wait()
        pltpu.make_async_copy(src, dst, keep_sem.at[unit, lax.rem(job, 2)]).wait()

    def one_way(unit, step):
        return 1 <= step <= counts[unit] and shapes[unit][step - 1][2]

    def finish(unit, step, job):
        copy, sends, receives = remote(unit, step, job)
        add, _ = plan(unit, job)
        base = unit * half
        guarded(sends, copy.wait_send)
        turn = lax.rem(job, rings[unit][step])
        place_in = lax.rem(job, held)

        def arrived():
            copy.wait_recv()
            if step == 0:
                own = pl.ds(pl.multiple_of(unit * unit_rows + tower * half, 8), half)
                acc[place_in, pl.ds(base, half)] = part[lax.rem(job, 3), own] + mate_in[turn, pl.ds(base, half)]
            elif step <= counts[unit]:
                item = add[step - 1]
                rows = pl.ds(pl.multiple_of(base + item["keep"], 8), item["rows"])
                columns = side_columns(item, "keep_side")
                total = acc[place_in, rows, columns] + inbox[unit][step - 1][turn]
                if step == counts[unit]:
                    full[lax.rem(job, spread_held), rows, columns] = total
                else:
                    acc[place_in, rows, columns] = total
                if one_way(unit, step):
                    pl.when(job + rings[unit][step] < jobs)(
                        lambda: pl.semaphore_signal(
                            credit.at[unit * longest + step], 1,
                            device_id=(tower, item["peer"]), device_id_type=MESH,
                        )
                    )

        guarded(receives, arrived)

    def advance(unit, step, job):
        if step == steps[unit]:
            finish_last(unit, job)
            return
        if step > 0:
            finish(unit, step - 1, job)
        if step == steps[unit] - 1:
            begin_last(unit, job)
            return
        copy, sends, _ = remote(unit, step, job)

        def begin():
            if one_way(unit, step):
                pl.when(job >= rings[unit][step])(
                    lambda: pl.semaphore_wait(credit.at[unit * longest + step], 1)
                )
            copy.start()

        guarded(sends, begin)

    def small_copy(turn):
        return pltpu.make_async_remote_copy(
            src_ref=small_own.at[turn],
            dst_ref=small_in.at[turn],
            send_sem=small_sem.at[0, turn],
            recv_sem=small_sem.at[1, turn],
            device_id=turns[turn],
            device_id_type=MESH,
        )

    def small_turn(turn):
        if turn > 0:
            small_copy(turn - 1).wait()
            total = small_own[turn - 1] + small_in[turn - 1]
            if turn == len(turns):
                small_out[0:8] = total[0:8]
                small_out[8:, 0 : table.shape[1]] = exact_dot(total[8:24, : 4 * tile], offset_onehot(table.shape[1]), 1, 1)
            else:
                small_own[turn] = total
        if turn < len(turns):
            small_copy(turn).start()

    def heads_load(task, begin):
        rows = pl.ds(pl.multiple_of(task // pairs * slot_len, slot_len), slot_len)
        columns = pl.ds(pl.multiple_of(lax.rem(task, pairs) * group, group), group)
        slot = lax.rem(task, 2)
        for index, ref in enumerate((query, key, value, upstream)):
            copy = pltpu.make_async_copy(
                ref.at[rows, columns], heads_in.at[slot, index], heads_sem.at[slot, index]
            )
            copy.start() if begin else copy.wait()

    places = lax.broadcasted_iota(jnp.int32, (slot_len, 1), 0)
    lanes = lax.broadcasted_iota(jnp.int32, (1, pair), 1)

    def attend(task, carry):
        seq, index = task // pairs, lax.rem(task, pairs)
        slot = lax.rem(task, 2)
        heads_load(task, False)
        pl.when(task + 1 < tasks)(lambda: heads_load(task + 1, True))
        for inside in range(group // pair):
            attend_pair(seq, index * (group // pair) + inside, slot, inside)
        return carry

    def attend_pair(seq, index, slot, inside):
        span = slice(inside * pair, (inside + 1) * pair)
        queries, keys, values, upper = (heads_in[slot, n, :, span] for n in range(4))
        length = lengths[seq]
        keys_across = keys.T
        grads_out = [None] * 2
        query_rows = []
        for side in range(2):
            head = 2 * index + side
            mine = (lanes // (pair // 2) == side).astype(jnp.bfloat16)
            my_queries, my_upper = queries * mine, upper * mine
            raw = dot_across(keys, my_queries)
            soft_grad = dot_across(values, my_upper)
            line = totals[seq, pl.ds(head, 1), :]
            soft_columns, grad_columns = [], []
            near_total = [None] * 3
            far_total = [None] * 2
            for column in range(blocks):
                columns = slice(column * tile, (column + 1) * tile)
                scores = []
                for block in range(blocks):
                    rows = slice(block * tile, (block + 1) * tile)
                    bias = bias_tile(near_ref, head, block, column, *far_bias(table, head))
                    scores.append(jnp.where(places[rows] < length, raw[rows, columns] + bias, masked_score))
                soft = jnp.exp(jnp.concatenate(scores, axis=0) - line[:, columns])
                soft_columns.append(soft.astype(jnp.bfloat16))
                by_soft = soft_grad[:, columns]
                grads = soft * (by_soft - jnp.sum(soft * by_soft, axis=0, keepdims=True))
                grad_columns.append(grads.astype(jnp.bfloat16))
                for block in range(blocks):
                    piece = grads[block * tile : (block + 1) * tile]
                    ahead = block - column
                    group, spot = (near_total, 1 - ahead) if abs(ahead) <= 1 else (far_total, int(ahead > 0))
                    group[spot] = piece if group[spot] is None else group[spot] + piece
            for spot in range(3):
                if near_total[spot] is not None:
                    near_sums[head, :, spot * tile : (spot + 1) * tile] += near_total[spot]
            for spot in range(2):
                if far_total[spot] is not None:
                    far_sums[spot, pl.ds(head, 1), :] += jnp.sum(far_total[spot], axis=0, keepdims=True)
            soft_low = jnp.concatenate(soft_columns, axis=1)
            grads_low = jnp.concatenate(grad_columns, axis=1)
            half_rows = slice(side * (pair // 2), (side + 1) * (pair // 2))
            query_rows.append(low_dot(keys_across[half_rows], grads_low).astype(jnp.bfloat16))
            pieces = (low_dot(grads_low, my_queries), low_dot(soft_low, my_upper))
            grads_out = [new if old is None else old + new for old, new in zip(grads_out, pieces)]
        rows = pl.ds(pl.multiple_of(seq * slot_len, slot_len), slot_len)
        columns = pl.ds(pl.multiple_of(index * pair, pair), pair)
        by_query[rows, columns] = jnp.concatenate(query_rows, axis=0).T
        for ref, grads in zip((by_key, by_value), grads_out):
            ref[rows, columns] = grads.astype(jnp.bfloat16)

    def token_load(seq, begin):
        rows = pl.ds(pl.multiple_of(seq * slot_len, slot_len), slot_len)
        for index, (ref, target) in enumerate(((tokens, token_in), (mixed_grad, mixed_in))):
            copy = pltpu.make_async_copy(ref.at[rows], target, token_sem.at[index])
            copy.start() if begin else copy.wait()

    def token_store(seq):
        rows = pl.ds(pl.multiple_of(seq * slot_len, slot_len), slot_len)
        return pltpu.make_async_copy(token_buffer, token_out.at[rows], token_sem.at[2])

    def token_task(seq):
        rows = pl.ds(pl.multiple_of(seq * slot_len, slot_len), slot_len)
        token_load(seq, False)
        normed_grad = dot_across(by_query[rows, :], wq[...]) + dot_across(by_key[rows, :], wk[...])
        normed_grad += dot_across(by_value[rows, :], wv[...])
        by_tokens, token_gain = norm_back(token_in[...].astype(jnp.float32), gain[...][None], normed_grad)
        small_own[0, 0:1] += token_gain
        pl.when(seq > 0)(lambda: token_store(seq - 1).wait())
        token_buffer[...] = (mixed_in[...] + by_tokens).astype(jnp.bfloat16)
        token_store(seq).start()
        pl.when(seq + 1 < seqs)(lambda: token_load(seq + 1, True))

    def close():
        token_store(seqs - 1).wait()
        small_own[0, 8:24, :] = jnp.zeros((16, width), jnp.float32)
        for head in range(heads):
            turned = jnp.concatenate([near_sums[head], jnp.zeros((tile, tile), jnp.float32)], axis=1)
            count = tile // 2
            while count:
                upper = turned[count : 2 * count]
                turned = turned[:count] + pltpu.roll(upper, 4 * tile - count, 1)
                count //= 2
            small_own[0, 8 + head : 9 + head, : 4 * tile] = turned
        small_own[0, 8:24, 2 * tile : 3 * tile] += far_sums[0]
        small_own[0, 8:24, 3 * tile : 4 * tile] += far_sums[1]

    load(0)
    heads_load(0, True)
    token_load(0, True)
    small_own[0, 0:8, :] = small[...]
    compute(jnp.int32(0))
    pl.semaphore_wait(barrier, len(mates))

    last_attend = jobs - 3 * (width // job_rows) - 1
    first_token = last_attend + 1
    first_attend = 5
    first_small = slots - 1 - len(turns)

    def prepare():
        spread_bias(bias_ref, near_ref, heads)
        near_sums[...] = jnp.zeros_like(near_sums)
        far_sums[...] = jnp.zeros_like(far_sums)

    def products(time):
        pl.when(time < jobs)(functools.partial(compute, time))
        pl.when(time == 2)(prepare)

    def attention(time):
        past = jnp.maximum(time - first_attend, 0)
        span = last_attend - first_attend
        begin = jnp.minimum(past * tasks // span, tasks)
        end = jnp.where(time < first_attend, 0, jnp.minimum((past + 1) * tasks // span, tasks))
        lax.fori_loop(begin, end, attend, 0)

    def token_part(time):
        seq = time - first_token
        pl.when(jnp.logical_and(seq >= 0, seq < seqs))(functools.partial(token_task, seq))
        pl.when(time == first_token + seqs)(close)
        for turn in range(len(turns) + 1):
            pl.when(time == first_small + turn)(functools.partial(small_turn, turn))

    def slot(time, carry):
        for unit, work in ((2, products), (0, attention), (1, token_part)):
            for step in range(steps[unit] + 1):
                job = time - 1 - step
                pl.when(jnp.logical_and(job >= 0, job < jobs))(functools.partial(advance, unit, step, job))
            work(time)
        return carry

    lax.fori_loop(1, slots, slot, 0)


def sum_weights(batch_size, collective, lengths, bucket_bias, streamed, small, resident):
    hidden, normed = streamed[0], streamed[3]
    tokens, width = normed.shape
    seqs = lengths.shape[0]
    heads = bucket_bias.shape[0]
    slot_len = tokens // seqs
    pair = 2 * width // heads
    total = 2 * hidden.shape[1] + 4 * width
    jobs = total // job_rows
    dims = batch_dims(batch_size)
    half = unit_rows // 2
    shapes = [plan_shapes(order, dims, half) for order in orders]
    rings = [step_rings(shape) for shape in shapes]
    inboxes = [
        pltpu.VMEM((rings[unit][1 + index], rows, width // parts), jnp.float32)
        for unit, shape in enumerate(shapes)
        for index, (rows, parts, _) in enumerate(shape)
    ]
    steps = max(len(ring) for ring in rings)
    longest = max(max(ring) for ring in rings)
    turns = 1 + sum(size // 2 for _, size in dims.values())
    lines = 24
    low, full = jnp.bfloat16, jnp.float32
    in_vmem = pl.BlockSpec(memory_space=pltpu.VMEM)
    in_smem = pl.BlockSpec(memory_space=pltpu.SMEM)
    anywhere = pl.BlockSpec(memory_space=pl.ANY)
    return pl.pallas_call(
        functools.partial(sums_kernel, dims, jobs),
        out_shape=(
            jax.ShapeDtypeStruct((hidden.shape[1], width), full),
            jax.ShapeDtypeStruct((width, hidden.shape[1]), full),
            jax.ShapeDtypeStruct((4 * width, width), full),
            jax.ShapeDtypeStruct((tokens, width), low),
            jax.ShapeDtypeStruct((24, width), full),
        ),
        in_specs=[in_smem] * 2 + [anywhere] * len(streamed) + [in_vmem] * (1 + len(resident)),
        out_specs=(anywhere, anywhere, anywhere, anywhere, in_vmem),
        scratch_shapes=[
            pltpu.VMEM((2, tokens, job_rows), low),
            pltpu.VMEM((2, tokens, width), low),
            pltpu.VMEM((3, job_rows, width), full),
            pltpu.VMEM((steps // 2, 3 * half, width), full),
            pltpu.VMEM((steps, 3 * half, width), full),
            pltpu.VMEM((4, 3 * half, width), full),
            pltpu.VMEM((turns, lines, width), full),
            pltpu.VMEM((turns, lines, width), full),
            pltpu.VMEM((2, 4, slot_len, 1 * pair), low),
            pltpu.VMEM((tokens, width), low),
            pltpu.VMEM((tokens, width), low),
            pltpu.VMEM((tokens, width), low),
            pltpu.VMEM((heads, tile, near), full),
            pltpu.VMEM((heads, tile, near), full),
            pltpu.VMEM((2, 16, tile), full),
            pltpu.VMEM((slot_len, width), low),
            pltpu.VMEM((slot_len, width), full),
            pltpu.VMEM((slot_len, width), low),
            *inboxes,
            pltpu.SemaphoreType.DMA((2, 4)),
            pltpu.SemaphoreType.DMA((2,)),
            pltpu.SemaphoreType.DMA((3 * steps, longest)),
            pltpu.SemaphoreType.DMA((3 * steps, longest)),
            pltpu.SemaphoreType.DMA((3, 2)),
            pltpu.SemaphoreType.DMA((2, turns)),
            pltpu.SemaphoreType.DMA((2, 4)),
            pltpu.SemaphoreType.DMA((3,)),
            pltpu.SemaphoreType.REGULAR((3 * steps,)),
        ],
        compiler_params=pltpu.CompilerParams(
            collective_id=collective, has_side_effects=True, vmem_limit_bytes=66500000
        ),
        name="sum_weights",
    )(lengths, bucket_bias, *streamed, small, *resident)


tile = 128
near = 3 * tile


def offset_onehot(buckets):
    spots = lax.broadcasted_iota(jnp.int32, (buckets, 4 * tile), 1)
    labels = lax.broadcasted_iota(jnp.int32, (buckets, 4 * tile), 0)
    offset = tile - jnp.where(spots >= near, spots - 4 * tile, spots)
    spread = jnp.abs(offset)
    far_bucket = 8 + sum(((spread >= step).astype(jnp.int32) for step in far_steps))
    bucket = jnp.where(spread < 8, spread, far_bucket) + jnp.where(offset > 0, buckets // 2, 0)
    return (bucket == labels).astype(jnp.float32)


def spread_bias(bias_ref, near_ref, heads):
    lines = exact_dot(bias_ref[...], offset_onehot(bias_ref.shape[1]), 1, 0)
    for head in range(heads):
        line = jnp.broadcast_to(lines[head : head + 1, :], (tile, 4 * tile))
        near_ref[head] = pltpu.roll(line, 0, 1, stride=1, stride_axis=0)[:, :near]


def far_bias(table, head):
    buckets = table.shape[1]
    return table[head, buckets // 2 - 1], table[head, buckets - 1]


def bias_tile(near_ref, head, row_block, column_block, low_far, high_far):
    ahead = row_block - column_block
    if abs(ahead) <= 1:
        spot = 1 - ahead
        return near_ref[head, :, spot * tile : (spot + 1) * tile]
    return jnp.full((tile, tile), high_far if ahead > 0 else low_far, jnp.float32)


def unit_scale(values):
    return lax.rsqrt(jnp.mean(values * values, axis=-1, keepdims=True) + epsilon)


def low_dot(left, right):
    return jnp.dot(left, right, preferred_element_type=jnp.float32)


def dot_across(left, right):
    return lax.dot_general(left, right, (((1,), (1,)), ((), ())), preferred_element_type=jnp.float32)


def forward_kernel(
    groups, lengths, prefixes, table, x_ref, bias_ref, gain_a, wq, wk, wv, wo, gain_f, widen_far, narrow_far, gain_z,
    normed_ref, q_ref, k_ref, v_ref, lse_ref, context_ref, mixed_ref, ffn_ref, hidden_ref, output_ref, pooled_ref, units_ref,
    near_ref, widen, narrow, weight_sem, slots, block_ref, send_sem, recv_sem, mate_sem,
):
    seq = pl.program_id(0)
    heads = table.shape[0]
    slot_len, width = x_ref.shape
    blocks = slot_len // tile
    pair = 2 * width // heads
    length = lengths[seq]
    fetches = [
        pltpu.make_async_copy(widen_far, widen, weight_sem.at[0]),
        pltpu.make_async_copy(narrow_far, narrow, weight_sem.at[1]),
    ]

    def first():
        greet_all(groups)
        for fetch in fetches:
            fetch.start()
        spread_bias(bias_ref, near_ref, heads)

    pl.when(seq == 0)(first)
    tokens = x_ref[...].astype(jnp.float32)
    normed = (tokens * unit_scale(tokens) * gain_a[...][None]).astype(jnp.bfloat16)
    normed_ref[...] = normed
    q_ref[...] = low_dot(normed, wq[...]).astype(jnp.bfloat16)
    k_ref[...] = low_dot(normed, wk[...]).astype(jnp.bfloat16)
    v_ref[...] = low_dot(normed, wv[...]).astype(jnp.bfloat16)
    lanes = lax.broadcasted_iota(jnp.int32, (1, pair), 1)
    places = lax.broadcasted_iota(jnp.int32, (slot_len, 1), 0)

    def attend(index, carry):
        span = pl.ds(pl.multiple_of(index * pair, pair), pair)
        keys = k_ref[:, span]
        queries = q_ref[:, span]
        values_across = v_ref[:, span].T
        pieces = []
        for side in range(2):
            head = 2 * index + side
            mine = (lanes // (pair // 2) == side).astype(jnp.bfloat16)
            raw = dot_across(keys, queries * mine)
            soft_columns, lines = [], []
            for column in range(blocks):
                columns = slice(column * tile, (column + 1) * tile)
                scores = []
                for block in range(blocks):
                    rows = slice(block * tile, (block + 1) * tile)
                    bias = bias_tile(near_ref, head, block, column, *far_bias(table, head))
                    scores.append(jnp.where(places[rows] < length, raw[rows, columns] + bias, masked_score))
                scores = jnp.concatenate(scores, axis=0)
                peak = jnp.max(scores, axis=0, keepdims=True)
                raised = jnp.exp(scores - peak)
                total = jnp.sum(raised, axis=0, keepdims=True)
                soft_columns.append((raised * (1.0 / total)).astype(jnp.bfloat16))
                lines.append(peak + jnp.log(total))
            lse_ref[0, pl.ds(head, 1), :] = jnp.concatenate(lines, axis=1)
            soft_low = jnp.concatenate(soft_columns, axis=1)
            rows = slice(side * (pair // 2), (side + 1) * (pair // 2))
            pieces.append(low_dot(values_across[rows], soft_low).astype(jnp.bfloat16))
        context_ref[:, span] = jnp.concatenate(pieces, axis=0).T
        return carry

    lax.fori_loop(0, heads // 2, attend, 0, unroll=True)
    mixed = tokens + low_dot(context_ref[...], wo[...])
    mixed_ref[...] = mixed
    ffn_in = (mixed * unit_scale(mixed) * gain_f[...][None]).astype(jnp.bfloat16)
    ffn_ref[...] = ffn_in
    output_ref[...] = mixed
    pl.when(seq == 0)(lambda: [fetch.wait() for fetch in fetches] and None)

    def feed(index, carry):
        span = pl.ds(pl.multiple_of(index * width, 128), width)
        pre_act = low_dot(ffn_ref[...], widen[:, span])
        hidden = jnp.where(pre_act > 0, pre_act, 0.0).astype(jnp.bfloat16)
        hidden_ref[:, span] = hidden
        output_ref[...] += low_dot(hidden, narrow[span, :])
        return carry

    lax.fori_loop(0, widen.shape[1] // width, feed, 0, unroll=True)
    output = output_ref[...]
    mask = jnp.logical_and(places >= prefixes[seq], places < length).astype(jnp.float32)
    count = (length - prefixes[seq]).astype(jnp.float32)
    final = output * unit_scale(output) * gain_z[...][None]
    pooled_ref[pl.ds(seq, 1), :] = jnp.sum(final * (mask / count), axis=0, keepdims=True)

    def last():
        pooled = pooled_ref[...]
        block_ref[...] = pooled * lax.rsqrt(jnp.sum(pooled * pooled, axis=-1, keepdims=True) + epsilon)
        gather_units(groups, block_ref, units_ref, slots, send_sem, recv_sem, mate_sem)

    pl.when(seq == pl.num_programs(0) - 1)(last)


def run_forward(groups, collective, tokens, lengths, prefixes, bucket_bias, gains, weights):
    rows, width = tokens.shape
    seqs = lengths.shape[0]
    slot_len = rows // seqs
    heads = bucket_bias.shape[0]
    wq, wk, wv, wo, widen, narrow = weights
    gain_a, gain_f, gain_z = gains
    ff = widen.shape[1]
    units = (2, groups, seqs, width)

    def whole(shape):
        return pl.BlockSpec(shape, lambda n, *_: (0,) * len(shape), pipeline_mode=pl.Buffered(1))

    def block(columns):
        return pl.BlockSpec((slot_len, columns), lambda n, *_: (n, 0))

    square = whole((width, width))
    line = whole((width,))
    low, full = jnp.bfloat16, jnp.float32

    def shape(columns, kind):
        return jax.ShapeDtypeStruct((rows, columns), kind)

    return pl.pallas_call(
        functools.partial(forward_kernel, groups),
        grid_spec=pltpu.PrefetchScalarGridSpec(
            num_scalar_prefetch=3,
            grid=(seqs,),
            in_specs=[
                block(width), whole(bucket_bias.shape), line, square, square, square, square,
                line, pl.BlockSpec(memory_space=pl.ANY), pl.BlockSpec(memory_space=pl.ANY), line,
            ],
            out_specs=[
                block(width), block(width), block(width), block(width),
                pl.BlockSpec((1, 16, slot_len), lambda n, *_: (n, 0, 0)),
                block(width), block(width), block(width), block(ff), block(width),
                pl.BlockSpec((seqs, width), lambda n, *_: (0, 0)),
                pl.BlockSpec(units, lambda n, *_: (0, 0, 0, 0)),
            ],
            scratch_shapes=[
                pltpu.VMEM((heads, tile, near), jnp.float32),
                pltpu.VMEM((width, ff), low),
                pltpu.VMEM((ff, width), low),
                pltpu.SemaphoreType.DMA((2,)),
                pltpu.VMEM(units, full),
                pltpu.VMEM((seqs, width), full),
                pltpu.SemaphoreType.DMA((groups,)),
                pltpu.SemaphoreType.DMA((groups,)),
                pltpu.SemaphoreType.DMA((2,)),
            ],
        ),
        out_shape=(
            shape(width, low), shape(width, low), shape(width, low), shape(width, low),
            jax.ShapeDtypeStruct((seqs, 16, slot_len), full),
            shape(width, low), shape(width, full), shape(width, low), shape(ff, low), shape(width, full),
            jax.ShapeDtypeStruct((seqs, width), full),
            jax.ShapeDtypeStruct(units, full),
        ),
        compiler_params=pltpu.CompilerParams(
            collective_id=collective, has_side_effects=True, vmem_limit_bytes=60000000
        ),
        name="forward",
    )(lengths, prefixes, bucket_bias, tokens, bucket_bias, gain_a, wq, wk, wv, wo, gain_f, widen, narrow, gain_z)


def norm_back(values, gain, upstream):
    inverse = unit_scale(values)
    scaled = upstream * gain
    inner = jnp.mean(scaled * values, axis=-1, keepdims=True)
    by_values = inverse * scaled - values * (inverse * inverse * inverse) * inner
    return by_values, jnp.sum(upstream * values * inverse, axis=0, keepdims=True)


def exact_dot(left, right, left_dim, right_dim):
    return lax.dot_general(
        left, right, (((left_dim,), (right_dim,)), ((), ())),
        precision=highest, preferred_element_type=jnp.float32,
    )


def contrast(units_ref, pooled_ref, positives_ref, loss_ref, rows_ref, pooled_grad):
    tower, batch = place()
    _, groups, seqs, width = units_ref.shape
    count = groups * seqs
    queries = units_ref[0].reshape(count, width)
    docs = units_ref[1].reshape(count, width)
    scores = score_scale * exact_dot(queries, docs, 1, 1)
    labels = lax.broadcasted_iota(jnp.int32, (count, count), 1)
    target = (positives_ref[...] == labels).astype(jnp.float32)
    row_peak = jnp.max(scores, axis=1, keepdims=True)
    row_raised = jnp.exp(scores - row_peak)
    row_sum = jnp.sum(row_raised, axis=1, keepdims=True)
    column_peak = jnp.max(scores, axis=0, keepdims=True)
    column_raised = jnp.exp(scores - column_peak)
    column_sum = jnp.sum(column_raised, axis=0, keepdims=True)
    loss = 0.5 * jnp.sum(row_peak + jnp.log(row_sum), axis=0, keepdims=True)
    loss += 0.5 * jnp.sum(column_peak + jnp.log(column_sum), axis=1, keepdims=True)
    loss_ref[...] = loss - jnp.sum(jnp.sum(target * scores, axis=1, keepdims=True), axis=0, keepdims=True)
    grad = 0.5 * row_raised / row_sum + 0.5 * column_raised / column_sum - target
    mine = lax.broadcasted_iota(jnp.int32, (8, count), 0) + batch * seqs
    spots = lax.broadcasted_iota(jnp.int32, (8, count), 1)
    select = (mine == spots).astype(jnp.float32)
    my_rows = exact_dot(select, grad, 1, 0)
    my_columns = exact_dot(select, grad, 1, 1)
    rows_ref[...] = my_rows[:seqs]
    as_query = exact_dot(my_rows, docs, 1, 0)
    as_doc = exact_dot(my_columns, queries, 1, 0)
    unit_grad = (score_scale * jnp.where(tower == 0, as_query, as_doc))[:seqs]
    pooled = pooled_ref[...]
    inverse = lax.rsqrt(jnp.sum(pooled * pooled, axis=-1, keepdims=True) + epsilon)
    cubed = inverse * inverse * inverse
    pooled_grad[:seqs] = inverse * unit_grad - pooled * cubed * jnp.sum(unit_grad * pooled, axis=-1, keepdims=True)


def feed_back_kernel(
    lengths, prefixes, wo, gain_f, widen, narrow, gain_z, mixed_ref, hidden_ref, output_ref, pooled_ref,
    units_ref, positives_ref,
    branch_ref, pre_ref, attn_ref, context_ref, mixed_grad, gains_ref, loss_ref, rows_ref, feed_grad, pooled_grad,
):
    seq = pl.program_id(0)
    slot_len, width = mixed_ref.shape
    length = lengths[seq]

    def clear():
        gains_ref[...] = jnp.zeros_like(gains_ref)
        contrast(units_ref, pooled_ref, positives_ref, loss_ref, rows_ref, pooled_grad)

    pl.when(seq == 0)(clear)
    places = lax.broadcasted_iota(jnp.int32, (slot_len, 1), 0)
    mask = jnp.logical_and(places >= prefixes[seq], places < length).astype(jnp.float32)
    count = (length - prefixes[seq]).astype(jnp.float32)
    final_grad = (mask / count) * pooled_grad[pl.ds(seq, 1), :]
    output_grad, final_gain = norm_back(output_ref[...], gain_z[...][None], final_grad)
    gains_ref[2:3] += final_gain
    mixed_grad[...] = output_grad
    branch_ref[...] = output_grad.astype(jnp.bfloat16)
    feed_grad[...] = jnp.zeros_like(feed_grad)

    def feed(index, carry):
        span = pl.ds(pl.multiple_of(index * 2 * width, 128), 2 * width)
        hidden_grad = dot_across(branch_ref[...], narrow[span, :])
        pre_grad = jnp.where(hidden_ref[:, span] > 0, hidden_grad, 0.0).astype(jnp.bfloat16)
        pre_ref[:, span] = pre_grad
        feed_grad[...] += dot_across(pre_grad, widen[:, span])
        return carry

    lax.fori_loop(0, widen.shape[1] // (2 * width), feed, 0, unroll=True)
    by_mixed, feed_gain = norm_back(mixed_ref[...], gain_f[...][None], feed_grad[...])
    gains_ref[1:2] += feed_gain
    total_grad = mixed_grad[...] + by_mixed
    mixed_grad[...] = total_grad
    attn_low = total_grad.astype(jnp.bfloat16)
    attn_ref[...] = attn_low
    context_ref[...] = dot_across(attn_low, wo[...]).astype(jnp.bfloat16)


def whole(shape):
    return pl.BlockSpec(shape, lambda n, *_: (0,) * len(shape), pipeline_mode=pl.Buffered(1))


def run_feed_back(lengths, prefixes, gains, weights, mixed, hidden, output, pooled, units, positives):
    rows, width = mixed.shape
    seqs = lengths.shape[0]
    slot_len = rows // seqs
    wo, widen, narrow = weights
    ff = widen.shape[1]
    count = positives.shape[0]

    def block(columns):
        return pl.BlockSpec((slot_len, columns), lambda n, *_: (n, 0))

    def shape(columns, kind):
        return jax.ShapeDtypeStruct((rows, columns), kind)

    low, full = jnp.bfloat16, jnp.float32
    return pl.pallas_call(
        feed_back_kernel,
        grid_spec=pltpu.PrefetchScalarGridSpec(
            num_scalar_prefetch=2,
            grid=(seqs,),
            in_specs=[
                whole((width, width)), whole((width,)), whole((width, ff)), whole((ff, width)), whole((width,)),
                block(width), block(ff), block(width),
                whole(pooled.shape), whole(units.shape), whole((count, 1)),
            ],
            out_specs=[
                block(width), block(ff), block(width), block(width), block(width),
                pl.BlockSpec((8, width), lambda n, *_: (0, 0)),
                pl.BlockSpec((1, 1), lambda n, *_: (0, 0)),
                pl.BlockSpec((seqs, count), lambda n, *_: (0, 0)),
            ],
            scratch_shapes=[pltpu.VMEM((slot_len, width), jnp.float32), pltpu.VMEM((8, width), jnp.float32)],
        ),
        out_shape=(
            shape(width, low), shape(ff, low), shape(width, low), shape(width, low), shape(width, full),
            jax.ShapeDtypeStruct((8, width), full),
            jax.ShapeDtypeStruct((1, 1), full),
            jax.ShapeDtypeStruct((seqs, count), full),
        ),
        compiler_params=pltpu.CompilerParams(vmem_limit_bytes=60000000),
        name="feed_back",
    )(
        lengths, prefixes, wo, gains[0], widen, narrow, gains[1], mixed, hidden, output, pooled, units,
        positives[:, None],
    )


def settle_kernel(count, sums, *refs):
    for source, target in zip(refs[:count], refs[count : 2 * count]):
        target[...] = source[...]
    *gains, bucket = refs[2 * count :]

    def small():
        for index, gain in enumerate(gains):
            gain[...] = sums[index, :]
        heads, buckets = bucket.shape
        bucket[...] = sums[8 : 8 + heads, 0:buckets]

    pl.when(pl.program_id(0) == 0)(small)


def settle(narrow, widen, squares, token, sums, table):
    width = widen.shape[0]
    steps = 8

    def rows(array, parts=1, first=0):
        block = array.shape[0] // parts // steps
        return pl.BlockSpec((block, array.shape[1]), lambda n: (first * steps + n, 0))

    square = jax.ShapeDtypeStruct((width, width), squares.dtype)
    return pl.pallas_call(
        functools.partial(settle_kernel, 7),
        grid=(steps,),
        in_specs=[
            pl.BlockSpec(sums.shape, lambda n: (0, 0)), rows(narrow), rows(widen), *(rows(squares, 4, n) for n in range(4)), rows(token),
        ],
        out_specs=[
            rows(narrow), rows(widen), *(rows(squares, 4) for n in range(4)), rows(token),
            *(pl.BlockSpec((width,), lambda n: (0,)) for _ in range(3)), pl.BlockSpec(table, lambda n: (0, 0)),
        ],
        out_shape=(
            jax.ShapeDtypeStruct(narrow.shape, narrow.dtype),
            jax.ShapeDtypeStruct(widen.shape, widen.dtype),
            square, square, square, square,
            jax.ShapeDtypeStruct(token.shape, token.dtype),
            *(jax.ShapeDtypeStruct((width,), sums.dtype) for _ in range(3)),
            jax.ShapeDtypeStruct(table, sums.dtype),
        ),
        compiler_params=pltpu.CompilerParams(vmem_limit_bytes=66500000),
        name="settle",
    )(sums, narrow, widen, squares, squares, squares, squares, token)


def local(
    batch_size,
    tokens,
    lengths,
    prefixes,
    positives,
    gain_attention,
    query_weight,
    key_weight,
    value_weight,
    output_weight,
    bucket_bias,
    gain_feedforward,
    widen_weight,
    narrow_weight,
    gain_final,
):
    seqs = lengths.shape[1]
    width = tokens.shape[2]
    gains = (gain_attention, gain_feedforward, gain_final)
    weights = (query_weight, key_weight, value_weight, output_weight, widen_weight, narrow_weight)
    normed, query, key, value, totals, context, mixed, ffn_in, hidden, output, pooled, units = run_forward(
        batch_size, 0, tokens[0], lengths[0], prefixes[0], bucket_bias.T, gains, weights
    )
    branch, pre, attn, context_grad, mixed_grad, feed_gains, loss, my_rows = run_feed_back(
        lengths[0], prefixes[0], gains[1:], weights[3:], mixed, hidden, output, pooled, units, positives
    )
    streamed = (
        hidden, ffn_in, context, normed, branch, pre, attn, query, key, value, context_grad, tokens[0], mixed_grad
    )
    resident = (totals, bucket_bias.T, gain_attention, *weights[:3])
    sum_narrow, sum_widen, squares, token_gradient, sums = sum_weights(batch_size, 1, lengths[0], bucket_bias.T, streamed, feed_gains, resident)
    (
        sum_narrow, sum_widen, sum_output, sum_query, sum_key, sum_value, token_gradient,
        sum_attention, sum_feedforward, sum_final, sum_bucket,
    ) = settle(sum_narrow, sum_widen, squares, token_gradient, sums, bucket_bias.shape[::-1])
    return (
        loss[0, 0],
        my_rows,
        token_gradient[None],
        sum_attention,
        sum_query,
        sum_key,
        sum_value,
        sum_output,
        sum_bucket.T,
        sum_feedforward,
        sum_widen,
        sum_narrow,
        sum_final,
    )


def solution(mesh):
    placed = (
        P("tower", "batch", None),
        P("tower", "batch"),
        P("tower", "batch"),
        P(),
        P(),
        P(),
        P(),
        P(),
        P(),
        P(),
        P(),
        P(),
        P(),
        P(),
    )
    return jax.shard_map(
        functools.partial(local, mesh.shape["batch"]),
        mesh=mesh,
        in_specs=placed,
        out_specs=(
            P(),
            P("batch", None),
            P("tower", "batch", None),
            P(),
            P(),
            P(),
            P(),
            P(),
            P(),
            P(),
            P(),
            P(),
            P(),
        ),
        check_vma=False,
    )
```

```python
import functools

import jax
import jax.numpy as jnp
from jax import lax
from jax.experimental import pallas as pl
from jax.experimental.pallas import tpu as pltpu
from jax.sharding import PartitionSpec as P

epsilon = 1e-06
masked_score = -1000000000.0
score_scale = 100.0
far_steps = (12, 16, 23, 32, 46, 64, 91)
highest = lax.Precision.HIGHEST


MESH = pl.DeviceIdType.MESH
job_rows = 384
unit_rows = 128


def batch_dims(size):
    sizes = {16: (2, 2, 4), 64: (4, 4, 4)}[size]
    strides = (1, sizes[0], sizes[0] * sizes[1])
    return dict(zip("xyz", zip(strides, sizes)))


def place():
    return lax.axis_index("tower"), lax.axis_index("batch")


def gather_peer(groups, step):
    tower, batch = place()
    return tower, lax.rem(batch + step, groups)


def greet_all(groups):
    tower, batch = place()
    barrier = pltpu.get_barrier_semaphore()

    def greet(step, carry):
        pl.semaphore_signal(barrier, 1, device_id=gather_peer(groups, step), device_id_type=MESH)
        return carry

    lax.fori_loop(1, groups, greet, 0)
    pl.semaphore_signal(barrier, 1, device_id=(1 - tower, batch), device_id_type=MESH)


def gather_units(groups, block_ref, out_ref, slots, send_sem, recv_sem, mate_sem):
    tower, batch = place()
    slots[tower, batch] = block_ref[...]
    pl.semaphore_wait(pltpu.get_barrier_semaphore(), groups)

    def copy(step, owner):
        return pltpu.make_async_remote_copy(
            src_ref=block_ref,
            dst_ref=slots.at[tower, owner],
            send_sem=send_sem.at[step],
            recv_sem=recv_sem.at[owner],
            device_id=gather_peer(groups, step),
            device_id_type=MESH,
        )

    def begin(step, carry):
        copy(step, batch).start()
        return carry

    def finish(step, carry):
        copy(step, batch).wait_send()
        copy(step, gather_peer(groups, step)[1]).wait_recv()
        return carry

    lax.fori_loop(1, groups, begin, 0)
    lax.fori_loop(1, groups, finish, 0)
    side = pltpu.make_async_remote_copy(
        src_ref=slots.at[tower],
        dst_ref=slots.at[tower],
        send_sem=mate_sem.at[0],
        recv_sem=mate_sem.at[1],
        device_id=(1 - tower, batch),
        device_id_type=MESH,
    )
    side.start()
    side.wait()
    out_ref[...] = slots[...]


def both(first, second):
    if first is None:
        return second
    if second is None:
        return first
    return jnp.logical_and(first, second)


def guarded(condition, action):
    if condition is None:
        action()
    else:
        pl.when(condition)(action)


def hands_back(order, dims, index):
    return index == 0 and all(dims[name][1] == 2 for name in order[1:])


def plan_unit(order, dims, coords, batch, rows):
    add, spread = [], []
    start, active, column = 0, None, None
    for index, name in enumerate(order):
        stride, size = dims[name]
        coord = coords[name]
        if size == 4:
            low_side = coord < 2
            inner = jnp.logical_or(coord == 1, coord == 2)
            outer = jnp.logical_not(inner)
            mate = batch + stride * (1 - 2 * lax.rem(coord, 2))
            share = hands_back(order, dims, index)
            sent = rows * 3 // 4 if share else rows
            first = start + jnp.where(low_side, rows // 4, 0) if share else start
            add.append(
                dict(rows=sent, send=first, keep=first, peer=mate, one_way=True,
                     sends=both(active, outer), receives=both(active, inner)))
            spread.append(
                dict(rows=sent, send=first, peer=mate,
                     sends=both(active, inner), receives=both(active, outer)))
            active_inner = both(active, inner)
            bit = coord // 2
            half = rows // 2
            kept = start + bit * half
            other = batch + stride * (3 - 2 * coord)
            add.append(
                dict(rows=half, send=start + (1 - bit) * half, keep=kept, peer=other, one_way=False,
                     sends=active_inner, receives=active_inner))
            spread.append(dict(rows=half, send=kept, peer=other, sends=active_inner, receives=active_inner))
            if share:
                quarter = rows // 4
                last = start + jnp.where(low_side, 0, 3 * quarter)
                add.append(
                    dict(rows=quarter, send=last, keep=last, peer=mate, one_way=True,
                         sends=active_inner, receives=both(active, outer)))
                spread.append(
                    dict(rows=quarter, send=last, peer=mate,
                         sends=both(active, outer), receives=active_inner))
                start, rows = start + coord * quarter, quarter
            else:
                start, rows, active = kept, half, active_inner
            continue
        mate = batch + stride * (1 - 2 * coord)
        if rows > 8:
            rows = rows // 2
            kept = start + coord * rows
            add.append(
                dict(rows=rows, send=start + (1 - coord) * rows, keep=kept, peer=mate, one_way=False,
                     sends=active, receives=active))
            spread.append(dict(rows=rows, send=kept, peer=mate, sends=active, receives=active))
            start = kept
        else:
            add.append(
                dict(rows=rows, send=start, keep=start, peer=mate, one_way=False, sends=active, receives=active,
                     send_side=1 - coord, keep_side=coord))
            spread.append(
                dict(rows=rows, send=start, peer=mate, sends=active, receives=active, send_side=coord))
    return add, spread[::-1]


def plan_shapes(order, dims, rows):
    result = []
    for index, name in enumerate(order):
        if dims[name][1] == 4:
            share = hands_back(order, dims, index)
            result.append((rows * 3 // 4 if share else rows, 1, True))
            result.append((rows // 2, 1, False))
            if share:
                result.append((rows // 4, 1, True))
            rows = rows // 4 if share else rows // 2
        elif rows > 8:
            rows //= 2
            result.append((rows, 1, False))
        else:
            result.append((rows, 2, False))
    return result


def step_rings(shapes):
    steps = 2 + 2 * len(shapes)
    rings = [4] * steps
    for index, (_, _, single) in enumerate(shapes):
        if single:
            first, last = 1 + index, steps - 2 - index
            rings[last] = last - first + 4
    return rings


orders = ("xyz", "yxz", "zxy")


def sums_kernel(dims, jobs, *refs):
    (lengths, table, hidden, ffn_in, context, normed, branch, pre, attn, query, key, value, upstream) = refs[:13]
    (tokens, mixed_grad, small, totals, bias_ref, gain, wq, wk, wv) = refs[13:22]
    (narrow_out, widen_out, square_out, token_out, small_out) = refs[22:27]
    (left, right, part, acc, full, mate_in, small_own, small_in, heads_in, by_query, by_key, by_value) = refs[27:39]
    (near_ref, near_sums, far_sums, token_in, mixed_in, token_buffer) = refs[39:45]
    rest = refs[45:]
    half = unit_rows // 2
    shapes = [plan_shapes(order, dims, half) for order in orders]
    counts = [len(shape) for shape in shapes]
    inbox, where = [], 0
    for count in counts:
        inbox.append(rest[where : where + count])
        where += count
    load_sem, right_sem, send_sem, recv_sem, keep_sem, small_sem, heads_sem, token_sem, credit = rest[where:]
    tower, batch = place()
    steps = [2 + 2 * count for count in counts]
    longest = max(steps)
    slots = jobs + longest + 1
    rings = [step_rings(shape) for shape in shapes]
    coords = {name: lax.rem(batch // stride, size) for name, (stride, size) in dims.items()}
    plans = [plan_unit(order, dims, coords, batch, half) for order in orders]
    turned_dims = dict(dims, x=dims["y"], y=dims["x"])
    turned_coords = dict(coords, x=coords["y"], y=coords["x"])
    turned = plan_unit(orders[-1], turned_dims, turned_coords, batch, half)

    def pick(odd, first, second):
        if isinstance(first, int) and isinstance(second, int) and first == second or first is None:
            return first
        if isinstance(first, bool):
            return first
        if getattr(first, "dtype", None) == jnp.bool_:
            return jnp.logical_or(jnp.logical_and(odd, second), jnp.logical_and(jnp.logical_not(odd), first))
        return jnp.where(odd, second, first)

    def plan(unit, job):
        if unit < len(orders) - 1:
            return plans[unit]
        odd = lax.rem(job, 2) == 1
        return tuple(
            [{key: pick(odd, one[key], two[key]) for key in one} for one, two in zip(ones, twos)]
            for ones, twos in zip(plans[unit], turned)
        )

    held, spread_held = acc.shape[0], full.shape[0]
    width = narrow_out.shape[1]
    heads = table.shape[0]
    seqs = lengths.shape[0]
    slot_len = tokens.shape[0] // seqs
    pair = 2 * width // heads
    group = heads_in.shape[3]
    pairs = width // group
    tasks = seqs * pairs
    blocks = slot_len // tile

    barrier = pltpu.get_barrier_semaphore()
    mate = (1 - tower, batch)
    mates, turns = [mate], [mate]
    for stride, size in dims.values():
        coord = lax.rem(batch // stride, size)
        near_mate = (tower, batch + stride * (1 - 2 * lax.rem(coord, 2)))
        mates.append(near_mate)
        turns.append(near_mate)
        if size == 4:
            mates.append((tower, batch + stride * (3 - 2 * coord)))
            turns.append((tower, batch + stride * (2 - 4 * (coord // 2))))
            mates.append(turns[-1])
    for other in mates:
        pl.semaphore_signal(barrier, 1, device_id=other, device_id_type=MESH)

    per_narrow = hidden.shape[1] // job_rows
    per_side = width // job_rows
    sources = [(hidden, branch, per_narrow), (ffn_in, pre, per_narrow), (context, attn, per_side)]
    sources += [(normed, grads, per_side) for grads in (by_query, by_key, by_value)]

    def right_place(job):
        past = job - per_narrow
        group = jnp.where(past < 0, 0, 1 + past // per_side)
        fresh = jnp.where(past < 0, job == 0, lax.rem(past, per_side) == 0)
        return lax.rem(group, 2), fresh

    def left_copies(target, job, columns):
        quarter = target.shape[1] // 4
        return [
            pltpu.make_async_copy(
                columns(pl.ds(n * quarter, quarter)), target.at[lax.rem(job, 2), pl.ds(n * quarter, quarter)],
                load_sem.at[lax.rem(job, 2), n],
            )
            for n in range(4)
        ]

    def load(job):
        place_right, fresh = right_place(job)
        first = 0
        for index, (left_ref, right_ref, count) in enumerate(sources):
            local = job - first

            def go(local=local, left_ref=left_ref, right_ref=right_ref, index=index):
                block = lax.rem(local, per_side) if index == 1 else local
                span = pl.ds(pl.multiple_of(block * job_rows, 128), job_rows)
                for copy in left_copies(left, job, lambda rows: left_ref.at[rows, span]):
                    copy.start()

                def go_right():
                    block = local // per_side if index == 1 else 0
                    span = pl.ds(pl.multiple_of(block * width, 128), width)
                    pltpu.make_async_copy(
                        right_ref.at[:, span], right.at[place_right], right_sem.at[place_right]
                    ).start()

                pl.when(fresh)(go_right)

            pl.when(jnp.logical_and(local >= 0, local < count))(go)
            first += count

    def compute(job):
        slot = lax.rem(job, 2)
        place_right, fresh = right_place(job)
        for copy in left_copies(left, job, lambda rows: normed.at[rows, pl.ds(0, job_rows)]):
            copy.wait()
        pl.when(fresh)(
            lambda: pltpu.make_async_copy(attn, right.at[place_right], right_sem.at[place_right]).wait()
        )
        pl.when(job + 1 < jobs)(lambda: load(job + 1))
        part[lax.rem(job, 3)] = lax.dot_general(
            left[slot], right[place_right], (((0,), (0,)), ((), ())), preferred_element_type=jnp.float32
        )

    def side_columns(item, key):
        if key not in item:
            return slice(None)
        return pl.ds(pl.multiple_of(item[key] * (width // 2), 128), width // 2)

    def remote(unit, step, job):
        add, spread = plan(unit, job)
        turn = lax.rem(job, rings[unit][step])
        place_in = lax.rem(job, held)
        sems = dict(
            send_sem=send_sem.at[unit * longest + step, turn],
            recv_sem=recv_sem.at[unit * longest + step, turn],
            device_id_type=MESH,
        )
        base = unit * half
        if step == 0:
            src = part.at[lax.rem(job, 3), pl.ds(pl.multiple_of(unit * unit_rows + (1 - tower) * half, 8), half)]
            dst = mate_in.at[turn, pl.ds(base, half)]
            return pltpu.make_async_remote_copy(src, dst, device_id=(1 - tower, batch), **sems), None, None
        count = counts[unit]
        item = add[step - 1] if step <= count else spread[step - 1 - count]
        rows = pl.ds(pl.multiple_of(base + item["send"], 8), item["rows"])
        columns = side_columns(item, "send_side")
        if step <= count:
            src, dst = acc.at[place_in, rows, columns], inbox[unit][step - 1].at[turn]
        else:
            src = dst = full.at[lax.rem(job, spread_held), rows, columns]
        copy = pltpu.make_async_remote_copy(src, dst, device_id=(tower, item["peer"]), **sems)
        return copy, item["sends"], item["receives"]

    def place_sums(unit, job, action):
        src = full.at[lax.rem(job, spread_held), pl.ds(unit * half, half)]
        first = unit * unit_rows + tower * half

        def at(ref, row, *columns):
            return lambda: action(src, ref.at[(pl.ds(pl.multiple_of(row + first, 8), half), *columns)])

        past = job - per_narrow
        pl.when(past < 0)(at(narrow_out, job * job_rows))
        columns = pl.ds(pl.multiple_of(past // per_side * width, 128), width)
        pl.when(jnp.logical_and(past >= 0, past < per_narrow))(
            at(widen_out, lax.rem(past, per_side) * job_rows, columns)
        )
        pl.when(past >= per_narrow)(at(square_out, (past - per_narrow) * job_rows))

    def last_copy(unit, job, src, dst):
        turn = lax.rem(job, rings[unit][steps[unit] - 1])
        index = unit * longest + steps[unit] - 1
        return pltpu.make_async_remote_copy(
            src, dst, send_sem=send_sem.at[index, turn], recv_sem=recv_sem.at[index, turn],
            device_id=(1 - tower, batch), device_id_type=MESH,
        )

    def begin_last(unit, job):
        def both_ways(src, dst):
            last_copy(unit, job, src, dst).start()
            pltpu.make_async_copy(src, dst, keep_sem.at[unit, lax.rem(job, 2)]).start()

        place_sums(unit, job, both_ways)

    def finish_last(unit, job):
        src = full.at[lax.rem(job, spread_held), pl.ds(unit * half, half)]
        dst = narrow_out.at[pl.ds(0, half)]
        last_copy(unit, job, src, dst).wait()
        pltpu.make_async_copy(src, dst, keep_sem.at[unit, lax.rem(job, 2)]).wait()

    def one_way(unit, step):
        return 1 <= step <= counts[unit] and shapes[unit][step - 1][2]

    def finish(unit, step, job):
        copy, sends, receives = remote(unit, step, job)
        add, _ = plan(unit, job)
        base = unit * half
        guarded(sends, copy.wait_send)
        turn = lax.rem(job, rings[unit][step])
        place_in = lax.rem(job, held)

        def arrived():
            copy.wait_recv()
            if step == 0:
                own = pl.ds(pl.multiple_of(unit * unit_rows + tower * half, 8), half)
                acc[place_in, pl.ds(base, half)] = part[lax.rem(job, 3), own] + mate_in[turn, pl.ds(base, half)]
            elif step <= counts[unit]:
                item = add[step - 1]
                rows = pl.ds(pl.multiple_of(base + item["keep"], 8), item["rows"])
                columns = side_columns(item, "keep_side")
                total = acc[place_in, rows, columns] + inbox[unit][step - 1][turn]
                if step == counts[unit]:
                    full[lax.rem(job, spread_held), rows, columns] = total
                else:
                    acc[place_in, rows, columns] = total
                if one_way(unit, step):
                    pl.when(job + rings[unit][step] < jobs)(
                        lambda: pl.semaphore_signal(
                            credit.at[unit * longest + step], 1,
                            device_id=(tower, item["peer"]), device_id_type=MESH,
                        )
                    )

        guarded(receives, arrived)

    def advance(unit, step, job):
        if step == steps[unit]:
            finish_last(unit, job)
            return
        if step > 0:
            finish(unit, step - 1, job)
        if step == steps[unit] - 1:
            begin_last(unit, job)
            return
        copy, sends, _ = remote(unit, step, job)

        def begin():
            if one_way(unit, step):
                pl.when(job >= rings[unit][step])(
                    lambda: pl.semaphore_wait(credit.at[unit * longest + step], 1)
                )
            copy.start()

        guarded(sends, begin)

    def small_copy(turn):
        return pltpu.make_async_remote_copy(
            src_ref=small_own.at[turn],
            dst_ref=small_in.at[turn],
            send_sem=small_sem.at[0, turn],
            recv_sem=small_sem.at[1, turn],
            device_id=turns[turn],
            device_id_type=MESH,
        )

    def small_turn(turn):
        if turn > 0:
            small_copy(turn - 1).wait()
            total = small_own[turn - 1] + small_in[turn - 1]
            if turn == len(turns):
                small_out[0:8] = total[0:8]
                small_out[8:, 0 : table.shape[1]] = exact_dot(total[8:24, : 4 * tile], offset_onehot(table.shape[1]), 1, 1)
            else:
                small_own[turn] = total
        if turn < len(turns):
            small_copy(turn).start()

    def heads_load(task, begin):
        rows = pl.ds(pl.multiple_of(task // pairs * slot_len, slot_len), slot_len)
        columns = pl.ds(pl.multiple_of(lax.rem(task, pairs) * group, group), group)
        slot = lax.rem(task, 2)
        for index, ref in enumerate((query, key, value, upstream)):
            copy = pltpu.make_async_copy(
                ref.at[rows, columns], heads_in.at[slot, index], heads_sem.at[slot, index]
            )
            copy.start() if begin else copy.wait()

    places = lax.broadcasted_iota(jnp.int32, (slot_len, 1), 0)
    lanes = lax.broadcasted_iota(jnp.int32, (1, pair), 1)

    def attend(task, carry):
        seq, index = task // pairs, lax.rem(task, pairs)
        slot = lax.rem(task, 2)
        heads_load(task, False)
        pl.when(task + 1 < tasks)(lambda: heads_load(task + 1, True))
        for inside in range(group // pair):
            attend_pair(seq, index * (group // pair) + inside, slot, inside)
        return carry

    def attend_pair(seq, index, slot, inside):
        span = slice(inside * pair, (inside + 1) * pair)
        queries, keys, values, upper = (heads_in[slot, n, :, span] for n in range(4))
        length = lengths[seq]
        keys_across = keys.T
        grads_out = [None] * 2
        query_rows = []
        for side in range(2):
            head = 2 * index + side
            mine = (lanes // (pair // 2) == side).astype(jnp.bfloat16)
            my_queries, my_upper = queries * mine, upper * mine
            raw = dot_across(keys, my_queries)
            soft_grad = dot_across(values, my_upper)
            line = totals[seq, pl.ds(head, 1), :]
            soft_columns, grad_columns = [], []
            near_total = [None] * 3
            far_total = [None] * 2
            for column in range(blocks):
                columns = slice(column * tile, (column + 1) * tile)
                scores = []
                for block in range(blocks):
                    rows = slice(block * tile, (block + 1) * tile)
                    bias = bias_tile(near_ref, head, block, column, *far_bias(table, head))
                    scores.append(jnp.where(places[rows] < length, raw[rows, columns] + bias, masked_score))
                soft = jnp.exp(jnp.concatenate(scores, axis=0) - line[:, columns])
                soft_columns.append(soft.astype(jnp.bfloat16))
                by_soft = soft_grad[:, columns]
                grads = soft * (by_soft - jnp.sum(soft * by_soft, axis=0, keepdims=True))
                grad_columns.append(grads.astype(jnp.bfloat16))
                for block in range(blocks):
                    piece = grads[block * tile : (block + 1) * tile]
                    ahead = block - column
                    group, spot = (near_total, 1 - ahead) if abs(ahead) <= 1 else (far_total, int(ahead > 0))
                    group[spot] = piece if group[spot] is None else group[spot] + piece
            for spot in range(3):
                if near_total[spot] is not None:
                    near_sums[head, :, spot * tile : (spot + 1) * tile] += near_total[spot]
            for spot in range(2):
                if far_total[spot] is not None:
                    far_sums[spot, pl.ds(head, 1), :] += jnp.sum(far_total[spot], axis=0, keepdims=True)
            soft_low = jnp.concatenate(soft_columns, axis=1)
            grads_low = jnp.concatenate(grad_columns, axis=1)
            half_rows = slice(side * (pair // 2), (side + 1) * (pair // 2))
            query_rows.append(low_dot(keys_across[half_rows], grads_low).astype(jnp.bfloat16))
            pieces = (low_dot(grads_low, my_queries), low_dot(soft_low, my_upper))
            grads_out = [new if old is None else old + new for old, new in zip(grads_out, pieces)]
        rows = pl.ds(pl.multiple_of(seq * slot_len, slot_len), slot_len)
        columns = pl.ds(pl.multiple_of(index * pair, pair), pair)
        by_query[rows, columns] = jnp.concatenate(query_rows, axis=0).T
        for ref, grads in zip((by_key, by_value), grads_out):
            ref[rows, columns] = grads.astype(jnp.bfloat16)

    def token_load(seq, begin):
        rows = pl.ds(pl.multiple_of(seq * slot_len, slot_len), slot_len)
        for index, (ref, target) in enumerate(((tokens, token_in), (mixed_grad, mixed_in))):
            copy = pltpu.make_async_copy(ref.at[rows], target, token_sem.at[index])
            copy.start() if begin else copy.wait()

    def token_store(seq):
        rows = pl.ds(pl.multiple_of(seq * slot_len, slot_len), slot_len)
        return pltpu.make_async_copy(token_buffer, token_out.at[rows], token_sem.at[2])

    def token_task(seq):
        rows = pl.ds(pl.multiple_of(seq * slot_len, slot_len), slot_len)
        token_load(seq, False)
        normed_grad = dot_across(by_query[rows, :], wq[...]) + dot_across(by_key[rows, :], wk[...])
        normed_grad += dot_across(by_value[rows, :], wv[...])
        by_tokens, token_gain = norm_back(token_in[...].astype(jnp.float32), gain[...][None], normed_grad)
        small_own[0, 0:1] += token_gain
        pl.when(seq > 0)(lambda: token_store(seq - 1).wait())
        token_buffer[...] = (mixed_in[...] + by_tokens).astype(jnp.bfloat16)
        token_store(seq).start()
        pl.when(seq + 1 < seqs)(lambda: token_load(seq + 1, True))

    def close():
        token_store(seqs - 1).wait()
        small_own[0, 8:24, :] = jnp.zeros((16, width), jnp.float32)
        for head in range(heads):
            turned = jnp.concatenate([near_sums[head], jnp.zeros((tile, tile), jnp.float32)], axis=1)
            count = tile // 2
            while count:
                upper = turned[count : 2 * count]
                turned = turned[:count] + pltpu.roll(upper, 4 * tile - count, 1)
                count //= 2
            small_own[0, 8 + head : 9 + head, : 4 * tile] = turned
        small_own[0, 8:24, 2 * tile : 3 * tile] += far_sums[0]
        small_own[0, 8:24, 3 * tile : 4 * tile] += far_sums[1]

    load(0)
    heads_load(0, True)
    token_load(0, True)
    small_own[0, 0:8, :] = small[...]
    compute(jnp.int32(0))
    pl.semaphore_wait(barrier, len(mates))

    last_attend = jobs - 3 * (width // job_rows) - 1
    first_token = last_attend + 1
    first_attend = 5
    first_small = slots - 1 - len(turns)

    def prepare():
        spread_bias(bias_ref, near_ref, heads)
        near_sums[...] = jnp.zeros_like(near_sums)
        far_sums[...] = jnp.zeros_like(far_sums)

    def products(time):
        pl.when(time < jobs)(functools.partial(compute, time))
        pl.when(time == 2)(prepare)

    def attention(time):
        past = jnp.maximum(time - first_attend, 0)
        span = last_attend - first_attend
        begin = jnp.minimum(past * tasks // span, tasks)
        end = jnp.where(time < first_attend, 0, jnp.minimum((past + 1) * tasks // span, tasks))
        lax.fori_loop(begin, end, attend, 0)

    def token_part(time):
        seq = time - first_token
        pl.when(jnp.logical_and(seq >= 0, seq < seqs))(functools.partial(token_task, seq))
        pl.when(time == first_token + seqs)(close)
        for turn in range(len(turns) + 1):
            pl.when(time == first_small + turn)(functools.partial(small_turn, turn))

    def slot(time, carry):
        for unit, work in ((2, products), (0, attention), (1, token_part)):
            for step in range(steps[unit] + 1):
                job = time - 1 - step
                pl.when(jnp.logical_and(job >= 0, job < jobs))(functools.partial(advance, unit, step, job))
            work(time)
        return carry

    lax.fori_loop(1, slots, slot, 0)


def sum_weights(batch_size, collective, lengths, bucket_bias, streamed, small, resident):
    hidden, normed = streamed[0], streamed[3]
    tokens, width = normed.shape
    seqs = lengths.shape[0]
    heads = bucket_bias.shape[0]
    slot_len = tokens // seqs
    pair = 2 * width // heads
    total = 2 * hidden.shape[1] + 4 * width
    jobs = total // job_rows
    dims = batch_dims(batch_size)
    half = unit_rows // 2
    shapes = [plan_shapes(order, dims, half) for order in orders]
    rings = [step_rings(shape) for shape in shapes]
    inboxes = [
        pltpu.VMEM((rings[unit][1 + index], rows, width // parts), jnp.float32)
        for unit, shape in enumerate(shapes)
        for index, (rows, parts, _) in enumerate(shape)
    ]
    steps = max(len(ring) for ring in rings)
    longest = max(max(ring) for ring in rings)
    turns = 1 + sum(size // 2 for _, size in dims.values())
    lines = 24
    low, full = jnp.bfloat16, jnp.float32
    in_vmem = pl.BlockSpec(memory_space=pltpu.VMEM)
    in_smem = pl.BlockSpec(memory_space=pltpu.SMEM)
    anywhere = pl.BlockSpec(memory_space=pl.ANY)
    return pl.pallas_call(
        functools.partial(sums_kernel, dims, jobs),
        out_shape=(
            jax.ShapeDtypeStruct((hidden.shape[1], width), full),
            jax.ShapeDtypeStruct((width, hidden.shape[1]), full),
            jax.ShapeDtypeStruct((4 * width, width), full),
            jax.ShapeDtypeStruct((tokens, width), low),
            jax.ShapeDtypeStruct((24, width), full),
        ),
        in_specs=[in_smem] * 2 + [anywhere] * len(streamed) + [in_vmem] * (1 + len(resident)),
        out_specs=(anywhere, anywhere, anywhere, anywhere, in_vmem),
        scratch_shapes=[
            pltpu.VMEM((2, tokens, job_rows), low),
            pltpu.VMEM((2, tokens, width), low),
            pltpu.VMEM((3, job_rows, width), full),
            pltpu.VMEM((steps // 2, 3 * half, width), full),
            pltpu.VMEM((steps, 3 * half, width), full),
            pltpu.VMEM((4, 3 * half, width), full),
            pltpu.VMEM((turns, lines, width), full),
            pltpu.VMEM((turns, lines, width), full),
            pltpu.VMEM((2, 4, slot_len, 1 * pair), low),
            pltpu.VMEM((tokens, width), low),
            pltpu.VMEM((tokens, width), low),
            pltpu.VMEM((tokens, width), low),
            pltpu.VMEM((heads, tile, near), full),
            pltpu.VMEM((heads, tile, near), full),
            pltpu.VMEM((2, 16, tile), full),
            pltpu.VMEM((slot_len, width), low),
            pltpu.VMEM((slot_len, width), full),
            pltpu.VMEM((slot_len, width), low),
            *inboxes,
            pltpu.SemaphoreType.DMA((2, 4)),
            pltpu.SemaphoreType.DMA((2,)),
            pltpu.SemaphoreType.DMA((3 * steps, longest)),
            pltpu.SemaphoreType.DMA((3 * steps, longest)),
            pltpu.SemaphoreType.DMA((3, 2)),
            pltpu.SemaphoreType.DMA((2, turns)),
            pltpu.SemaphoreType.DMA((2, 4)),
            pltpu.SemaphoreType.DMA((3,)),
            pltpu.SemaphoreType.REGULAR((3 * steps,)),
        ],
        compiler_params=pltpu.CompilerParams(
            collective_id=collective, has_side_effects=True, vmem_limit_bytes=66500000
        ),
        name="sum_weights",
    )(lengths, bucket_bias, *streamed, small, *resident)


tile = 128
near = 3 * tile


def offset_onehot(buckets):
    spots = lax.broadcasted_iota(jnp.int32, (buckets, 4 * tile), 1)
    labels = lax.broadcasted_iota(jnp.int32, (buckets, 4 * tile), 0)
    offset = tile - jnp.where(spots >= near, spots - 4 * tile, spots)
    spread = jnp.abs(offset)
    far_bucket = 8 + sum(((spread >= step).astype(jnp.int32) for step in far_steps))
    bucket = jnp.where(spread < 8, spread, far_bucket) + jnp.where(offset > 0, buckets // 2, 0)
    return (bucket == labels).astype(jnp.float32)


def spread_bias(bias_ref, near_ref, heads):
    lines = exact_dot(bias_ref[...], offset_onehot(bias_ref.shape[1]), 1, 0)
    for head in range(heads):
        line = jnp.broadcast_to(lines[head : head + 1, :], (tile, 4 * tile))
        near_ref[head] = pltpu.roll(line, 0, 1, stride=1, stride_axis=0)[:, :near]


def far_bias(table, head):
    buckets = table.shape[1]
    return table[head, buckets // 2 - 1], table[head, buckets - 1]


def bias_tile(near_ref, head, row_block, column_block, low_far, high_far):
    ahead = row_block - column_block
    if abs(ahead) <= 1:
        spot = 1 - ahead
        return near_ref[head, :, spot * tile : (spot + 1) * tile]
    return jnp.full((tile, tile), high_far if ahead > 0 else low_far, jnp.float32)


def unit_scale(values):
    return lax.rsqrt(jnp.mean(values * values, axis=-1, keepdims=True) + epsilon)


def low_dot(left, right):
    return jnp.dot(left, right, preferred_element_type=jnp.float32)


def dot_across(left, right):
    return lax.dot_general(left, right, (((1,), (1,)), ((), ())), preferred_element_type=jnp.float32)


def forward_kernel(
    groups, lengths, prefixes, table, x_ref, bias_ref, gain_a, wq, wk, wv, wo, gain_f, widen_far, narrow_far, gain_z,
    normed_ref, q_ref, k_ref, v_ref, lse_ref, context_ref, mixed_ref, ffn_ref, hidden_ref, output_ref, pooled_ref, units_ref,
    near_ref, widen, narrow, weight_sem, slots, block_ref, send_sem, recv_sem, mate_sem,
):
    seq = pl.program_id(0)
    heads = table.shape[0]
    slot_len, width = x_ref.shape
    blocks = slot_len // tile
    pair = 2 * width // heads
    length = lengths[seq]
    fetches = [
        pltpu.make_async_copy(widen_far, widen, weight_sem.at[0]),
        pltpu.make_async_copy(narrow_far, narrow, weight_sem.at[1]),
    ]

    def first():
        greet_all(groups)
        for fetch in fetches:
            fetch.start()
        spread_bias(bias_ref, near_ref, heads)

    pl.when(seq == 0)(first)
    tokens = x_ref[...].astype(jnp.float32)
    normed = (tokens * unit_scale(tokens) * gain_a[...][None]).astype(jnp.bfloat16)
    normed_ref[...] = normed
    q_ref[...] = low_dot(normed, wq[...]).astype(jnp.bfloat16)
    k_ref[...] = low_dot(normed, wk[...]).astype(jnp.bfloat16)
    v_ref[...] = low_dot(normed, wv[...]).astype(jnp.bfloat16)
    lanes = lax.broadcasted_iota(jnp.int32, (1, pair), 1)
    places = lax.broadcasted_iota(jnp.int32, (slot_len, 1), 0)

    def attend(index, carry):
        span = pl.ds(pl.multiple_of(index * pair, pair), pair)
        keys = k_ref[:, span]
        queries = q_ref[:, span]
        values_across = v_ref[:, span].T
        pieces = []
        for side in range(2):
            head = 2 * index + side
            mine = (lanes // (pair // 2) == side).astype(jnp.bfloat16)
            raw = dot_across(keys, queries * mine)
            soft_columns, lines = [], []
            for column in range(blocks):
                columns = slice(column * tile, (column + 1) * tile)
                scores = []
                for block in range(blocks):
                    rows = slice(block * tile, (block + 1) * tile)
                    bias = bias_tile(near_ref, head, block, column, *far_bias(table, head))
                    scores.append(jnp.where(places[rows] < length, raw[rows, columns] + bias, masked_score))
                scores = jnp.concatenate(scores, axis=0)
                peak = jnp.max(scores, axis=0, keepdims=True)
                raised = jnp.exp(scores - peak)
                total = jnp.sum(raised, axis=0, keepdims=True)
                soft_columns.append((raised * (1.0 / total)).astype(jnp.bfloat16))
                lines.append(peak + jnp.log(total))
            lse_ref[0, pl.ds(head, 1), :] = jnp.concatenate(lines, axis=1)
            soft_low = jnp.concatenate(soft_columns, axis=1)
            rows = slice(side * (pair // 2), (side + 1) * (pair // 2))
            pieces.append(low_dot(values_across[rows], soft_low).astype(jnp.bfloat16))
        context_ref[:, span] = jnp.concatenate(pieces, axis=0).T
        return carry

    lax.fori_loop(0, heads // 2, attend, 0, unroll=True)
    mixed = tokens + low_dot(context_ref[...], wo[...])
    mixed_ref[...] = mixed
    ffn_in = (mixed * unit_scale(mixed) * gain_f[...][None]).astype(jnp.bfloat16)
    ffn_ref[...] = ffn_in
    output_ref[...] = mixed
    pl.when(seq == 0)(lambda: [fetch.wait() for fetch in fetches] and None)

    def feed(index, carry):
        span = pl.ds(pl.multiple_of(index * width, 128), width)
        pre_act = low_dot(ffn_ref[...], widen[:, span])
        hidden = jnp.where(pre_act > 0, pre_act, 0.0).astype(jnp.bfloat16)
        hidden_ref[:, span] = hidden
        output_ref[...] += low_dot(hidden, narrow[span, :])
        return carry

    lax.fori_loop(0, widen.shape[1] // width, feed, 0, unroll=True)
    output = output_ref[...]
    mask = jnp.logical_and(places >= prefixes[seq], places < length).astype(jnp.float32)
    count = (length - prefixes[seq]).astype(jnp.float32)
    final = output * unit_scale(output) * gain_z[...][None]
    pooled_ref[pl.ds(seq, 1), :] = jnp.sum(final * (mask / count), axis=0, keepdims=True)

    def last():
        pooled = pooled_ref[...]
        block_ref[...] = pooled * lax.rsqrt(jnp.sum(pooled * pooled, axis=-1, keepdims=True) + epsilon)
        gather_units(groups, block_ref, units_ref, slots, send_sem, recv_sem, mate_sem)

    pl.when(seq == pl.num_programs(0) - 1)(last)


def run_forward(groups, collective, tokens, lengths, prefixes, bucket_bias, gains, weights):
    rows, width = tokens.shape
    seqs = lengths.shape[0]
    slot_len = rows // seqs
    heads = bucket_bias.shape[0]
    wq, wk, wv, wo, widen, narrow = weights
    gain_a, gain_f, gain_z = gains
    ff = widen.shape[1]
    units = (2, groups, seqs, width)

    def whole(shape):
        return pl.BlockSpec(shape, lambda n, *_: (0,) * len(shape), pipeline_mode=pl.Buffered(1))

    def block(columns):
        return pl.BlockSpec((slot_len, columns), lambda n, *_: (n, 0))

    square = whole((width, width))
    line = whole((width,))
    low, full = jnp.bfloat16, jnp.float32

    def shape(columns, kind):
        return jax.ShapeDtypeStruct((rows, columns), kind)

    return pl.pallas_call(
        functools.partial(forward_kernel, groups),
        grid_spec=pltpu.PrefetchScalarGridSpec(
            num_scalar_prefetch=3,
            grid=(seqs,),
            in_specs=[
                block(width), whole(bucket_bias.shape), line, square, square, square, square,
                line, pl.BlockSpec(memory_space=pl.ANY), pl.BlockSpec(memory_space=pl.ANY), line,
            ],
            out_specs=[
                block(width), block(width), block(width), block(width),
                pl.BlockSpec((1, 16, slot_len), lambda n, *_: (n, 0, 0)),
                block(width), block(width), block(width), block(ff), block(width),
                pl.BlockSpec((seqs, width), lambda n, *_: (0, 0)),
                pl.BlockSpec(units, lambda n, *_: (0, 0, 0, 0)),
            ],
            scratch_shapes=[
                pltpu.VMEM((heads, tile, near), jnp.float32),
                pltpu.VMEM((width, ff), low),
                pltpu.VMEM((ff, width), low),
                pltpu.SemaphoreType.DMA((2,)),
                pltpu.VMEM(units, full),
                pltpu.VMEM((seqs, width), full),
                pltpu.SemaphoreType.DMA((groups,)),
                pltpu.SemaphoreType.DMA((groups,)),
                pltpu.SemaphoreType.DMA((2,)),
            ],
        ),
        out_shape=(
            shape(width, low), shape(width, low), shape(width, low), shape(width, low),
            jax.ShapeDtypeStruct((seqs, 16, slot_len), full),
            shape(width, low), shape(width, full), shape(width, low), shape(ff, low), shape(width, full),
            jax.ShapeDtypeStruct((seqs, width), full),
            jax.ShapeDtypeStruct(units, full),
        ),
        compiler_params=pltpu.CompilerParams(
            collective_id=collective, has_side_effects=True, vmem_limit_bytes=60000000
        ),
        name="forward",
    )(lengths, prefixes, bucket_bias, tokens, bucket_bias, gain_a, wq, wk, wv, wo, gain_f, widen, narrow, gain_z)


def norm_back(values, gain, upstream):
    inverse = unit_scale(values)
    scaled = upstream * gain
    inner = jnp.mean(scaled * values, axis=-1, keepdims=True)
    by_values = inverse * scaled - values * (inverse * inverse * inverse) * inner
    return by_values, jnp.sum(upstream * values * inverse, axis=0, keepdims=True)


def exact_dot(left, right, left_dim, right_dim):
    return lax.dot_general(
        left, right, (((left_dim,), (right_dim,)), ((), ())),
        precision=highest, preferred_element_type=jnp.float32,
    )


def contrast(units_ref, pooled_ref, positives_ref, loss_ref, rows_ref, pooled_grad):
    tower, batch = place()
    _, groups, seqs, width = units_ref.shape
    count = groups * seqs
    queries = units_ref[0].reshape(count, width)
    docs = units_ref[1].reshape(count, width)
    scores = score_scale * exact_dot(queries, docs, 1, 1)
    labels = lax.broadcasted_iota(jnp.int32, (count, count), 1)
    target = (positives_ref[...] == labels).astype(jnp.float32)
    row_peak = jnp.max(scores, axis=1, keepdims=True)
    row_raised = jnp.exp(scores - row_peak)
    row_sum = jnp.sum(row_raised, axis=1, keepdims=True)
    column_peak = jnp.max(scores, axis=0, keepdims=True)
    column_raised = jnp.exp(scores - column_peak)
    column_sum = jnp.sum(column_raised, axis=0, keepdims=True)
    loss = 0.5 * jnp.sum(row_peak + jnp.log(row_sum), axis=0, keepdims=True)
    loss += 0.5 * jnp.sum(column_peak + jnp.log(column_sum), axis=1, keepdims=True)
    loss_ref[...] = loss - jnp.sum(jnp.sum(target * scores, axis=1, keepdims=True), axis=0, keepdims=True)
    grad = 0.5 * row_raised / row_sum + 0.5 * column_raised / column_sum - target
    mine = lax.broadcasted_iota(jnp.int32, (8, count), 0) + batch * seqs
    spots = lax.broadcasted_iota(jnp.int32, (8, count), 1)
    select = (mine == spots).astype(jnp.float32)
    my_rows = exact_dot(select, grad, 1, 0)
    my_columns = exact_dot(select, grad, 1, 1)
    rows_ref[...] = my_rows[:seqs]
    as_query = exact_dot(my_rows, docs, 1, 0)
    as_doc = exact_dot(my_columns, queries, 1, 0)
    unit_grad = (score_scale * jnp.where(tower == 0, as_query, as_doc))[:seqs]
    pooled = pooled_ref[...]
    inverse = lax.rsqrt(jnp.sum(pooled * pooled, axis=-1, keepdims=True) + epsilon)
    cubed = inverse * inverse * inverse
    pooled_grad[:seqs] = inverse * unit_grad - pooled * cubed * jnp.sum(unit_grad * pooled, axis=-1, keepdims=True)


def feed_back_kernel(
    lengths, prefixes, wo, gain_f, widen, narrow, gain_z, mixed_ref, hidden_ref, output_ref, pooled_ref,
    units_ref, positives_ref,
    branch_ref, pre_ref, attn_ref, context_ref, mixed_grad, gains_ref, loss_ref, rows_ref, feed_grad, pooled_grad,
):
    seq = pl.program_id(0)
    slot_len, width = mixed_ref.shape
    length = lengths[seq]

    def clear():
        gains_ref[...] = jnp.zeros_like(gains_ref)
        contrast(units_ref, pooled_ref, positives_ref, loss_ref, rows_ref, pooled_grad)

    pl.when(seq == 0)(clear)
    places = lax.broadcasted_iota(jnp.int32, (slot_len, 1), 0)
    mask = jnp.logical_and(places >= prefixes[seq], places < length).astype(jnp.float32)
    count = (length - prefixes[seq]).astype(jnp.float32)
    final_grad = (mask / count) * pooled_grad[pl.ds(seq, 1), :]
    output_grad, final_gain = norm_back(output_ref[...], gain_z[...][None], final_grad)
    gains_ref[2:3] += final_gain
    mixed_grad[...] = output_grad
    branch_ref[...] = output_grad.astype(jnp.bfloat16)
    feed_grad[...] = jnp.zeros_like(feed_grad)

    def feed(index, carry):
        span = pl.ds(pl.multiple_of(index * 2 * width, 128), 2 * width)
        hidden_grad = dot_across(branch_ref[...], narrow[span, :])
        pre_grad = jnp.where(hidden_ref[:, span] > 0, hidden_grad, 0.0).astype(jnp.bfloat16)
        pre_ref[:, span] = pre_grad
        feed_grad[...] += dot_across(pre_grad, widen[:, span])
        return carry

    lax.fori_loop(0, widen.shape[1] // (2 * width), feed, 0, unroll=True)
    by_mixed, feed_gain = norm_back(mixed_ref[...], gain_f[...][None], feed_grad[...])
    gains_ref[1:2] += feed_gain
    total_grad = mixed_grad[...] + by_mixed
    mixed_grad[...] = total_grad
    attn_low = total_grad.astype(jnp.bfloat16)
    attn_ref[...] = attn_low
    context_ref[...] = dot_across(attn_low, wo[...]).astype(jnp.bfloat16)


def whole(shape):
    return pl.BlockSpec(shape, lambda n, *_: (0,) * len(shape), pipeline_mode=pl.Buffered(1))


def run_feed_back(lengths, prefixes, gains, weights, mixed, hidden, output, pooled, units, positives):
    rows, width = mixed.shape
    seqs = lengths.shape[0]
    slot_len = rows // seqs
    wo, widen, narrow = weights
    ff = widen.shape[1]
    count = positives.shape[0]

    def block(columns):
        return pl.BlockSpec((slot_len, columns), lambda n, *_: (n, 0))

    def shape(columns, kind):
        return jax.ShapeDtypeStruct((rows, columns), kind)

    low, full = jnp.bfloat16, jnp.float32
    return pl.pallas_call(
        feed_back_kernel,
        grid_spec=pltpu.PrefetchScalarGridSpec(
            num_scalar_prefetch=2,
            grid=(seqs,),
            in_specs=[
                whole((width, width)), whole((width,)), whole((width, ff)), whole((ff, width)), whole((width,)),
                block(width), block(ff), block(width),
                whole(pooled.shape), whole(units.shape), whole((count, 1)),
            ],
            out_specs=[
                block(width), block(ff), block(width), block(width), block(width),
                pl.BlockSpec((8, width), lambda n, *_: (0, 0)),
                pl.BlockSpec((1, 1), lambda n, *_: (0, 0)),
                pl.BlockSpec((seqs, count), lambda n, *_: (0, 0)),
            ],
            scratch_shapes=[pltpu.VMEM((slot_len, width), jnp.float32), pltpu.VMEM((8, width), jnp.float32)],
        ),
        out_shape=(
            shape(width, low), shape(ff, low), shape(width, low), shape(width, low), shape(width, full),
            jax.ShapeDtypeStruct((8, width), full),
            jax.ShapeDtypeStruct((1, 1), full),
            jax.ShapeDtypeStruct((seqs, count), full),
        ),
        compiler_params=pltpu.CompilerParams(vmem_limit_bytes=60000000),
        name="feed_back",
    )(
        lengths, prefixes, wo, gains[0], widen, narrow, gains[1], mixed, hidden, output, pooled, units,
        positives[:, None],
    )


def settle_kernel(count, sums, *refs):
    for source, target in zip(refs[:count], refs[count : 2 * count]):
        target[...] = source[...]
    *gains, bucket = refs[2 * count :]

    def small():
        for index, gain in enumerate(gains):
            gain[...] = sums[index, :]
        heads, buckets = bucket.shape
        bucket[...] = sums[8 : 8 + heads, 0:buckets]

    pl.when(pl.program_id(0) == 0)(small)


def settle(narrow, widen, squares, token, sums, table):
    width = widen.shape[0]
    steps = 16

    def rows(array, parts=1, first=0):
        block = array.shape[0] // parts // steps
        return pl.BlockSpec((block, array.shape[1]), lambda n: (first * steps + n, 0))

    square = jax.ShapeDtypeStruct((width, width), squares.dtype)
    return pl.pallas_call(
        functools.partial(settle_kernel, 7),
        grid=(steps,),
        in_specs=[
            pl.BlockSpec(sums.shape, lambda n: (0, 0)), rows(narrow), rows(widen), *(rows(squares, 4, n) for n in range(4)), rows(token),
        ],
        out_specs=[
            rows(narrow), rows(widen), *(rows(squares, 4) for n in range(4)), rows(token),
            *(pl.BlockSpec((width,), lambda n: (0,)) for _ in range(3)), pl.BlockSpec(table, lambda n: (0, 0)),
        ],
        out_shape=(
            jax.ShapeDtypeStruct(narrow.shape, narrow.dtype),
            jax.ShapeDtypeStruct(widen.shape, widen.dtype),
            square, square, square, square,
            jax.ShapeDtypeStruct(token.shape, token.dtype),
            *(jax.ShapeDtypeStruct((width,), sums.dtype) for _ in range(3)),
            jax.ShapeDtypeStruct(table, sums.dtype),
        ),
        compiler_params=pltpu.CompilerParams(vmem_limit_bytes=66500000),
        name="settle",
    )(sums, narrow, widen, squares, squares, squares, squares, token)


def local(
    batch_size,
    tokens,
    lengths,
    prefixes,
    positives,
    gain_attention,
    query_weight,
    key_weight,
    value_weight,
    output_weight,
    bucket_bias,
    gain_feedforward,
    widen_weight,
    narrow_weight,
    gain_final,
):
    seqs = lengths.shape[1]
    width = tokens.shape[2]
    gains = (gain_attention, gain_feedforward, gain_final)
    weights = (query_weight, key_weight, value_weight, output_weight, widen_weight, narrow_weight)
    normed, query, key, value, totals, context, mixed, ffn_in, hidden, output, pooled, units = run_forward(
        batch_size, 0, tokens[0], lengths[0], prefixes[0], bucket_bias.T, gains, weights
    )
    branch, pre, attn, context_grad, mixed_grad, feed_gains, loss, my_rows = run_feed_back(
        lengths[0], prefixes[0], gains[1:], weights[3:], mixed, hidden, output, pooled, units, positives
    )
    streamed = (
        hidden, ffn_in, context, normed, branch, pre, attn, query, key, value, context_grad, tokens[0], mixed_grad
    )
    resident = (totals, bucket_bias.T, gain_attention, *weights[:3])
    sum_narrow, sum_widen, squares, token_gradient, sums = sum_weights(batch_size, 1, lengths[0], bucket_bias.T, streamed, feed_gains, resident)
    (
        sum_narrow, sum_widen, sum_output, sum_query, sum_key, sum_value, token_gradient,
        sum_attention, sum_feedforward, sum_final, sum_bucket,
    ) = settle(sum_narrow, sum_widen, squares, token_gradient, sums, bucket_bias.shape[::-1])
    return (
        loss[0, 0],
        my_rows,
        token_gradient[None],
        sum_attention,
        sum_query,
        sum_key,
        sum_value,
        sum_output,
        sum_bucket.T,
        sum_feedforward,
        sum_widen,
        sum_narrow,
        sum_final,
    )


def solution(mesh):
    placed = (
        P("tower", "batch", None),
        P("tower", "batch"),
        P("tower", "batch"),
        P(),
        P(),
        P(),
        P(),
        P(),
        P(),
        P(),
        P(),
        P(),
        P(),
        P(),
    )
    return jax.shard_map(
        functools.partial(local, mesh.shape["batch"]),
        mesh=mesh,
        in_specs=placed,
        out_specs=(
            P(),
            P("batch", None),
            P("tower", "batch", None),
            P(),
            P(),
            P(),
            P(),
            P(),
            P(),
            P(),
            P(),
            P(),
            P(),
        ),
        check_vma=False,
    )
```
